32 devices in a mesh: seq: 4 (over y, x), fsdp: 8 (over z, core).
Axes of the slice: x: 2, y: 2, z: 4, core: 2. Of those that a mesh axis runs over, the one named last changes fastest.
Arguments:
- hidden_in: bfloat16 [8, 1024, 1024], P('fsdp', 'seq'), may hold values from -10 to 10
- segment_ids: int32 [8, 1024], P('fsdp'), may hold values from 0 to 2, never falling along the last dimension, each value on 1 to 768 neighbouring positions
- valid_tokens: int32 [8, 1024], P('fsdp'), may hold values from 0 to 1
- w_qkv: bfloat16 [1024, 3072], P('fsdp'), may hold values from -0.1875 to 0.1875
- w_attn_out: bfloat16 [1024, 1024], P('fsdp'), may hold values from -2 to 2
- w_in_proj: bfloat16 [1024, 5248], P('fsdp'), may hold values from -0.1875 to 0.1875
- w_out_proj: bfloat16 [2624, 1024], P('fsdp'), may hold values from -0.125 to 0.125
- attn_gain: bfloat16 [1024], P('fsdp'), may hold values from 0.25 to 1.75
- mlp_gain: bfloat16 [1024], P('fsdp'), may hold values from 0.25 to 1.75
- cotangent: bfloat16 [8, 1024, 1024], P('fsdp', 'seq'), may hold values from -6 to 6
Outputs:
- hidden_out: bfloat16 [8, 1024, 1024], P('fsdp', 'seq')
- grad_in: float32 [8, 1024, 1024], P('fsdp', 'seq')
- grad_qkv: float32 [1024, 3072], P('fsdp')
- grad_attn_out: float32 [1024, 1024], P('fsdp')
- grad_in_proj: float32 [1024, 5248], P('fsdp')
- grad_out_proj: float32 [2624, 1024], P('fsdp')
- grad_attn_gain: float32 [1024], P('fsdp')
- grad_mlp_gain: float32 [1024], P('fsdp')
- rms_values: float32 [3], replicated
The draws below stay inside these ranges and needn't reach their ends.
All inputs are finite; a program needn't handle non-finite values.
Results may differ from the reference program's by a relative error of at most 0.014.
The reference program's roundings to bfloat16 on the way count: a program that leaves them out, or rounds other values in their place, can miss the bound.
Values may be sent and summed in bfloat16 or wider, within the bound.
No kernel may reach another device: no remote copies, remote signals or barrier semaphores. Data moves between devices by JAX's collectives and lax.ppermute only.
A program may use at most 192 MiB of HBM per device.

```python
import math
import jax
import jax.numpy as jnp
import numpy as np
from jax import lax

D = 1024
HEADS = 16
HD = 64
FF = 2624
LENGTH = 1024
SEQS = 8


def draw_hidden_in(key, part):
    positions = jnp.arange(SEQS * LENGTH, dtype=jnp.float32).reshape(SEQS, LENGTH, 1)
    fraction = positions / (SEQS * LENGTH)
    rising = 0.6 * jnp.exp(jnp.log(3.0) * fraction)
    base = jnp.clip(jax.random.normal(key, (SEQS, LENGTH, D), jnp.float32), -4.0, 4.0)
    return (base * rising).astype(jnp.bfloat16)


def draw_valid_tokens(key, part):
    positions = jnp.arange(SEQS * LENGTH, dtype=jnp.int32).reshape(SEQS, LENGTH)
    threshold = 300 + 650 * positions // (SEQS * LENGTH)
    picks = jax.random.randint(jax.random.fold_in(key, 7), (SEQS, LENGTH), 0, 1000, dtype=jnp.int32)
    return (picks < threshold).astype(jnp.int32)


def block_levels(rng, shape, shards, least, high):
    def one(dim, blocks):
        steps = jax.random.uniform(jax.random.fold_in(jax.random.fold_in(rng, 6), dim), (blocks,), jnp.float32, least / len(shards), high / len(shards))
        return jnp.repeat(jnp.exp(steps), shape[dim] // blocks).reshape((-1,) + (1,) * (len(shape) - dim - 1))

    loudness = one(*shards[0])
    for cut in shards[1:]:
        loudness = loudness * one(*cut)
    return loudness


def profile(amount, total, most, slope):
    weights = [(1 << 20) // math.isqrt(rank ** slope) + 1 for rank in range(2, amount + 1)]
    surplus, holding = total - most - (amount - 1), [1] * (amount - 1)
    while surplus > 0:
        candidates = [i for i in range(amount - 1) if holding[i] < most]
        whole, left = sum([weights[i] for i in candidates]), surplus
        for i in candidates:
            more = min(most - holding[i], max(1, left * weights[i] // whole), surplus)
            holding[i] = holding[i] + more
            surplus = surplus - more
    return np.array([most] + holding)


def uneven(rng, number_of, total, bound, slope):
    if number_of == 2:
        one = jax.random.randint(rng, (), max(1, total - bound), min(bound, total - 1) + 1)
        return jnp.stack([one, total - one])
    sizes = jnp.asarray(profile(number_of, total, bound, slope), jnp.int32)
    pairs = (number_of - 1) // 2
    donor, taker = sizes[1:1 + 2 * pairs:2], sizes[2:2 + 2 * pairs:2]
    room = jnp.minimum(donor - 1, bound - taker)
    shifted = jax.random.randint(jax.random.fold_in(rng, 1), (pairs,), 0, 1 << 20) % (room + 1)
    sizes = sizes.at[1:1 + 2 * pairs:2].set(donor - shifted).at[2:2 + 2 * pairs:2].set(taker + shifted)
    return sizes[jax.random.permutation(jax.random.fold_in(rng, 2), number_of)]


def noise(key, extent, deviation, most, split=(), held_as=jnp.bfloat16):
    array = jax.random.normal(key, extent, jnp.float32) * deviation
    if len(split) > 0:
        array = block_levels(key, extent, split, -0.22, 0.18) * array
    return jnp.clip(array, min=-most, max=most).astype(held_as)


def setup_inputs(seed: int = 0) -> dict:
    keys = jax.random.split(jax.random.key(seed), 11)
    hidden_in = draw_hidden_in(jax.random.fold_in(keys[10], 71), 0)
    segment_ids = jax.vmap(lambda own: jnp.searchsorted(jnp.cumsum(uneven(own, max(3, LENGTH // 512), LENGTH, min(2000, LENGTH * 3 // 4), 1)), jnp.arange(LENGTH), side="right"))(jax.random.split(keys[1], SEQS)).reshape((SEQS, LENGTH)).astype(jnp.int32)
    valid_tokens = draw_valid_tokens(jax.random.fold_in(keys[10], 71), 0)
    w_qkv = noise(keys[3], (D, 3 * D), D ** -0.5, 0.1875, ((0, 8),))
    w_attn_out = noise(keys[4], (D, D), (max(1, D // 128)) ** -0.5, 2.0, ((0, 8),))
    w_in_proj = noise(keys[5], (D, 2 * FF), D ** -0.5, 0.1875, ((0, 8),))
    w_out_proj = noise(keys[6], (FF, D), FF ** -0.5, 0.125, ((0, 8),))
    attn_gain = jnp.clip(1.0 + 0.15 * jax.random.normal(keys[7], (D,), jnp.float32), 0.25, 1.75).astype(jnp.bfloat16)
    mlp_gain = jnp.clip(1.0 + 0.15 * jax.random.normal(keys[8], (D,), jnp.float32), 0.25, 1.75).astype(jnp.bfloat16)
    cotangent = noise(keys[9], (SEQS, LENGTH, D), 1.0, 6.0, ((0, 8), (1, 4)))
    return {"hidden_in": hidden_in, "segment_ids": segment_ids, "valid_tokens": valid_tokens, "w_qkv": w_qkv, "w_attn_out": w_attn_out, "w_in_proj": w_in_proj, "w_out_proj": w_out_proj, "attn_gain": attn_gain, "mlp_gain": mlp_gain, "cotangent": cotangent}


ROPE_BASE = 160000.0
NORM_EPS = 1e-05
HIGHEST = lax.Precision.HIGHEST

@jax.custom_vjp
def low(v):
    return lax.optimization_barrier(v.astype(jnp.bfloat16)).astype(jnp.float32)

@jax.custom_vjp
def low_back(v):
    return v

def low_keep(v):
    return (low(v), None)

def low_pass(kept, grad):
    return (grad,)

def back_keep(v):
    return (v, None)

def back_low(kept, grad):
    return (low(grad),)
low.defvjp(low_keep, low_pass)
low_back.defvjp(back_keep, back_low)

def norm_rows(values, gain_row):
    average = lax.optimization_barrier(jnp.mean(values, axis=-1, keepdims=True))
    centered = values - average
    variance = lax.optimization_barrier(jnp.mean(centered * centered, axis=-1, keepdims=True))
    return centered * lax.rsqrt(variance + NORM_EPS) * gain_row

def rotate(head_values, positions):
    half_width = head_values.shape[-1] // 2
    frequency = ROPE_BASE ** (-2.0 * jnp.arange(half_width, dtype=jnp.float32) / head_values.shape[-1])
    angles = positions.astype(jnp.float32)[:, None] * frequency[None, :]
    cosine = jnp.cos(angles)[:, None, :]
    sine_part = jnp.sin(angles)[:, None, :]
    first_half = head_values[..., :half_width]
    second = head_values[..., half_width:]
    return jnp.concatenate([first_half * cosine - second * sine_part, second * cosine + first_half * sine_part], axis=-1)

def gelu_gate(inputs, gates):
    return 0.5 * inputs * (1.0 + jax.scipy.special.erf(inputs * 0.7071067811865476)) * gates

def product(left, right):
    return jnp.dot(left, right, precision=HIGHEST)

def layer_forward(inputs, seg_row, valid_row, gain_one, gain_two, qkv_weight, out_weight, in_weight, down_weight):
    length = inputs.shape[0]
    normed = low(norm_rows(inputs, gain_one))
    projected = low_back(product(normed, qkv_weight)).reshape(length, 3, HEADS, HD)
    positions = jnp.arange(length, dtype=jnp.int32)
    queries = low_back(low(rotate(projected[:, 0], positions)))
    key_heads = low_back(low(rotate(projected[:, 1], positions)))
    value_heads = low_back(low(projected[:, 2]))
    score_scale = float(HD) ** (-0.5)
    block_rows = min(512, length)
    block_count = length // block_rows
    col_ids = jnp.arange(length, dtype=jnp.int32)

    def attend(block_items):
        query_block, seg_block, row_ids = block_items
        scores = low_back(jnp.einsum('qhd,khd->hqk', query_block, key_heads, precision=HIGHEST) * score_scale)
        allowed = (seg_block[:, None] == seg_row[None, :]) & ((valid_row[None, :] > 0) | (row_ids[:, None] == col_ids[None, :]))
        scores = jnp.where(allowed[None], scores, -1e+30)
        row_max = lax.optimization_barrier(jnp.max(scores, axis=-1, keepdims=True))
        exponent = jnp.exp(scores - row_max)
        weights = low(exponent / lax.optimization_barrier(jnp.sum(exponent, axis=-1, keepdims=True)))
        return jnp.einsum('hqk,khd->qhd', weights, value_heads, precision=HIGHEST)
    attended = lax.map(jax.checkpoint(attend), (queries.reshape(block_count, block_rows, HEADS, HD), seg_row.reshape(block_count, block_rows), col_ids.reshape(block_count, block_rows)))
    mixed = low_back(low(attended.reshape(length, D)))
    attn_branch = low_back(product(mixed, out_weight))
    middle = inputs + attn_branch
    normed_two = low(norm_rows(middle, gain_two))
    widened = low_back(product(normed_two, in_weight))
    hidden = low(gelu_gate(widened[:, :FF], widened[:, FF:]))
    mlp_branch = low_back(product(hidden, down_weight))
    return (middle + mlp_branch, (attn_branch, mlp_branch))

def reference(hidden_in, segment_ids, valid_tokens, w_qkv, w_attn_out, w_in_proj, w_out_proj, attn_gain, mlp_gain, cotangent):
    weights = (attn_gain.astype(jnp.float32), mlp_gain.astype(jnp.float32), w_qkv.astype(jnp.float32), w_attn_out.astype(jnp.float32), w_in_proj.astype(jnp.float32), w_out_proj.astype(jnp.float32))

    def one_sequence(carried, seq_items):
        grad_totals, stat_totals = carried
        inputs, seg_row, valid_row, grad_row = seq_items

        def forward(inputs, *params):
            return layer_forward(inputs, seg_row, valid_row, *params)
        result, pull, branches = jax.vjp(forward, inputs.astype(jnp.float32), *weights, has_aux=True)
        gradients = pull(grad_row.astype(jnp.float32))
        attn_branch, mlp_branch = branches
        valid_col = valid_row.astype(jnp.float32)[:, None]
        stat_terms = jnp.stack([jnp.sum(valid_col * result * result), jnp.sum(valid_col * attn_branch * attn_branch), jnp.sum(valid_col * mlp_branch * mlp_branch), jnp.sum(valid_col)])
        new_totals = tuple((summed + gradient for summed, gradient in zip(grad_totals, gradients[1:])))
        return ((new_totals, stat_totals + stat_terms), (result.astype(jnp.bfloat16), gradients[0]))
    start = (tuple((jnp.zeros_like(weight) for weight in weights)), jnp.zeros((4,), jnp.float32))
    (grad_totals, stat_totals), (outputs, input_grads) = lax.scan(one_sequence, start, (hidden_in, segment_ids, valid_tokens, cotangent))
    valid_count = jnp.maximum(stat_totals[3], 1.0)
    root_means = jnp.sqrt(stat_totals[:3] / (valid_count * D))
    return (outputs, input_grads, grad_totals[2], grad_totals[3], grad_totals[4], grad_totals[5], grad_totals[0], grad_totals[1], root_means)
```

```python
import functools

import jax
import jax.numpy as jnp
from jax import lax
from jax.experimental import pallas as pl
from jax.experimental.pallas import tpu as pltpu
from jax.sharding import PartitionSpec as P

D = 1024
HEADS = 16
HD = 64
FF = 2624

ROPE_BASE = 160000.0
NORM_EPS = 1e-05
BF = jnp.bfloat16
F32 = jnp.float32


def swap(x, axis, bit):
    return lax.ppermute(x, axis, [(i, i ^ bit) for i in range(lax.axis_size(axis))])


def share_seq(block):
    size = lax.axis_size("seq")
    if size != 4:
        return [block] + [swap(block, "seq", k) for k in range(1, size)]
    half = block.shape[0] // 2
    one = swap(block, "seq", 1)
    two = swap(block, "seq", 2)
    upper = swap(two[:half], "seq", 1)
    lower = swap(one[half:], "seq", 2)
    return [block, one, two, jnp.concatenate([upper, lower], axis=0)]


def reduce_seq(blocks):
    total = blocks[0]
    for k in range(1, len(blocks)):
        total = total + swap(blocks[k].astype(BF), "seq", k).astype(F32)
    return total


def reduce_seq_relay(blocks):
    if len(blocks) != 4:
        return reduce_seq(blocks)
    own, one, two, three = blocks
    half = own.shape[0] // 2
    upper = swap(three[:half].astype(BF), "seq", 1).astype(F32)
    lower = swap(three[half:].astype(BF), "seq", 2).astype(F32)
    to_two = jnp.concatenate([two[:half] + upper, two[half:]], axis=0).astype(BF)
    to_one = jnp.concatenate([one[:half], one[half:] + lower], axis=0).astype(BF)
    return own + swap(to_two, "seq", 2).astype(F32) + swap(to_one, "seq", 1).astype(F32)


def paired():
    return lax.axis_size("fsdp") == 2 * lax.axis_size("seq")


def spread_rows(block):
    size = lax.axis_size("fsdp")
    same = [block] + [swap(block, "fsdp", k) for k in range(2, size, 2)]
    other = [swap(b, "fsdp", 1) for b in same]
    return [b for pair in zip(same, other) for b in pair]


def gather_rows(block):
    if not paired():
        return lax.all_gather(block, "fsdp", axis=0)
    me = lax.axis_index("fsdp")
    parts = spread_rows(block)
    whole = jnp.zeros((len(parts),) + block.shape, block.dtype)
    for k, part in enumerate(parts):
        whole = lax.dynamic_update_index_in_dim(whole, part, me ^ k, 0)
    return whole


def transpose_devices(x):
    seq, fsdp = lax.axis_size("seq"), lax.axis_size("fsdp")
    pairs = [
        (s * fsdp + 2 * z + c, z * fsdp + 2 * s + c)
        for s in range(seq)
        for z in range(fsdp // 2)
        for c in range(2)
    ]
    return lax.ppermute(x, ("seq", "fsdp"), pairs)


def stack_seq(block):
    me = lax.axis_index("seq")
    parts = share_seq(block)
    whole = jnp.zeros((len(parts),) + block.shape, block.dtype)
    for k, part in enumerate(parts):
        whole = lax.dynamic_update_index_in_dim(whole, part, me ^ k, 0)
    return whole


def reduce_z(blocks):
    count = blocks.shape[0]
    z = lax.axis_index("fsdp") // 2
    low = blocks.astype(BF)
    total = lax.dynamic_index_in_dim(blocks, z, 0, keepdims=False)
    for k in range(1, count):
        part = lax.dynamic_index_in_dim(low, z ^ k, 0, keepdims=False)
        total = total + swap(part, "fsdp", 2 * k).astype(F32)
    return total


def reduce_core(pairs):
    core = lax.axis_index("fsdp") % 2
    away = lax.dynamic_index_in_dim(pairs, 1 - core, 1, keepdims=False)
    mine = lax.dynamic_index_in_dim(pairs, core, 1, keepdims=False)
    return mine + swap(away.astype(BF), "fsdp", 1).astype(F32)


def reduce_rows(partial):
    size = lax.axis_size("fsdp")
    if not paired():
        return lax.psum_scatter(partial, "fsdp", scatter_dimension=0, tiled=True)
    rows = partial.shape[0] // size
    return reduce_z(reduce_core(partial.reshape(size // 2, 2, rows, partial.shape[1])))


def sum_everywhere(values):
    for axis in ("fsdp", "seq"):
        bit = 1
        while bit < lax.axis_size(axis):
            values = values + swap(values, axis, bit)
            bit *= 2
    return values


def gather_gains(gains):
    size, rows = lax.axis_size("fsdp"), gains.shape[1]
    whole = jnp.zeros((2, size * rows), gains.dtype)
    whole = lax.dynamic_update_slice(whole, gains, (0, lax.axis_index("fsdp") * rows))
    bit = 1
    while bit < size:
        whole = whole + swap(whole, "fsdp", bit)
        bit *= 2
    return whole


def half_swap(values):
    width = values.shape[1]
    lane = lax.broadcasted_iota(jnp.int32, values.shape, 1)
    ahead = pltpu.roll(values, width - HD // 2, 1)
    behind = pltpu.roll(values, HD // 2, 1)
    return jnp.where(lane % HD < HD // 2, ahead, behind)


def wide(table, width):
    return jnp.concatenate([table] * (width // table.shape[1]), axis=1)


def qkv_kernel(*refs):
    count = 4
    xs = refs[:count]
    w_ref, gain_ref, cos_ref, sin_ref, a_ref, q_ref, k_ref, v_ref, held = refs[count:]
    step = pl.program_id(0)
    for i in range(count):

        @pl.when(step == i)
        def _():
            held[...] = xs[i][...].astype(F32)

    values = held[...]
    centered = values - jnp.mean(values, axis=1, keepdims=True)
    variance = jnp.mean(centered * centered, axis=1, keepdims=True)
    low = (centered * lax.rsqrt(variance + NORM_EPS) * gain_ref[...]).astype(BF)
    a_ref[...] = low
    p = jnp.dot(low, w_ref[...], preferred_element_type=F32)
    part = p.shape[1] // 3
    turned = p[:, : 2 * part]
    turned = turned * wide(cos_ref[...], 2 * part) + half_swap(turned) * wide(sin_ref[...], 2 * part)
    q_ref[...] = turned[:, :part].astype(BF) * (HD**-0.5)
    k_ref[...] = turned[:, part:].astype(BF)
    v_ref[...] = p[:, 2 * part :].astype(BF)


def project_qkv(blocks, weight, gain, cosine, sine):
    rows, width = blocks[0].shape
    part = weight.shape[1] // 3
    count = len(blocks)
    whole = lambda a: pl.BlockSpec(a.shape, lambda i: (0, 0))
    tile = lambda n: pl.BlockSpec((rows, n), lambda i: (i, 0))
    shape = lambda n: jax.ShapeDtypeStruct((rows * count, n), BF)
    return pl.pallas_call(
        qkv_kernel,
        grid=(count,),
        in_specs=[whole(b) for b in blocks]
        + [whole(weight), whole(gain), tile(cosine.shape[1]), tile(sine.shape[1])],
        out_specs=[tile(width), tile(part), tile(part), tile(part)],
        out_shape=[shape(width), shape(part), shape(part), shape(part)],
        scratch_shapes=[pltpu.VMEM((rows, width), F32)],
        cost_estimate=pl.CostEstimate(
            flops=2 * rows * count * width * 3 * part,
            bytes_accessed=2 * rows * count * (2 * width + 3 * part) + 2 * width * 3 * part,
            transcendentals=0,
        ),
        name="qkv",
    )(*blocks, weight, gain, cosine, sine)


def mask_bias(seg_col, valid_col, seg_row, first_row):
    shape = (seg_col.shape[0], seg_row.shape[1])
    key = lax.broadcasted_iota(jnp.int32, shape, 0)
    query = lax.broadcasted_iota(jnp.int32, shape, 1) + first_row
    allowed = (seg_col == seg_row) & ((valid_col > 0) | (key == query))
    return jnp.where(allowed, 0.0, -1e30)


def forward_kernel(q_ref, k_ref, v_ref, segc_ref, valc_ref, segr_ref, o_ref, lse_ref, vt_ref, ot_ref, bias_ref):
    step = pl.program_id(0)
    rows, width = q_ref.shape

    @pl.when(step == 0)
    def _():
        vt_ref[...] = v_ref[...].T

    bias_ref[...] = mask_bias(segc_ref[...], valc_ref[...], segr_ref[...], step * rows)
    qt = q_ref[...].T
    feature = lax.broadcasted_iota(jnp.int32, qt.shape, 0) // HD

    def head(h, carry):
        mine = jnp.where(feature == h, qt, jnp.zeros_like(qt))
        scores = jnp.dot(k_ref[...], mine, preferred_element_type=F32) + bias_ref[...]
        top = jnp.max(scores, axis=0, keepdims=True)
        exponent = jnp.exp(scores - top)
        total = jnp.sum(exponent, axis=0, keepdims=True)
        weights = (exponent * (1.0 / total)).astype(BF)
        start = pl.multiple_of(h * HD, HD)
        ot_ref[pl.ds(start, HD), :] = jnp.dot(
            vt_ref[pl.ds(start, HD), :], weights, preferred_element_type=F32
        )
        lse_ref[pl.ds(h, 1), :] = top + jnp.log(total)
        return carry

    lax.fori_loop(0, width // HD, head, 0)
    o_ref[...] = ot_ref[...].T.astype(BF)


def attend_forward(q, k, v, seg_col, valid_col, seg_row, rows):
    length, width = q.shape
    whole = lambda a: pl.BlockSpec(a.shape, lambda i: (0, 0))
    tile = pl.BlockSpec((rows, width), lambda i: (i, 0))
    return pl.pallas_call(
        forward_kernel,
        grid=(length // rows,),
        in_specs=[tile, whole(k), whole(v), whole(seg_col), whole(valid_col), pl.BlockSpec((1, rows), lambda i: (0, i))],
        out_specs=[tile, pl.BlockSpec((8, rows), lambda i: (0, i))],
        out_shape=[jax.ShapeDtypeStruct((length, width), BF), jax.ShapeDtypeStruct((8, length), F32)],
        scratch_shapes=[pltpu.VMEM((width, length), BF), pltpu.VMEM((width, rows), F32), pltpu.VMEM((length, rows), F32)],
        cost_estimate=pl.CostEstimate(
            flops=4 * length * length * width, bytes_accessed=8 * length * width, transcendentals=length * length * 4
        ),
        name="attend",
    )(q, k, v, seg_col, valid_col, seg_row)


def backward_kernel(
    q_ref, go_ref, lse_ref, k_ref, v_ref, segc_ref, valc_ref, segr_ref, cos_ref, sin_ref,
    gp_ref, kt_ref, dk_ref, dv_ref, dqt_ref, bias_ref,
):
    step = pl.program_id(0)
    rows, width = q_ref.shape

    @pl.when(step == 0)
    def _():
        kt_ref[...] = k_ref[...].T
        dk_ref[...] = jnp.zeros_like(dk_ref)
        dv_ref[...] = jnp.zeros_like(dv_ref)

    bias_ref[...] = mask_bias(segc_ref[...], valc_ref[...], segr_ref[...], step * rows)
    qt, got = q_ref[...].T, go_ref[...].T
    feature = lax.broadcasted_iota(jnp.int32, qt.shape, 0) // HD
    lane = lax.broadcasted_iota(jnp.int32, (rows, width), 1) // HD
    none = jnp.zeros_like(qt)
    none_row = jnp.zeros((rows, width), BF)

    def head(h, carry):
        scores = jnp.dot(k_ref[...], jnp.where(feature == h, qt, none), preferred_element_type=F32)
        weights = jnp.exp(scores + bias_ref[...] - lse_ref[pl.ds(h, 1), :])
        upstream = jnp.dot(v_ref[...], jnp.where(feature == h, got, none), preferred_element_type=F32)
        inner = jnp.sum(weights * upstream, axis=0, keepdims=True)
        low = (weights * (upstream - inner)).astype(BF)
        dv_ref[...] += jnp.dot(
            weights.astype(BF), jnp.where(lane == h, go_ref[...], none_row), preferred_element_type=F32
        )
        dk_ref[...] += jnp.dot(low, jnp.where(lane == h, q_ref[...], none_row), preferred_element_type=F32)
        start = pl.multiple_of(h * HD, HD)
        dqt_ref[pl.ds(start, HD), :] = jnp.dot(kt_ref[pl.ds(start, HD), :], low, preferred_element_type=F32)
        return carry

    lax.fori_loop(0, width // HD, head, 0)

    def unturn(values, cosine, sine):
        values = values.astype(BF).astype(F32)
        return (values * wide(cosine, width) - half_swap(values) * wide(sine, width)).astype(BF)

    here = pl.ds(pl.multiple_of(step * rows, rows), rows)
    gp_ref[here, :width] = unturn(dqt_ref[...].T * (HD**-0.5), cos_ref[here, :], sin_ref[here, :])

    @pl.when(step == pl.num_programs(0) - 1)
    def _():
        gp_ref[:, width : 2 * width] = unturn(dk_ref[...], cos_ref[...], sin_ref[...])
        gp_ref[:, 2 * width :] = dv_ref[...].astype(BF)


def attend_backward(q, k, v, grad_out, lse, seg_col, valid_col, seg_row, cosine, sine, rows):
    length, width = q.shape
    whole = lambda a: pl.BlockSpec(a.shape, lambda i: (0, 0))
    tile = pl.BlockSpec((rows, width), lambda i: (i, 0))
    return pl.pallas_call(
        backward_kernel,
        grid=(length // rows,),
        in_specs=[
            tile, tile, pl.BlockSpec((8, rows), lambda i: (0, i)), whole(k), whole(v),
            whole(seg_col), whole(valid_col), pl.BlockSpec((1, rows), lambda i: (0, i)), whole(cosine), whole(sine),
        ],
        out_specs=pl.BlockSpec((length, 3 * width), lambda i: (0, 0)),
        out_shape=jax.ShapeDtypeStruct((length, 3 * width), BF),
        scratch_shapes=[
            pltpu.VMEM((width, length), BF), pltpu.VMEM((length, width), F32), pltpu.VMEM((length, width), F32),
            pltpu.VMEM((width, rows), F32), pltpu.VMEM((length, rows), F32),
        ],
        cost_estimate=pl.CostEstimate(
            flops=10 * length * length * width, bytes_accessed=20 * length * width, transcendentals=length * length * 4
        ),
        name="attend_back",
    )(q, grad_out, lse, k, v, seg_col, valid_col, seg_row, cosine, sine)


def normal(values):
    centered = values - jnp.mean(values, axis=-1, keepdims=True)
    scale = lax.rsqrt(jnp.mean(centered * centered, axis=-1, keepdims=True) + NORM_EPS)
    return centered * scale, scale


def norm_back(upstream, gain, values):
    unit, scale = normal(values)
    weighted = upstream * gain
    return scale * (
        weighted
        - jnp.mean(weighted, axis=-1, keepdims=True)
        - unit * jnp.mean(weighted * unit, axis=-1, keepdims=True)
    )


def gelu_gate(inputs, gates):
    return 0.5 * inputs * (1.0 + lax.erf(inputs * 0.7071067811865476)) * gates


def matmul(a, b):
    return jnp.dot(a, b, preferred_element_type=F32)


def matmul_nt(a, b):
    return lax.dot_general(a, b, (((1,), (1,)), ((), ())), preferred_element_type=F32)


def matmul_tn(a, b):
    return lax.dot_general(a, b, (((0,), (0,)), ((), ())), preferred_element_type=F32)


def on_device(
    hidden_in, segment_ids, valid_tokens, w_qkv, w_attn_out, w_in_proj, w_out_proj, attn_gain, mlp_gain, cotangent
):
    seq_size, fsdp_size = lax.axis_size("seq"), lax.axis_size("fsdp")
    seq, fsdp = lax.axis_index("seq"), lax.axis_index("fsdp")
    x_low, cot = hidden_in[0], cotangent[0]
    tokens = x_low.shape[0]
    length = tokens * seq_size
    part = D // seq_size
    hidden = FF // seq_size
    rel = [seq ^ k for k in range(seq_size)]

    x_blocks = share_seq(x_low)
    gains = gather_gains(jnp.stack([attn_gain, mlp_gain])).astype(F32)
    gain_one, gain_two = gains[0:1], gains[1:2]
    qkv_mine = jnp.concatenate(
        [lax.dynamic_slice_in_dim(w_qkv, i * D + seq * part, part, axis=1) for i in range(3)], axis=1
    )
    qkv_weight = gather_rows(qkv_mine).reshape(D, 3 * part)
    cot_blocks = share_seq(cot)
    in_mine = jnp.stack(
        [lax.dynamic_slice_in_dim(w_in_proj, i * FF + seq * hidden, hidden, axis=1) for i in range(2)]
    )
    in_weight = jnp.swapaxes(gather_rows(in_mine), 0, 1).reshape(2, D, hidden)
    if paired():
        down_mine = transpose_devices(lax.dynamic_slice_in_dim(w_out_proj, seq * part, part, axis=1))
        down_weight = gather_rows(down_mine).reshape(seq_size, 2, down_mine.shape[0], part)
        down_weight = down_weight.transpose(1, 2, 0, 3).reshape(hidden, D)
        out_mine = gather_rows(lax.dynamic_slice_in_dim(w_attn_out, seq * part, part, axis=1)).reshape(D, part)
        out_cols = stack_seq(out_mine)
        out_weight = jnp.swapaxes(out_cols, 0, 1).reshape(D, D)
    else:
        down_weight = lax.all_gather(w_out_proj, "fsdp", axis=0, tiled=True)
        down_weight = lax.dynamic_slice_in_dim(down_weight, seq * hidden, hidden, axis=0)
        out_weight = lax.all_gather(w_attn_out, "fsdp", axis=0, tiled=True)

    def by_block(row):
        return jnp.concatenate([lax.dynamic_slice_in_dim(row, r * tokens, tokens) for r in rel])

    seg_all, valid_all = by_block(segment_ids[0]), by_block(valid_tokens[0])
    positions = by_block(jnp.arange(length, dtype=jnp.int32))
    frequency = ROPE_BASE ** (-2.0 * jnp.arange(HD // 2, dtype=F32) / HD)
    angles = positions.astype(F32)[:, None] * frequency[None, :]
    cosine, sine = lax.optimization_barrier((jnp.cos(angles), jnp.sin(angles)))
    cosine = jnp.concatenate([cosine] * 4, axis=1)
    sine = jnp.concatenate([-sine, sine] * 2, axis=1)
    seg_col, valid_col, seg_row = seg_all[:, None], valid_all[:, None], seg_all[None, :]

    a_low, q, k, v = project_qkv(x_blocks, qkv_weight, gain_one, cosine, sine)
    mixed, lse = attend_forward(q, k, v, seg_col, valid_col, seg_row, tokens)

    def to_tokens(blocks):
        came = [blocks[:tokens]] + [
            swap(blocks[i * tokens : (i + 1) * tokens], "seq", i) for i in range(1, seq_size)
        ]
        whole = jnp.zeros((tokens, D), blocks.dtype)
        for r, block in zip(rel, came):
            whole = lax.dynamic_update_slice(whole, block, (0, r * part))
        return whole

    mixed_low = to_tokens(mixed)
    x = x_low.astype(F32)
    attn_branch = matmul(mixed_low, out_weight)
    middle = x + attn_branch
    normed_two = (normal(middle)[0] * gain_two).astype(BF)

    b_blocks = share_seq(normed_two)
    m_blocks, gz_i, gz_g, gb_blocks = [], [], [], []
    for b, g in zip(b_blocks, cot_blocks):
        grad_hidden = matmul_nt(g, down_weight)
        inner, gate = matmul(b, in_weight[0]), matmul(b, in_weight[1])
        value, pull = jax.vjp(gelu_gate, inner, gate)
        gi, gg = pull(grad_hidden)
        gi, gg = gi.astype(BF), gg.astype(BF)
        m_blocks.append(value.astype(BF))
        gz_i.append(gi)
        gz_g.append(gg)
        gb_blocks.append(matmul_nt(gi, in_weight[0]) + matmul_nt(gg, in_weight[1]))
    grad_normed_two = reduce_seq(gb_blocks)
    grad_middle = cot.astype(F32) + norm_back(grad_normed_two, gain_two, middle)
    grad_attn_low = grad_middle.astype(BF)
    grad_mixed = matmul_nt(grad_attn_low, out_weight).astype(BF)

    def to_heads(blocks):
        sent = [lax.dynamic_slice_in_dim(blocks, r * part, part, axis=1) for r in rel]
        return jnp.concatenate([sent[0]] + [swap(sent[i], "seq", i) for i in range(1, seq_size)], axis=0)

    grad_by_heads = to_heads(grad_mixed)

    mlp_branch = reduce_seq([matmul(m, down_weight) for m in m_blocks])
    result = middle + mlp_branch
    valid_mine = valid_all[:tokens].astype(F32)[:, None]
    stats = jnp.stack(
        [
            jnp.sum(valid_mine * result * result),
            jnp.sum(valid_mine * attn_branch * attn_branch),
            jnp.sum(valid_mine * mlp_branch * mlp_branch),
            jnp.sum(valid_mine),
        ]
    )
    stats = sum_everywhere(jnp.broadcast_to(stats[:, None], (4, 128)))[:, 0]
    root_means = jnp.sqrt(stats[:3] / (jnp.maximum(stats[3], 1.0) * D))

    def share_columns(mine):
        rows, count, width = mine.shape
        low = mine.astype(BF)
        if paired():
            every = stack_seq(low)
        else:
            every = lax.all_gather(low, "seq", axis=0)
        return every.transpose(1, 2, 0, 3).reshape(rows, count * seq_size * width).astype(F32)

    b_all, m_all = jnp.concatenate(b_blocks), jnp.concatenate(m_blocks)
    cot_all = jnp.concatenate(cot_blocks)
    gz_all = jnp.concatenate([jnp.concatenate(gz_i), jnp.concatenate(gz_g)], axis=1)
    grad_in_mine = reduce_rows(matmul_tn(b_all, gz_all))
    grad_in_weight = share_columns(grad_in_mine.reshape(-1, 2, hidden))
    grad_down_part = matmul_tn(m_all, cot_all)
    grad_out_part = matmul_tn(mixed_low, grad_attn_low)
    if paired():
        rows = hidden // 2
        halves = reduce_core(grad_down_part.reshape(1, 2, rows, D))[0]
        quarter = reduce_z(halves.reshape(rows, seq_size, part).transpose(1, 0, 2))
        quarter = transpose_devices(quarter.astype(BF)).astype(F32)
        grad_down = share_columns(quarter[:, None, :])
        rows = D // fsdp_size
        out_core = reduce_core(grad_out_part.reshape(fsdp_size // 2, 2, rows, D)).reshape(D // 2, D)
        out_seq = reduce_seq([lax.dynamic_slice_in_dim(out_core, r * part, part, axis=1) for r in rel])
        out_mine = reduce_z(out_seq.reshape(fsdp_size // 2, rows, part))
        grad_out_weight = share_columns(out_mine[:, None, :])
    else:
        spread = jnp.zeros((FF, D), F32)
        spread = lax.dynamic_update_slice(spread, grad_down_part, (seq * hidden, 0))
        grad_down = lax.psum(lax.psum_scatter(spread, "fsdp", scatter_dimension=0, tiled=True), "seq")
        grad_out_weight = lax.psum(
            lax.psum_scatter(grad_out_part, "fsdp", scatter_dimension=0, tiled=True), "seq"
        )

    gp = attend_backward(
        q, k, v, grad_by_heads, lse, seg_col, valid_col, seg_row, cosine, sine, tokens
    )
    ga_parts = matmul_nt(gp, qkv_weight)
    grad_qkv_mine = reduce_rows(matmul_tn(a_low, gp))
    grad_normed = reduce_seq_relay([ga_parts[i * tokens : (i + 1) * tokens] for i in range(seq_size)])
    grad_inputs = grad_middle + norm_back(grad_normed, gain_one, x)
    grad_qkv_weight = share_columns(grad_qkv_mine.reshape(-1, 3, part))

    def gain_gradient(weight, gradient, gain):
        return jnp.sum(weight.astype(F32) * gradient, axis=1) / gain.astype(F32)

    return (
        result.astype(BF)[None],
        grad_inputs[None],
        grad_qkv_weight,
        grad_out_weight,
        grad_in_weight,
        grad_down,
        gain_gradient(w_qkv, grad_qkv_weight, attn_gain),
        gain_gradient(w_in_proj, grad_in_weight, mlp_gain),
        root_means,
    )


def solution(mesh):
    in_specs = (
        P("fsdp", "seq", None),
        P("fsdp", None),
        P("fsdp", None),
        P("fsdp", None),
        P("fsdp", None),
        P("fsdp", None),
        P("fsdp", None),
        P("fsdp"),
        P("fsdp"),
        P("fsdp", "seq", None),
    )
    out_specs = (
        P("fsdp", "seq", None),
        P("fsdp", "seq", None),
        P("fsdp", None),
        P("fsdp", None),
        P("fsdp", None),
        P("fsdp", None),
        P("fsdp"),
        P("fsdp"),
        P(),
    )
    return jax.shard_map(on_device, mesh=mesh, in_specs=in_specs, out_specs=out_specs, check_vma=False)
```

```python
import functools

import jax
import jax.numpy as jnp
from jax import lax
from jax.experimental import pallas as pl
from jax.experimental.pallas import tpu as pltpu
from jax.sharding import PartitionSpec as P

D = 1024
HEADS = 16
HD = 64
FF = 2624

ROPE_BASE = 160000.0
NORM_EPS = 1e-05
LANES = 128
BF = jnp.bfloat16
F32 = jnp.float32


def swap(x, axis, bit):
    return lax.ppermute(x, axis, [(i, i ^ bit) for i in range(lax.axis_size(axis))])


def after(x, *others):
    return lax.optimization_barrier((x, others))[0]


def share_seq(block):
    return [block] + [swap(block, "seq", k) for k in range(1, lax.axis_size("seq"))]


def reduce_seq(blocks):
    total = blocks[0]
    for k in range(1, len(blocks)):
        total = total + swap(blocks[k].astype(BF), "seq", k).astype(F32)
    return total


def paired():
    return lax.axis_size("fsdp") == 2 * lax.axis_size("seq")


def gather_rows(block):
    return lax.all_gather(block, "fsdp", axis=0, tiled=True)


def transpose_devices(x):
    seq, fsdp = lax.axis_size("seq"), lax.axis_size("fsdp")
    pairs = [
        (s * fsdp + 2 * z + c, z * fsdp + 2 * s + c)
        for s in range(seq)
        for z in range(fsdp // 2)
        for c in range(2)
    ]
    return lax.ppermute(x, ("seq", "fsdp"), pairs)


def reduce_rows(mine, away, size):
    mine = mine + swap(away, "fsdp", 1).astype(F32)
    rows = mine.shape[0] // (size // 2)
    total = mine[:rows]
    for k in range(1, size // 2):
        part = mine[k * rows : (k + 1) * rows].astype(BF)
        total = total + swap(part, "fsdp", 2 * k).astype(F32)
    return total


def sum_everywhere(values):
    for axis in ("fsdp", "seq"):
        bit = 1
        while bit < lax.axis_size(axis):
            values = values + swap(values, axis, bit)
            bit *= 2
    return values


def gather_gains(gains):
    size, rows = lax.axis_size("fsdp"), gains.shape[1]
    whole = jnp.zeros((2, size * rows), gains.dtype)
    whole = lax.dynamic_update_slice(whole, gains, (0, lax.axis_index("fsdp") * rows))
    bit = 1
    while bit < size:
        whole = whole + swap(whole, "fsdp", bit)
        bit *= 2
    return whole


def half_swap(values):
    width = values.shape[1]
    lane = lax.broadcasted_iota(jnp.int32, values.shape, 1)
    ahead = pltpu.roll(values, width - HD // 2, 1)
    behind = pltpu.roll(values, HD // 2, 1)
    return jnp.where(lane % HD < HD // 2, ahead, behind)


def wide(table, width):
    return jnp.concatenate([table] * (width // table.shape[1]), axis=1)


def qkv_kernel(*refs):
    count = 4
    xs = refs[:count]
    w_ref, gain_ref, cos_ref, sin_ref, a_ref, q_ref, k_ref, v_ref, held = refs[count:]
    step = pl.program_id(0)
    for i in range(count):

        @pl.when(step == i)
        def _():
            held[...] = xs[i][...].astype(F32)

    values = held[...]
    centered = values - jnp.mean(values, axis=1, keepdims=True)
    variance = jnp.mean(centered * centered, axis=1, keepdims=True)
    low = (centered * lax.rsqrt(variance + NORM_EPS) * gain_ref[...]).astype(BF)
    a_ref[...] = low
    p = jnp.dot(low, w_ref[...], preferred_element_type=F32)
    part = p.shape[1] // 3
    turned = p[:, : 2 * part]
    turned = turned * wide(cos_ref[...], 2 * part) + half_swap(turned) * wide(sin_ref[...], 2 * part)
    q_ref[...] = turned[:, :part].astype(BF) * (HD**-0.5)
    k_ref[...] = turned[:, part:].astype(BF)
    v_ref[...] = p[:, 2 * part :].astype(BF)


def project_qkv(blocks, weight, gain, cosine, sine):
    rows, width = blocks[0].shape
    part = weight.shape[1] // 3
    count = len(blocks)
    whole = lambda a: pl.BlockSpec(a.shape, lambda i: (0, 0))
    tile = lambda n: pl.BlockSpec((rows, n), lambda i: (i, 0))
    shape = lambda n: jax.ShapeDtypeStruct((rows * count, n), BF)
    return pl.pallas_call(
        qkv_kernel,
        grid=(count,),
        in_specs=[whole(b) for b in blocks]
        + [whole(weight), whole(gain), tile(cosine.shape[1]), tile(sine.shape[1])],
        out_specs=[tile(width), tile(part), tile(part), tile(part)],
        out_shape=[shape(width), shape(part), shape(part), shape(part)],
        scratch_shapes=[pltpu.VMEM((rows, width), F32)],
        cost_estimate=pl.CostEstimate(
            flops=2 * rows * count * width * 3 * part,
            bytes_accessed=2 * rows * count * (2 * width + 3 * part) + 2 * width * 3 * part,
            transcendentals=0,
        ),
        name="qkv",
    )(*blocks, weight, gain, cosine, sine)


def mask_bias(seg_col, valid_col, seg_row, first_row):
    shape = (seg_col.shape[0], seg_row.shape[1])
    key = lax.broadcasted_iota(jnp.int32, shape, 0)
    query = lax.broadcasted_iota(jnp.int32, shape, 1) + first_row
    allowed = (seg_col == seg_row) & ((valid_col > 0) | (key == query))
    return jnp.where(allowed, 0.0, -1e30)


def forward_kernel(q_ref, k_ref, v_ref, segc_ref, valc_ref, segr_ref, o_ref, lse_ref, vt_ref, ot_ref, bias_ref):
    step = pl.program_id(0)
    rows, width = q_ref.shape

    @pl.when(step == 0)
    def _():
        vt_ref[...] = v_ref[...].T

    bias_ref[...] = mask_bias(segc_ref[...], valc_ref[...], segr_ref[...], step * rows)
    qt = q_ref[...].T
    feature = lax.broadcasted_iota(jnp.int32, qt.shape, 0) // HD

    def head(h, carry):
        mine = jnp.where(feature == h, qt, jnp.zeros_like(qt))
        scores = jnp.dot(k_ref[...], mine, preferred_element_type=F32) + bias_ref[...]
        top = jnp.max(scores, axis=0, keepdims=True)
        exponent = jnp.exp(scores - top)
        total = jnp.sum(exponent, axis=0, keepdims=True)
        weights = (exponent * (1.0 / total)).astype(BF)
        start = pl.multiple_of(h * HD, HD)
        ot_ref[pl.ds(start, HD), :] = jnp.dot(
            vt_ref[pl.ds(start, HD), :], weights, preferred_element_type=F32
        )
        lse_ref[pl.ds(h, 1), :] = top + jnp.log(total)
        return carry

    lax.fori_loop(0, width // HD, head, 0)
    o_ref[...] = ot_ref[...].T.astype(BF)


def attend_forward(q, k, v, seg_col, valid_col, seg_row, rows):
    length, width = q.shape
    whole = lambda a: pl.BlockSpec(a.shape, lambda i: (0, 0))
    tile = pl.BlockSpec((rows, width), lambda i: (i, 0))
    return pl.pallas_call(
        forward_kernel,
        grid=(length // rows,),
        in_specs=[tile, whole(k), whole(v), whole(seg_col), whole(valid_col), pl.BlockSpec((1, rows), lambda i: (0, i))],
        out_specs=[tile, pl.BlockSpec((8, rows), lambda i: (0, i))],
        out_shape=[jax.ShapeDtypeStruct((length, width), BF), jax.ShapeDtypeStruct((8, length), F32)],
        scratch_shapes=[pltpu.VMEM((width, length), BF), pltpu.VMEM((width, rows), F32), pltpu.VMEM((length, rows), F32)],
        cost_estimate=pl.CostEstimate(
            flops=4 * length * length * width, bytes_accessed=8 * length * width, transcendentals=length * length * 4
        ),
        name="attend",
    )(q, k, v, seg_col, valid_col, seg_row)


def backward_kernel(
    q_ref, go_ref, lse_ref, k_ref, v_ref, segc_ref, valc_ref, segr_ref, cos_ref, sin_ref,
    gp_ref, kt_ref, dk_ref, dv_ref, dqt_ref, bias_ref,
):
    step = pl.program_id(0)
    rows, width = q_ref.shape

    @pl.when(step == 0)
    def _():
        kt_ref[...] = k_ref[...].T
        dk_ref[...] = jnp.zeros_like(dk_ref)
        dv_ref[...] = jnp.zeros_like(dv_ref)

    bias_ref[...] = mask_bias(segc_ref[...], valc_ref[...], segr_ref[...], step * rows)
    qt, got = q_ref[...].T, go_ref[...].T
    feature = lax.broadcasted_iota(jnp.int32, qt.shape, 0) // HD
    lane = lax.broadcasted_iota(jnp.int32, (rows, width), 1) // HD
    none = jnp.zeros_like(qt)
    none_row = jnp.zeros((rows, width), BF)

    def head(h, carry):
        scores = jnp.dot(k_ref[...], jnp.where(feature == h, qt, none), preferred_element_type=F32)
        weights = jnp.exp(scores + bias_ref[...] - lse_ref[pl.ds(h, 1), :])
        upstream = jnp.dot(v_ref[...], jnp.where(feature == h, got, none), preferred_element_type=F32)
        inner = jnp.sum(weights * upstream, axis=0, keepdims=True)
        low = (weights * (upstream - inner)).astype(BF)
        dv_ref[...] += jnp.dot(
            weights.astype(BF), jnp.where(lane == h, go_ref[...], none_row), preferred_element_type=F32
        )
        dk_ref[...] += jnp.dot(low, jnp.where(lane == h, q_ref[...], none_row), preferred_element_type=F32)
        start = pl.multiple_of(h * HD, HD)
        dqt_ref[pl.ds(start, HD), :] = jnp.dot(kt_ref[pl.ds(start, HD), :], low, preferred_element_type=F32)
        return carry

    lax.fori_loop(0, width // HD, head, 0)

    def unturn(values, cosine, sine):
        values = values.astype(BF).astype(F32)
        return (values * wide(cosine, width) - half_swap(values) * wide(sine, width)).astype(BF)

    here = pl.ds(pl.multiple_of(step * rows, rows), rows)
    gp_ref[here, :width] = unturn(dqt_ref[...].T * (HD**-0.5), cos_ref[here, :], sin_ref[here, :])

    @pl.when(step == pl.num_programs(0) - 1)
    def _():
        gp_ref[:, width : 2 * width] = unturn(dk_ref[...], cos_ref[...], sin_ref[...])
        gp_ref[:, 2 * width :] = dv_ref[...].astype(BF)


def attend_backward(q, k, v, grad_out, lse, seg_col, valid_col, seg_row, cosine, sine, rows):
    length, width = q.shape
    whole = lambda a: pl.BlockSpec(a.shape, lambda i: (0, 0))
    tile = pl.BlockSpec((rows, width), lambda i: (i, 0))
    return pl.pallas_call(
        backward_kernel,
        grid=(length // rows,),
        in_specs=[
            tile, tile, pl.BlockSpec((8, rows), lambda i: (0, i)), whole(k), whole(v),
            whole(seg_col), whole(valid_col), pl.BlockSpec((1, rows), lambda i: (0, i)), whole(cosine), whole(sine),
        ],
        out_specs=pl.BlockSpec((length, 3 * width), lambda i: (0, 0)),
        out_shape=jax.ShapeDtypeStruct((length, 3 * width), BF),
        scratch_shapes=[
            pltpu.VMEM((width, length), BF), pltpu.VMEM((length, width), F32), pltpu.VMEM((length, width), F32),
            pltpu.VMEM((width, rows), F32), pltpu.VMEM((length, rows), F32),
        ],
        cost_estimate=pl.CostEstimate(
            flops=10 * length * length * width, bytes_accessed=20 * length * width, transcendentals=length * length * 4
        ),
        name="attend_back",
    )(q, grad_out, lse, k, v, seg_col, valid_col, seg_row, cosine, sine)


def erf(x):
    x = jnp.clip(x, -3.832506856900711, 3.832506856900711)
    square = x * x
    top = 0.00022905065861350646
    for c in (0.0034082910107109506, 0.050955695062380861, 0.18520832239976145, 1.128379143519084):
        top = top * square + c
    low = -1.1791602954361697e-7
    for c in (0.000023547966471313185, 0.0010179625278914885, 0.014070470171167667, 0.11098505178285362, 0.49746925110067538, 1.0):
        low = low * square + c
    return x * top / low


def nt(a, b):
    return lax.dot_general(a, b, (((1,), (1,)), ((), ())), preferred_element_type=F32)


def feed_kernel(b_ref, g_ref, w_ref, wd_ref, m_ref, gi_ref, gg_ref, gb_ref, mlp_ref):
    b = b_ref[...]
    hidden, slot = wd_ref.shape[0], w_ref.shape[1] // 2
    wi_ref, wg_ref = w_ref.at[:, :hidden], w_ref.at[:, slot : slot + hidden]
    inner = jnp.dot(b, wi_ref[...], preferred_element_type=F32)
    gate = jnp.dot(b, wg_ref[...], preferred_element_type=F32)
    upstream = nt(g_ref[...], wd_ref[...])
    half = 0.5 * (1.0 + erf(inner * 0.7071067811865476))
    gelu = inner * half
    slope = half + inner * jnp.exp(-0.5 * inner * inner) * 0.3989422804014327
    m = (gelu * gate).astype(BF)
    gi = (upstream * gate * slope).astype(BF)
    gg = (upstream * gelu).astype(BF)
    m_ref[...] = m
    gi_ref[...] = gi
    gg_ref[...] = gg
    gb_ref[...] = (nt(gi, wi_ref[...]) + nt(gg, wg_ref[...])).astype(gb_ref.dtype)
    mlp_ref[...] = jnp.dot(m, wd_ref[...], preferred_element_type=F32).astype(mlp_ref.dtype)


def feed_forward(b, g, w, wd, dtype):
    rows, width = b.shape
    hidden = wd.shape[0]
    narrow = jax.ShapeDtypeStruct((rows, hidden), BF)
    full = jax.ShapeDtypeStruct((rows, width), dtype)
    return pl.pallas_call(
        feed_kernel,
        out_shape=[narrow, narrow, narrow, full, full],
        cost_estimate=pl.CostEstimate(
            flops=12 * rows * width * hidden,
            bytes_accessed=6 * width * hidden + 8 * rows * width + 6 * rows * hidden,
            transcendentals=rows * hidden,
        ),
        name="feed",
    )(b, g, w, wd)


def tn(a, b):
    return lax.dot_general(a, b, (((0,), (0,)), ((), ())), preferred_element_type=F32)


def weight_kernel(count, slot, *refs):
    bs, gs, gis, ggs, ms = (refs[i * count : (i + 1) * count] for i in range(5))
    out_ref = refs[5 * count]
    hidden = gis[0].shape[1]
    for place, (lefts, rights) in enumerate(((bs, gis), (bs, ggs), (gs, ms))):
        total = tn(lefts[0][...], rights[0][...])
        for left, right in zip(lefts[1:], rights[1:]):
            total = total + tn(left[...], right[...])
        out_ref[:, place * slot : place * slot + hidden] = total.astype(BF)


def weight_gradients(bs, gs, gis, ggs, ms):
    count = len(bs)
    rows, width = bs[0].shape
    hidden = gis[0].shape[1]
    slot = -(-hidden // LANES) * LANES
    wide_spec = pl.BlockSpec((rows, 256), lambda i: (0, i))
    whole = pl.BlockSpec((rows, hidden), lambda i: (0, 0))
    return pl.pallas_call(
        functools.partial(weight_kernel, count, slot),
        grid=(width // 256,),
        in_specs=[wide_spec] * (2 * count) + [whole] * (3 * count),
        out_specs=pl.BlockSpec((256, 3 * slot), lambda i: (i, 0)),
        out_shape=jax.ShapeDtypeStruct((width, 3 * slot), BF),
        cost_estimate=pl.CostEstimate(
            flops=6 * rows * count * width * hidden,
            bytes_accessed=4 * rows * count * width + 6 * rows * count * hidden + 6 * width * hidden,
            transcendentals=0,
        ),
        name="weight_gradients",
    )(*bs, *gs, *gis, *ggs, *ms)


def last_kernel(me_ref, a_ref, gp_ref, mine_ref, away_ref):
    total = tn(a_ref[...], gp_ref[...])

    @pl.when(pl.program_id(0) % 2 == 0)
    def _():
        mine_ref[...] = total

    @pl.when(pl.program_id(0) % 2 == 1)
    def _():
        away_ref[...] = total.astype(BF)


def last_gradients(a, gp, me, size):
    length, width = a.shape
    rows, columns = width // size, gp.shape[1]
    out = lambda dtype: jax.ShapeDtypeStruct((width // 2, columns), dtype)
    return pl.pallas_call(
        last_kernel,
        grid_spec=pltpu.PrefetchScalarGridSpec(
            num_scalar_prefetch=1,
            grid=(size,),
            in_specs=[
                pl.BlockSpec((length, rows), lambda i, me: (0, me[0] ^ i)),
                pl.BlockSpec((length, columns), lambda i, me: (0, 0)),
            ],
            out_specs=[pl.BlockSpec((rows, columns), lambda i, me: (i // 2, 0))] * 2,
        ),
        out_shape=[out(F32), out(BF)],
        cost_estimate=pl.CostEstimate(
            flops=2 * length * width * columns,
            bytes_accessed=2 * length * (width + columns) + 3 * width * columns,
            transcendentals=0,
        ),
        name="last_gradients",
    )(me[None], a, gp)


def normal(values):
    centered = values - jnp.mean(values, axis=-1, keepdims=True)
    scale = lax.rsqrt(jnp.mean(centered * centered, axis=-1, keepdims=True) + NORM_EPS)
    return centered * scale, scale


def norm_back(upstream, gain, values):
    unit, scale = normal(values)
    weighted = upstream * gain
    return scale * (
        weighted
        - jnp.mean(weighted, axis=-1, keepdims=True)
        - unit * jnp.mean(weighted * unit, axis=-1, keepdims=True)
    )


def matmul(a, b):
    return jnp.dot(a, b, preferred_element_type=F32)


def matmul_nt(a, b):
    return lax.dot_general(a, b, (((1,), (1,)), ((), ())), preferred_element_type=F32)


def matmul_tn(a, b):
    return lax.dot_general(a, b, (((0,), (0,)), ((), ())), preferred_element_type=F32)


def on_device(
    hidden_in, segment_ids, valid_tokens, w_qkv, w_attn_out, w_in_proj, w_out_proj, attn_gain, mlp_gain, cotangent
):
    seq_size, fsdp_size = lax.axis_size("seq"), lax.axis_size("fsdp")
    seq, fsdp = lax.axis_index("seq"), lax.axis_index("fsdp")
    x_low, cot = hidden_in[0], cotangent[0]
    tokens = x_low.shape[0]
    length = tokens * seq_size
    part = D // seq_size
    hidden = FF // seq_size
    rel = [seq ^ k for k in range(seq_size)]

    first_mine = [lax.dynamic_slice_in_dim(w_qkv, i * D + seq * part, part, axis=1) for i in range(3)]
    first_mine.append(lax.dynamic_slice_in_dim(w_attn_out, seq * part, part, axis=1))
    first_mine = jnp.concatenate(first_mine, axis=1)
    first_weight = gather_rows(first_mine)
    x_blocks = share_seq(x_low)
    gains = gather_gains(jnp.stack([attn_gain, mlp_gain])).astype(F32)
    gain_one, gain_two = gains[0:1], gains[1:2]
    qkv_weight, out_mine = first_weight[:, : 3 * part], first_weight[:, 3 * part :]
    w_in_proj_late, w_out_proj_late, cot_late = after((w_in_proj, w_out_proj, cot), gains, *x_blocks)
    slot = -(-hidden // LANES) * LANES
    in_mine = [
        jnp.pad(
            lax.dynamic_slice_in_dim(w_in_proj_late, i * FF + seq * hidden, hidden, axis=1),
            ((0, 0), (0, slot - hidden)),
        )
        for i in range(2)
    ]
    in_weight = gather_rows(jnp.concatenate(in_mine, axis=1))
    if paired():
        down_mine = transpose_devices(lax.dynamic_slice_in_dim(w_out_proj_late, seq * part, part, axis=1))
        down_weight = gather_rows(down_mine).reshape(seq_size, 2, down_mine.shape[0], part)
        down_weight = down_weight.transpose(1, 2, 0, 3).reshape(hidden, D)
    else:
        down_weight = lax.all_gather(w_out_proj_late, "fsdp", axis=0, tiled=True)
        down_weight = lax.dynamic_slice_in_dim(down_weight, seq * hidden, hidden, axis=0)
    cot_blocks = [cot] + share_seq(cot_late)[1:]

    def in_order(blocks):
        bit = 1
        while bit < seq_size:
            flip = (seq & bit) != 0
            blocks = [jnp.where(flip, blocks[k ^ bit], blocks[k]) for k in range(seq_size)]
            bit *= 2
        return blocks

    out_weight = jnp.concatenate(in_order(share_seq(out_mine)), axis=1)

    def by_block(row):
        return jnp.concatenate([lax.dynamic_slice_in_dim(row, r * tokens, tokens) for r in rel])

    seg_all, valid_all = by_block(segment_ids[0]), by_block(valid_tokens[0])
    positions = by_block(jnp.arange(length, dtype=jnp.int32))
    frequency = ROPE_BASE ** (-2.0 * jnp.arange(HD // 2, dtype=F32) / HD)
    angles = positions.astype(F32)[:, None] * frequency[None, :]
    cosine, sine = lax.optimization_barrier((jnp.cos(angles), jnp.sin(angles)))
    cosine = jnp.concatenate([cosine] * 4, axis=1)
    sine = jnp.concatenate([-sine, sine] * 2, axis=1)
    seg_col, valid_col, seg_row = seg_all[:, None], valid_all[:, None], seg_all[None, :]

    a_low, q, k, v = project_qkv(x_blocks, qkv_weight, gain_one, cosine, sine)
    mixed, lse = attend_forward(q, k, v, seg_col, valid_col, seg_row, tokens)

    def to_tokens(blocks):
        came = [blocks[:tokens]] + [
            swap(blocks[i * tokens : (i + 1) * tokens], "seq", i) for i in range(1, seq_size)
        ]
        return jnp.concatenate(in_order(came), axis=1)

    mixed_low = to_tokens(mixed)
    x = x_low.astype(F32)
    attn_branch = matmul(mixed_low, out_weight)
    middle = x + attn_branch
    normed_two = (normal(middle)[0] * gain_two).astype(BF)

    b_blocks = share_seq(normed_two)
    fed = [
        feed_forward(b, g, in_weight, down_weight, F32 if i == 0 else BF)
        for i, (b, g) in enumerate(zip(b_blocks, cot_blocks))
    ]
    m_blocks, gz_i, gz_g, gb_blocks, mlp_blocks = zip(*fed)
    grad_normed_two = reduce_seq(gb_blocks)
    grad_middle = cot.astype(F32) + norm_back(grad_normed_two, gain_two, middle)
    grad_attn_low = grad_middle.astype(BF)
    grad_mixed = matmul_nt(grad_attn_low, out_weight).astype(BF)

    def to_heads(blocks):
        sent = [lax.dynamic_slice_in_dim(blocks, r * part, part, axis=1) for r in rel]
        return jnp.concatenate([sent[0]] + [swap(sent[i], "seq", i) for i in range(1, seq_size)], axis=0)

    grad_by_heads = to_heads(grad_mixed)

    mlp_branch = reduce_seq([mlp_blocks[0]] + [after(m, grad_by_heads) for m in mlp_blocks[1:]])
    result = middle + mlp_branch
    valid_mine = valid_all[:tokens].astype(F32)[:, None]
    stats = jnp.stack(
        [
            jnp.sum(valid_mine * result * result),
            jnp.sum(valid_mine * attn_branch * attn_branch),
            jnp.sum(valid_mine * mlp_branch * mlp_branch),
            jnp.sum(valid_mine),
        ]
    )
    stats = sum_everywhere(jnp.broadcast_to(stats[:, None], (4, 128)))[:, 0]
    root_means = jnp.sqrt(stats[:3] / (jnp.maximum(stats[3], 1.0) * D))

    def own_rows(partial):
        return lax.psum_scatter(partial, "fsdp", scatter_dimension=0, tiled=True)

    fed_grads = weight_gradients(b_blocks, cot_blocks, gz_i, gz_g, m_blocks)
    fed_rows = own_rows(fed_grads)
    out_part = matmul_tn(mixed_low, after(grad_attn_low, grad_by_heads)).astype(BF)
    out_quarter = reduce_seq(
        [lax.dynamic_slice_in_dim(out_part, r * part, part, axis=1) for r in rel]
    )
    out_rows = own_rows(after(out_quarter.astype(BF), fed_rows))

    gp = attend_backward(
        q, k, v, grad_by_heads, lse, seg_col, valid_col, seg_row, cosine, sine, tokens
    )
    if paired():
        mine, away = last_gradients(a_low, gp, fsdp, fsdp_size)
        last = reduce_rows(mine, away, fsdp_size)
    else:
        last = lax.psum_scatter(matmul_tn(a_low, gp), "fsdp", scatter_dimension=0, tiled=True)
    ga_parts = matmul_nt(gp, qkv_weight)

    fed = [fed_rows[:, i * slot : i * slot + hidden] for i in range(3)]
    if paired():
        every = lax.all_gather(jnp.stack([fed[0], fed[1], transpose_devices(fed[2])]), "seq", axis=0)
        half = hidden // 2
        core = fsdp % 2
        low, high = every[:, 2, :, :half], every[:, 2, :, half:]
        kept, came = jnp.where(core == 0, low, high), swap(jnp.where(core == 0, high, low), "fsdp", 1)
        even, odd = jnp.where(core == 0, kept, came), jnp.where(core == 0, came, kept)
        grad_down = jnp.concatenate([half_rows[i].T for i in range(seq_size) for half_rows in (even, odd)], axis=1)
        grad_down = grad_down.astype(F32)
    else:
        every = lax.all_gather(jnp.stack(fed[:2]), "seq", axis=0)
        down = lax.all_gather(fed[2], ("seq", "fsdp"), axis=0, tiled=True)
        down = down.reshape(seq_size, D, hidden).transpose(0, 2, 1).reshape(FF, D)
        mine = FF // fsdp_size
        grad_down = lax.dynamic_slice_in_dim(down, fsdp * mine, mine, axis=0).astype(F32)
    grad_in_weight = jnp.concatenate([every[j, i] for i in range(2) for j in range(seq_size)], axis=1).astype(F32)

    last = last.astype(BF)
    last = jnp.stack([last[:, i * part : (i + 1) * part] for i in range(3)] + [out_rows])
    last = in_order(share_seq(last))
    grad_qkv_weight = jnp.concatenate([p[i] for i in range(3) for p in last], axis=1).astype(F32)
    grad_out_weight = jnp.concatenate([p[3] for p in last], axis=1).astype(F32)

    grad_normed = reduce_seq([ga_parts[i * tokens : (i + 1) * tokens] for i in range(seq_size)])
    grad_inputs = grad_middle + norm_back(grad_normed, gain_one, x)

    def gain_gradient(weight, gradient, gain):
        return jnp.sum(weight.astype(F32) * gradient, axis=1) / gain.astype(F32)

    return (
        result.astype(BF)[None],
        grad_inputs[None],
        grad_qkv_weight,
        grad_out_weight,
        grad_in_weight,
        grad_down,
        gain_gradient(w_qkv, grad_qkv_weight, attn_gain),
        gain_gradient(w_in_proj, grad_in_weight, mlp_gain),
        root_means,
    )


def solution(mesh):
    in_specs = (
        P("fsdp", "seq", None),
        P("fsdp", None),
        P("fsdp", None),
        P("fsdp", None),
        P("fsdp", None),
        P("fsdp", None),
        P("fsdp", None),
        P("fsdp"),
        P("fsdp"),
        P("fsdp", "seq", None),
    )
    out_specs = (
        P("fsdp", "seq", None),
        P("fsdp", "seq", None),
        P("fsdp", None),
        P("fsdp", None),
        P("fsdp", None),
        P("fsdp", None),
        P("fsdp"),
        P("fsdp"),
        P(),
    )
    return jax.shard_map(on_device, mesh=mesh, in_specs=in_specs, out_specs=out_specs, check_vma=False)
```

```python
import functools

import jax
import jax.numpy as jnp
from jax import lax
from jax.experimental import pallas as pl
from jax.experimental.pallas import tpu as pltpu
from jax.sharding import PartitionSpec as P

D = 1024
HEADS = 16
HD = 64
FF = 2624

ROPE_BASE = 160000.0
NORM_EPS = 1e-05
LANES = 128
BF = jnp.bfloat16
F32 = jnp.float32


def swap(x, axis, bit):
    return lax.ppermute(x, axis, [(i, i ^ bit) for i in range(lax.axis_size(axis))])


def after(x, *others):
    return lax.optimization_barrier((x, others))[0]


def share_seq(block):
    return [block] + [swap(block, "seq", k) for k in range(1, lax.axis_size("seq"))]


def relay_first(block):
    return swap(block, "seq", 1), swap(block, "seq", 2)


def relay_last(block, one, two):
    if lax.axis_size("seq") != 4:
        return share_seq(block)
    half = block.shape[0] // 2
    upper, lower = swap(two[:half], "seq", 1), swap(one[half:], "seq", 2)
    return [block, one, two, jnp.concatenate([upper, lower], axis=0)]


def relay_seq(block):
    return relay_last(block, *relay_first(block))


def exchange_seq(blocks):
    return lax.all_to_all(blocks, "seq", split_axis=0, concat_axis=0, tiled=True)


def sum_blocks(blocks):
    rows = blocks.shape[0] // lax.axis_size("seq")
    total = blocks[:rows].astype(F32)
    for i in range(1, lax.axis_size("seq")):
        total = total + blocks[i * rows : (i + 1) * rows].astype(F32)
    return total


def paired():
    return lax.axis_size("fsdp") == 2 * lax.axis_size("seq")


def gather_rows(block):
    return lax.all_gather(block, "fsdp", axis=0, tiled=True)


def transpose_devices(x):
    seq, fsdp = lax.axis_size("seq"), lax.axis_size("fsdp")
    pairs = [
        (s * fsdp + 2 * z + c, z * fsdp + 2 * s + c)
        for s in range(seq)
        for z in range(fsdp // 2)
        for c in range(2)
    ]
    return lax.ppermute(x, ("seq", "fsdp"), pairs)


def sum_along(values, axis, bit=1):
    while bit < lax.axis_size(axis):
        values = values + swap(values, axis, bit)
        bit *= 2
    return values


def gather_gains(gains):
    size, rows = lax.axis_size("fsdp"), gains.shape[1]
    whole = jnp.zeros((2, size * rows), gains.dtype)
    whole = lax.dynamic_update_slice(whole, gains, (0, lax.axis_index("fsdp") * rows))
    bit = 1
    while bit < size:
        whole = whole + swap(whole, "fsdp", bit)
        bit *= 2
    return whole


def half_swap(values):
    width = values.shape[1]
    lane = lax.broadcasted_iota(jnp.int32, values.shape, 1)
    ahead = pltpu.roll(values, width - HD // 2, 1)
    behind = pltpu.roll(values, HD // 2, 1)
    return jnp.where(lane % HD < HD // 2, ahead, behind)


def wide(table, width):
    return jnp.concatenate([table] * (width // table.shape[1]), axis=1)


def qkv_kernel(*refs):
    count = 4
    xs = refs[:count]
    w_ref, gain_ref, cos_ref, sin_ref, a_ref, q_ref, k_ref, v_ref, held = refs[count:]
    step = pl.program_id(0)
    for i in range(count):

        @pl.when(step == i)
        def _():
            held[...] = xs[i][...].astype(F32)

    values = held[...]
    centered = values - jnp.mean(values, axis=1, keepdims=True)
    variance = jnp.mean(centered * centered, axis=1, keepdims=True)
    low = (centered * lax.rsqrt(variance + NORM_EPS) * gain_ref[...]).astype(BF)
    a_ref[...] = low
    p = jnp.dot(low, w_ref[...], preferred_element_type=F32)
    part = p.shape[1] // 3
    turned = p[:, : 2 * part]
    turned = turned * wide(cos_ref[...], 2 * part) + half_swap(turned) * wide(sin_ref[...], 2 * part)
    q_ref[...] = turned[:, :part].astype(BF) * (HD**-0.5)
    k_ref[...] = turned[:, part:].astype(BF)
    v_ref[...] = p[:, 2 * part :].astype(BF)


def project_qkv(blocks, weight, gain, cosine, sine):
    rows, width = blocks[0].shape
    part = weight.shape[1] // 3
    count = len(blocks)
    whole = lambda a: pl.BlockSpec(a.shape, lambda i: (0, 0))
    tile = lambda n: pl.BlockSpec((rows, n), lambda i: (i, 0))
    shape = lambda n: jax.ShapeDtypeStruct((rows * count, n), BF)
    return pl.pallas_call(
        qkv_kernel,
        grid=(count,),
        in_specs=[whole(b) for b in blocks]
        + [whole(weight), whole(gain), tile(cosine.shape[1]), tile(sine.shape[1])],
        out_specs=[tile(width), tile(part), tile(part), tile(part)],
        out_shape=[shape(width), shape(part), shape(part), shape(part)],
        scratch_shapes=[pltpu.VMEM((rows, width), F32)],
        cost_estimate=pl.CostEstimate(
            flops=2 * rows * count * width * 3 * part,
            bytes_accessed=2 * rows * count * (2 * width + 3 * part) + 2 * width * 3 * part,
            transcendentals=0,
        ),
        name="qkv",
    )(*blocks, weight, gain, cosine, sine)


def mask_bias(seg_col, valid_col, seg_row, first_row):
    shape = (seg_col.shape[0], seg_row.shape[1])
    key = lax.broadcasted_iota(jnp.int32, shape, 0)
    query = lax.broadcasted_iota(jnp.int32, shape, 1) + first_row
    allowed = (seg_col == seg_row) & ((valid_col > 0) | (key == query))
    return jnp.where(allowed, 0.0, -1e30)


def forward_kernel(q_ref, k_ref, v_ref, segc_ref, valc_ref, segr_ref, o_ref, lse_ref, vt_ref, ot_ref, bias_ref):
    step = pl.program_id(0)
    rows, width = q_ref.shape

    @pl.when(step == 0)
    def _():
        vt_ref[...] = v_ref[...].T

    bias_ref[...] = mask_bias(segc_ref[...], valc_ref[...], segr_ref[...], step * rows)
    qt = q_ref[...].T
    feature = lax.broadcasted_iota(jnp.int32, qt.shape, 0) // HD

    def head(h, carry):
        mine = jnp.where(feature == h, qt, jnp.zeros_like(qt))
        scores = jnp.dot(k_ref[...], mine, preferred_element_type=F32) + bias_ref[...]
        top = jnp.max(scores, axis=0, keepdims=True)
        exponent = jnp.exp(scores - top)
        total = jnp.sum(exponent, axis=0, keepdims=True)
        weights = (exponent * (1.0 / total)).astype(BF)
        start = pl.multiple_of(h * HD, HD)
        ot_ref[pl.ds(start, HD), :] = jnp.dot(
            vt_ref[pl.ds(start, HD), :], weights, preferred_element_type=F32
        )
        lse_ref[pl.ds(h, 1), :] = top + jnp.log(total)
        return carry

    lax.fori_loop(0, width // HD, head, 0)
    o_ref[...] = ot_ref[...].T.astype(BF)


def attend_forward(q, k, v, seg_col, valid_col, seg_row, rows):
    length, width = q.shape
    whole = lambda a: pl.BlockSpec(a.shape, lambda i: (0, 0))
    tile = pl.BlockSpec((rows, width), lambda i: (i, 0))
    return pl.pallas_call(
        forward_kernel,
        grid=(length // rows,),
        in_specs=[tile, whole(k), whole(v), whole(seg_col), whole(valid_col), pl.BlockSpec((1, rows), lambda i: (0, i))],
        out_specs=[tile, pl.BlockSpec((8, rows), lambda i: (0, i))],
        out_shape=[jax.ShapeDtypeStruct((length, width), BF), jax.ShapeDtypeStruct((8, length), F32)],
        scratch_shapes=[pltpu.VMEM((width, length), BF), pltpu.VMEM((width, rows), F32), pltpu.VMEM((length, rows), F32)],
        cost_estimate=pl.CostEstimate(
            flops=4 * length * length * width, bytes_accessed=8 * length * width, transcendentals=length * length * 4
        ),
        name="attend",
    )(q, k, v, seg_col, valid_col, seg_row)


def backward_kernel(
    q_ref, go_ref, lse_ref, k_ref, v_ref, segc_ref, valc_ref, segr_ref, cos_ref, sin_ref,
    gp_ref, kt_ref, dk_ref, dv_ref, dqt_ref, bias_ref,
):
    step = pl.program_id(0)
    rows, width = q_ref.shape

    @pl.when(step == 0)
    def _():
        kt_ref[...] = k_ref[...].T
        dk_ref[...] = jnp.zeros_like(dk_ref)
        dv_ref[...] = jnp.zeros_like(dv_ref)

    bias_ref[...] = mask_bias(segc_ref[...], valc_ref[...], segr_ref[...], step * rows)
    qt, got = q_ref[...].T, go_ref[...].T
    feature = lax.broadcasted_iota(jnp.int32, qt.shape, 0) // HD
    lane = lax.broadcasted_iota(jnp.int32, (rows, width), 1) // HD
    none = jnp.zeros_like(qt)
    none_row = jnp.zeros((rows, width), BF)

    def head(h, carry):
        scores = jnp.dot(k_ref[...], jnp.where(feature == h, qt, none), preferred_element_type=F32)
        weights = jnp.exp(scores + bias_ref[...] - lse_ref[pl.ds(h, 1), :])
        upstream = jnp.dot(v_ref[...], jnp.where(feature == h, got, none), preferred_element_type=F32)
        inner = jnp.sum(weights * upstream, axis=0, keepdims=True)
        low = (weights * (upstream - inner)).astype(BF)
        dv_ref[...] += jnp.dot(
            weights.astype(BF), jnp.where(lane == h, go_ref[...], none_row), preferred_element_type=F32
        )
        dk_ref[...] += jnp.dot(low, jnp.where(lane == h, q_ref[...], none_row), preferred_element_type=F32)
        start = pl.multiple_of(h * HD, HD)
        dqt_ref[pl.ds(start, HD), :] = jnp.dot(kt_ref[pl.ds(start, HD), :], low, preferred_element_type=F32)
        return carry

    lax.fori_loop(0, width // HD, head, 0)

    def unturn(values, cosine, sine):
        values = values.astype(BF).astype(F32)
        return (values * wide(cosine, width) - half_swap(values) * wide(sine, width)).astype(BF)

    here = pl.ds(pl.multiple_of(step * rows, rows), rows)
    gp_ref[here, :width] = unturn(dqt_ref[...].T * (HD**-0.5), cos_ref[here, :], sin_ref[here, :])

    @pl.when(step == pl.num_programs(0) - 1)
    def _():
        gp_ref[:, width : 2 * width] = unturn(dk_ref[...], cos_ref[...], sin_ref[...])
        gp_ref[:, 2 * width :] = dv_ref[...].astype(BF)


def attend_backward(q, k, v, grad_out, lse, seg_col, valid_col, seg_row, cosine, sine, rows):
    length, width = q.shape
    whole = lambda a: pl.BlockSpec(a.shape, lambda i: (0, 0))
    tile = pl.BlockSpec((rows, width), lambda i: (i, 0))
    return pl.pallas_call(
        backward_kernel,
        grid=(length // rows,),
        in_specs=[
            tile, tile, pl.BlockSpec((8, rows), lambda i: (0, i)), whole(k), whole(v),
            whole(seg_col), whole(valid_col), pl.BlockSpec((1, rows), lambda i: (0, i)), whole(cosine), whole(sine),
        ],
        out_specs=pl.BlockSpec((length, 3 * width), lambda i: (0, 0)),
        out_shape=jax.ShapeDtypeStruct((length, 3 * width), BF),
        scratch_shapes=[
            pltpu.VMEM((width, length), BF), pltpu.VMEM((length, width), F32), pltpu.VMEM((length, width), F32),
            pltpu.VMEM((width, rows), F32), pltpu.VMEM((length, rows), F32),
        ],
        cost_estimate=pl.CostEstimate(
            flops=10 * length * length * width, bytes_accessed=20 * length * width, transcendentals=length * length * 4
        ),
        name="attend_back",
    )(q, grad_out, lse, k, v, seg_col, valid_col, seg_row, cosine, sine)


def erf(x):
    x = jnp.clip(x, -3.832506856900711, 3.832506856900711)
    square = x * x
    top = 0.00022905065861350646
    for c in (0.0034082910107109506, 0.050955695062380861, 0.18520832239976145, 1.128379143519084):
        top = top * square + c
    low = -1.1791602954361697e-7
    for c in (0.000023547966471313185, 0.0010179625278914885, 0.014070470171167667, 0.11098505178285362, 0.49746925110067538, 1.0):
        low = low * square + c
    return x * top / low


def nt(a, b):
    return lax.dot_general(a, b, (((1,), (1,)), ((), ())), preferred_element_type=F32)


def feed_kernel(hidden, me_ref, b_ref, g_ref, w_ref, *refs):
    m_ref, gi_ref, gg_ref, gb_ref, mlp_ref = refs[-5:]
    b = b_ref[...]
    slot = w_ref.shape[1] // 3
    wi_ref, wg_ref, wd_ref = (w_ref.at[:, i * slot : i * slot + hidden] for i in range(3))
    inner = jnp.dot(b, wi_ref[...], preferred_element_type=F32)
    gate = jnp.dot(b, wg_ref[...], preferred_element_type=F32)
    upstream = jnp.dot(g_ref[...], wd_ref[...], preferred_element_type=F32)
    half = 0.5 * (1.0 + erf(inner * 0.7071067811865476))
    gelu = inner * half
    slope = half + inner * jnp.exp(-0.5 * inner * inner) * 0.3989422804014327
    m = (gelu * gate).astype(BF)
    gi = (upstream * gate * slope).astype(BF)
    gg = (upstream * gelu).astype(BF)
    m_ref[...] = m
    gi_ref[...] = gi
    gg_ref[...] = gg
    gb_ref[...] = (nt(gi, wi_ref[...]) + nt(gg, wg_ref[...])).astype(gb_ref.dtype)
    mlp_ref[...] = nt(m, wd_ref[...]).astype(mlp_ref.dtype)


def feed_forward(b, g, w, hidden, me, place, count, dtype, onto):
    rows, width = b.shape
    whole = lambda r, n: pl.BlockSpec((r, n), lambda i, me: (0, 0))
    narrow = jax.ShapeDtypeStruct((rows, hidden), BF)
    operands, specs = [b, g, w], [whole(rows, width), whole(rows, width), whole(*w.shape)]
    if onto is not None:
        operands.append(onto)
        specs.append(pl.BlockSpec(memory_space=pl.ANY))
    return pl.pallas_call(
        functools.partial(feed_kernel, hidden),
        grid_spec=pltpu.PrefetchScalarGridSpec(
            num_scalar_prefetch=1,
            grid=(1,),
            in_specs=specs,
            out_specs=[whole(rows, hidden)] * 3
            + [whole(rows, width), pl.BlockSpec((rows, width), lambda i, me: (me[0] ^ place, 0))],
        ),
        out_shape=[narrow] * 3
        + [jax.ShapeDtypeStruct((rows, width), dtype), jax.ShapeDtypeStruct((rows * count, width), BF)],
        input_output_aliases={} if onto is None else {4: 4},
        cost_estimate=pl.CostEstimate(
            flops=12 * rows * width * hidden,
            bytes_accessed=6 * width * hidden + 8 * rows * width + 6 * rows * hidden,
            transcendentals=rows * hidden,
        ),
        name="feed",
    )(me[None], *operands)


def tn(a, b):
    return lax.dot_general(a, b, (((0,), (0,)), ((), ())), preferred_element_type=F32)


def weight_kernel(count, slot, pairs, *refs):
    out_ref = refs[-1]
    hidden = refs[(pairs[0][1]) * count].shape[1]
    for place, (left, right) in enumerate(pairs):
        total = None
        for i in range(count):
            term = tn(refs[left * count + i][...], refs[right * count + i][...])
            total = term if total is None else total + term
        out_ref[:, place * slot : place * slot + hidden] = total.astype(BF)
        if hidden < slot:
            out_ref[:, place * slot + hidden : (place + 1) * slot] = jnp.zeros((out_ref.shape[0], slot - hidden), BF)


def weight_gradients(lefts, rights, pairs, slots, place, onto=None):
    count = len(lefts[0])
    rows, width = lefts[0][0].shape
    hidden = rights[0][0].shape[1]
    slot = -(-hidden // LANES) * LANES
    wide_spec = pl.BlockSpec((rows, 256), lambda i: (0, i))
    whole = pl.BlockSpec((rows, hidden), lambda i: (0, 0))
    operands = [b for group in lefts for b in group] + [b for group in rights for b in group]
    specs = [wide_spec] * (len(lefts) * count) + [whole] * (len(rights) * count)
    aliases = {}
    if onto is not None:
        aliases = {len(operands): 0}
        operands.append(onto)
        specs.append(pl.BlockSpec(memory_space=pl.ANY))
    return pl.pallas_call(
        functools.partial(weight_kernel, count, slot, pairs),
        grid=(width // 256,),
        in_specs=specs,
        out_specs=pl.BlockSpec((256, len(pairs) * slot), lambda i: (i, place // len(pairs))),
        out_shape=jax.ShapeDtypeStruct((width, slots * slot), BF),
        input_output_aliases=aliases,
        cost_estimate=pl.CostEstimate(
            flops=2 * len(pairs) * rows * count * width * hidden,
            bytes_accessed=2 * count * rows * (len(lefts) * width + len(rights) * hidden),
            transcendentals=0,
        ),
        name="weight_gradients",
    )(*operands)


def last_kernel(me_ref, a_ref, gp_ref, mine_ref, away_ref):
    total = tn(a_ref[...], gp_ref[...])

    @pl.when(pl.program_id(0) % 2 == 0)
    def _():
        mine_ref[...] = total

    @pl.when(pl.program_id(0) % 2 == 1)
    def _():
        away_ref[...] = total.astype(BF)


def last_gradients(a, gp, me, size):
    length, width = a.shape
    rows, columns = width // size, gp.shape[1]
    out = lambda dtype: jax.ShapeDtypeStruct((width // 2, columns), dtype)
    return pl.pallas_call(
        last_kernel,
        grid_spec=pltpu.PrefetchScalarGridSpec(
            num_scalar_prefetch=1,
            grid=(size,),
            in_specs=[
                pl.BlockSpec((length, rows), lambda i, me: (0, me[0] ^ i)),
                pl.BlockSpec((length, columns), lambda i, me: (0, 0)),
            ],
            out_specs=[pl.BlockSpec((rows, columns), lambda i, me: (i // 2, 0))] * 2,
        ),
        out_shape=[out(F32), out(BF)],
        cost_estimate=pl.CostEstimate(
            flops=2 * length * width * columns,
            bytes_accessed=2 * length * (width + columns) + 3 * width * columns,
            transcendentals=0,
        ),
        name="last_gradients",
    )(me[None], a, gp)


def qkv_back_kernel(me_ref, gp_ref, w_ref, out_ref):
    out_ref[...] = nt(gp_ref[...], w_ref[...]).astype(BF)


def project_back(gp, weight, me, count):
    rows, width = gp.shape[0] // count, weight.shape[0]
    return pl.pallas_call(
        qkv_back_kernel,
        grid_spec=pltpu.PrefetchScalarGridSpec(
            num_scalar_prefetch=1,
            grid=(count,),
            in_specs=[
                pl.BlockSpec((rows, gp.shape[1]), lambda i, me: (i, 0)),
                pl.BlockSpec(weight.shape, lambda i, me: (0, 0)),
            ],
            out_specs=pl.BlockSpec((rows, width), lambda i, me: (me[0] ^ i, 0)),
        ),
        out_shape=jax.ShapeDtypeStruct((rows * count, width), BF),
        cost_estimate=pl.CostEstimate(
            flops=2 * rows * count * width * gp.shape[1],
            bytes_accessed=2 * (rows * count * (width + gp.shape[1]) + width * gp.shape[1]),
            transcendentals=0,
        ),
        name="project_back",
    )(me[None], gp, weight)


def ordered(refs, me, piece):
    values = [ref[piece] for ref in refs]
    bit = 1
    while bit < len(values):
        flip = (me & bit) != 0
        values = [jnp.where(flip, values[k ^ bit], values[k]) for k in range(len(values))]
        bit *= 2
    return values


def gain_part(w_ref, grad_ref, gain_ref, out_ref):
    total = jnp.sum(w_ref[...].astype(F32) * grad_ref[...], axis=1, keepdims=True)
    out_ref[...] = total / gain_ref[...].astype(F32)


def last_rows_kernel(count, me_ref, *refs):
    blocks, (w_ref, gain_ref, qkv_ref, out_ref, gg_ref) = refs[:count], refs[count:]
    part = blocks[0].shape[1] // (3 + count)
    piece = lambda i: (slice(None), slice(i * part, (i + 1) * part))
    for i in range(3):
        for j, value in enumerate(ordered(blocks, me_ref[0], piece(i))):
            first = (i * count + j) * part
            qkv_ref[:, first : first + part] = value.astype(F32)
    for j in range(count):
        total = None
        for value in ordered(blocks, me_ref[0], piece(3 + j)):
            total = value.astype(F32) if total is None else total + value.astype(F32)
        out_ref[:, j * part : (j + 1) * part] = total
    gain_part(w_ref, qkv_ref, gain_ref, gg_ref)


def in_rows_kernel(count, hidden, me_ref, *refs):
    blocks, (w_ref, gain_ref, in_ref, gg_ref) = refs[:count], refs[count:]
    slot = blocks[0].shape[1] // 2
    for i in range(2):
        piece = (slice(None), slice(i * slot, i * slot + hidden))
        values = [value.astype(F32) for value in ordered(blocks, me_ref[0], piece)]
        in_ref[:, i * count * hidden : (i + 1) * count * hidden] = jnp.concatenate(values, axis=1)
    gain_part(w_ref, in_ref, gain_ref, gg_ref)


def finish_rows(kernel, blocks, weight, gain, me, widths, name):
    rows = weight.shape[0]
    shapes = [jax.ShapeDtypeStruct((rows, n), F32) for n in widths]
    return pl.pallas_call(
        kernel,
        in_specs=[pl.BlockSpec(memory_space=pltpu.SMEM)] + [pl.BlockSpec(memory_space=pltpu.VMEM)] * (len(blocks) + 2),
        out_shape=shapes,
        cost_estimate=pl.CostEstimate(flops=0, bytes_accessed=8 * rows * sum(widths), transcendentals=0),
        name=name,
    )(me[None], *blocks, weight, gain[:, None])


def normal(values):
    centered = values - jnp.mean(values, axis=-1, keepdims=True)
    scale = lax.rsqrt(jnp.mean(centered * centered, axis=-1, keepdims=True) + NORM_EPS)
    return centered * scale, scale


def norm_back(upstream, gain, values):
    unit, scale = normal(values)
    weighted = upstream * gain
    return scale * (
        weighted
        - jnp.mean(weighted, axis=-1, keepdims=True)
        - unit * jnp.mean(weighted * unit, axis=-1, keepdims=True)
    )


def matmul(a, b):
    return jnp.dot(a, b, preferred_element_type=F32)


def matmul_nt(a, b):
    return lax.dot_general(a, b, (((1,), (1,)), ((), ())), preferred_element_type=F32)


def matmul_tn(a, b):
    return lax.dot_general(a, b, (((0,), (0,)), ((), ())), preferred_element_type=F32)


def on_device(
    hidden_in, segment_ids, valid_tokens, w_qkv, w_attn_out, w_in_proj, w_out_proj, attn_gain, mlp_gain, cotangent
):
    seq_size, fsdp_size = lax.axis_size("seq"), lax.axis_size("fsdp")
    seq, fsdp = lax.axis_index("seq"), lax.axis_index("fsdp")
    x_low, cot = hidden_in[0], cotangent[0]
    tokens = x_low.shape[0]
    length = tokens * seq_size
    part = D // seq_size
    hidden = FF // seq_size
    rel = [seq ^ k for k in range(seq_size)]

    first_mine = [lax.dynamic_slice_in_dim(w_qkv, i * D + seq * part, part, axis=1) for i in range(3)]
    first_mine.append(lax.dynamic_slice_in_dim(w_attn_out, seq * part, part, axis=1))
    first_mine = jnp.concatenate(first_mine, axis=1)
    first_weight = gather_rows(first_mine)
    x_near = relay_first(x_low)
    x_blocks = relay_last(x_low, *x_near)
    gains = gather_gains(jnp.stack([attn_gain, mlp_gain])).astype(F32)
    gain_one, gain_two = gains[0:1], gains[1:2]
    qkv_weight, out_mine = first_weight[:, : 3 * part], first_weight[:, 3 * part :]
    core = fsdp % 2
    slot = -(-hidden // LANES) * LANES
    w_out_proj_late = after(w_out_proj, *x_near)
    w_in_proj_late, cot_late = after((w_in_proj, cot), gains, *x_blocks)

    def padded(rows):
        return jnp.pad(rows, ((0, 0), (0, slot - hidden)))

    def halves(rows):
        half = rows.shape[1] // 2
        low, high = rows[:, :half], rows[:, half:]
        return jnp.where(core == 0, low, high), jnp.where(core == 0, high, low)

    def by_core(mine, other):
        return jnp.where(core == 0, mine, other), jnp.where(core == 0, other, mine)

    in_mine = [
        padded(lax.dynamic_slice_in_dim(w_in_proj_late, i * FF + seq * hidden, hidden, axis=1)) for i in range(2)
    ]
    if paired():
        down_mine = transpose_devices(lax.dynamic_slice_in_dim(w_out_proj_late, seq * part, part, axis=1))
        kept, sent = halves(down_mine)
        down_mine = jnp.concatenate(by_core(kept, swap(sent, "fsdp", 1)), axis=0)
        feed_weight = gather_rows(jnp.concatenate(in_mine + [padded(down_mine.T)], axis=1))
    else:
        down_weight = lax.all_gather(w_out_proj_late, "fsdp", axis=0, tiled=True)
        down_weight = lax.dynamic_slice_in_dim(down_weight, seq * hidden, hidden, axis=0)
        feed_weight = jnp.concatenate([gather_rows(jnp.concatenate(in_mine, axis=1)), padded(down_weight.T)], axis=1)
    cot_blocks = [cot] + relay_seq(cot_late)[1:]

    def in_order(blocks):
        bit = 1
        while bit < seq_size:
            flip = (seq & bit) != 0
            blocks = [jnp.where(flip, blocks[k ^ bit], blocks[k]) for k in range(seq_size)]
            bit *= 2
        return blocks

    out_weight = jnp.concatenate(in_order(share_seq(out_mine)), axis=1)

    def by_block(row):
        return jnp.concatenate([lax.dynamic_slice_in_dim(row, r * tokens, tokens) for r in rel])

    seg_all, valid_all = by_block(segment_ids[0]), by_block(valid_tokens[0])
    positions = by_block(jnp.arange(length, dtype=jnp.int32))
    frequency = ROPE_BASE ** (-2.0 * jnp.arange(HD // 2, dtype=F32) / HD)
    angles = positions.astype(F32)[:, None] * frequency[None, :]
    cosine, sine = lax.optimization_barrier((jnp.cos(angles), jnp.sin(angles)))
    cosine = jnp.concatenate([cosine] * 4, axis=1)
    sine = jnp.concatenate([-sine, sine] * 2, axis=1)
    seg_col, valid_col, seg_row = seg_all[:, None], valid_all[:, None], seg_all[None, :]

    a_low, q, k, v = project_qkv(x_blocks, qkv_weight, gain_one, cosine, sine)
    mixed, lse = attend_forward(q, k, v, seg_col, valid_col, seg_row, tokens)

    def to_tokens(blocks):
        came = [blocks[:tokens]] + [
            swap(blocks[i * tokens : (i + 1) * tokens], "seq", i) for i in range(1, seq_size)
        ]
        return jnp.concatenate(in_order(came), axis=1)

    mixed_low = to_tokens(mixed)
    x = x_low.astype(F32)
    attn_branch = matmul(mixed_low, out_weight)
    middle = x + attn_branch
    normed_two = (normal(middle)[0] * gain_two).astype(BF)
    normed_two = after(normed_two, *cot_blocks)

    b_blocks = share_seq(normed_two)
    fed, came, mlp_all = [None] * seq_size, [], None
    for i in [*range(1, seq_size), 0]:
        b = after(b_blocks[i], *came[:-2]) if len(came) > 2 else b_blocks[i]
        fed[i] = feed_forward(
            b, cot_blocks[i], feed_weight, hidden, seq, i, seq_size, F32 if i == 0 else BF, mlp_all
        )
        mlp_all = fed[i][4]
        if i > 0:
            came.append(swap(fed[i][3], "seq", i))
    m_blocks, gz_i, gz_g, gb_blocks, _ = zip(*fed)
    fed_grads = weight_gradients([after(b_blocks, *came[:-1])], [gz_i, gz_g], ((0, 1), (0, 2)), 3, 0)
    fed_grads = weight_gradients([after(cot_blocks, *came)], [m_blocks], ((0, 1),), 3, 2, fed_grads)
    grad_normed_two = gb_blocks[0]
    for block in came:
        grad_normed_two = grad_normed_two + block.astype(F32)
    grad_middle = cot.astype(F32) + norm_back(grad_normed_two, gain_two, middle)
    grad_attn_low = grad_middle.astype(BF)
    grad_mixed = matmul_nt(grad_attn_low, out_weight).astype(BF)

    sent = [lax.dynamic_slice_in_dim(grad_mixed, r * part, part, axis=1) for r in rel]
    came = [sent[0]] + [swap(sent[i], "seq", i) for i in range(1, seq_size)]
    out_part = matmul_tn(mixed_low, after(grad_attn_low, came[-1])).astype(BF)
    grad_by_heads = after(jnp.concatenate(came, axis=0), out_part, fed_grads)
    mlp_came = exchange_seq(after(mlp_all, grad_by_heads))

    def own_rows(partial):
        return lax.psum_scatter(partial, "fsdp", scatter_dimension=0, tiled=True)

    fed_rows = own_rows(fed_grads)
    out_rows = own_rows(out_part)

    gp = attend_backward(
        q, k, v, grad_by_heads, lse, seg_col, valid_col, seg_row, cosine, sine, tokens
    )
    fed_late = after(fed_rows, gp)
    in_rows, down_rows = fed_late[:, : 2 * slot], fed_late[:, 2 * slot : 2 * slot + hidden]
    in_all = share_seq(in_rows)
    mlp_branch = sum_blocks(after(mlp_came, gp))
    result = middle + mlp_branch
    valid_mine = valid_all[:tokens].astype(F32)[:, None]
    stats = jnp.stack(
        [
            jnp.sum(valid_mine * result * result),
            jnp.sum(valid_mine * attn_branch * attn_branch),
            jnp.sum(valid_mine * mlp_branch * mlp_branch),
            jnp.sum(valid_mine),
        ]
    )
    stats = sum_along(jnp.broadcast_to(stats[:, None], (4, 128)), "seq")
    if paired():
        down_rows = transpose_devices(down_rows)
        mine, away = last_gradients(a_low, after(gp, fed_rows), fsdp, fsdp_size)
        ga_parts = project_back(after(gp, away), qkv_weight, seq, seq_size)
        mine = mine + after(swap(away, "fsdp", 1), ga_parts, down_rows, stats, *in_all[1:3]).astype(F32)
        down_rows = after(down_rows, mine)
        kept, sent = halves(down_rows)
        down_rows = jnp.concatenate(by_core(kept, swap(sent, "fsdp", 1)), axis=0).T
        rows = mine.shape[0] // (fsdp_size // 2)
        came = [swap(mine[k * rows : (k + 1) * rows].astype(BF), "fsdp", 2 * k) for k in range(1, fsdp_size // 2)]
        came = after(came, down_rows, out_rows, *in_all)
        last = mine[:rows]
        for block in came:
            last = last + block.astype(F32)
    else:
        mine, ga_parts = matmul_tn(a_low, gp), project_back(gp, qkv_weight, seq, seq_size)
        last = lax.psum_scatter(mine, "fsdp", scatter_dimension=0, tiled=True)
    ga_came = exchange_seq(ga_parts)
    stats = sum_along(stats, "fsdp")[:, 0]
    root_means = jnp.sqrt(stats[:3] / (jnp.maximum(stats[3], 1.0) * D))
    last = jnp.concatenate([last.astype(BF), out_rows], axis=1)
    ga_came, in_all = after((ga_came, in_all), last)

    grad_in_weight, grad_gain_two = finish_rows(
        functools.partial(in_rows_kernel, seq_size, hidden), in_all, w_in_proj, mlp_gain, seq, (2 * FF, 1), "in_rows"
    )
    if paired():
        grad_down = jnp.concatenate(in_order(share_seq(down_rows)), axis=1).astype(F32)
    else:
        down = lax.all_gather(down_rows, ("seq", "fsdp"), axis=0, tiled=True)
        down = down.reshape(seq_size, D, hidden).transpose(0, 2, 1).reshape(FF, D)
        rows = FF // fsdp_size
        grad_down = lax.dynamic_slice_in_dim(down, fsdp * rows, rows, axis=0).astype(F32)

    grad_normed = sum_blocks(ga_came)
    grad_inputs = grad_middle + norm_back(grad_normed, gain_one, x)
    last = after(share_seq(last), grad_in_weight, grad_down, grad_inputs)
    grad_qkv_weight, grad_out_weight, grad_gain_one = finish_rows(
        functools.partial(last_rows_kernel, seq_size), last, w_qkv, attn_gain, seq, (3 * D, D, 1), "last_rows"
    )

    return (
        result.astype(BF)[None],
        grad_inputs[None],
        grad_qkv_weight,
        grad_out_weight,
        grad_in_weight,
        grad_down,
        grad_gain_one[:, 0],
        grad_gain_two[:, 0],
        root_means,
    )


def solution(mesh):
    in_specs = (
        P("fsdp", "seq", None),
        P("fsdp", None),
        P("fsdp", None),
        P("fsdp", None),
        P("fsdp", None),
        P("fsdp", None),
        P("fsdp", None),
        P("fsdp"),
        P("fsdp"),
        P("fsdp", "seq", None),
    )
    out_specs = (
        P("fsdp", "seq", None),
        P("fsdp", "seq", None),
        P("fsdp", None),
        P("fsdp", None),
        P("fsdp", None),
        P("fsdp", None),
        P("fsdp"),
        P("fsdp"),
        P(),
    )
    return jax.shard_map(on_device, mesh=mesh, in_specs=in_specs, out_specs=out_specs, check_vma=False)
```

```python
import functools

import jax
import jax.numpy as jnp
from jax import lax
from jax.experimental import pallas as pl
from jax.experimental.pallas import tpu as pltpu
from jax.sharding import PartitionSpec as P

D = 1024
HEADS = 16
HD = 64
FF = 2624

ROPE_BASE = 160000.0
NORM_EPS = 1e-05
LANES = 128
BF = jnp.bfloat16
F32 = jnp.float32


def swap(x, axis, bit):
    return lax.ppermute(x, axis, [(i, i ^ bit) for i in range(lax.axis_size(axis))])


def after(x, *others):
    return lax.optimization_barrier((x, others))[0]


def share_seq(block):
    return [block] + [swap(block, "seq", k) for k in range(1, lax.axis_size("seq"))]


def relay_first(block):
    return swap(block, "seq", 1), swap(block, "seq", 2)


def relay_last(block, one, two):
    if lax.axis_size("seq") != 4:
        return share_seq(block)
    half = block.shape[0] // 2
    upper, lower = swap(two[:half], "seq", 1), swap(one[half:], "seq", 2)
    return [block, one, two, jnp.concatenate([upper, lower], axis=0)]


def exchange_seq(blocks):
    return lax.all_to_all(blocks, "seq", split_axis=0, concat_axis=0, tiled=True)


def sum_blocks(blocks):
    rows = blocks.shape[0] // lax.axis_size("seq")
    total = blocks[:rows].astype(F32)
    for i in range(1, lax.axis_size("seq")):
        total = total + blocks[i * rows : (i + 1) * rows].astype(F32)
    return total


def paired():
    return lax.axis_size("fsdp") == 2 * lax.axis_size("seq")


def gather_rows(block):
    return lax.all_gather(block, "fsdp", axis=0, tiled=True)


def transpose_devices(x):
    seq, fsdp = lax.axis_size("seq"), lax.axis_size("fsdp")
    pairs = [
        (s * fsdp + 2 * z + c, z * fsdp + 2 * s + c)
        for s in range(seq)
        for z in range(fsdp // 2)
        for c in range(2)
    ]
    return lax.ppermute(x, ("seq", "fsdp"), pairs)


def sum_over(values, axis, bits):
    values = [values] + [swap(values, axis, bit) for bit in bits]
    while len(values) > 1:
        values = [values[i] + values[i + 1] for i in range(0, len(values), 2)]
    return values[0]


def half_swap(values):
    width = values.shape[1]
    lane = lax.broadcasted_iota(jnp.int32, values.shape, 1)
    ahead = pltpu.roll(values, width - HD // 2, 1)
    behind = pltpu.roll(values, HD // 2, 1)
    return jnp.where(lane % HD < HD // 2, ahead, behind)


def wide(table, width):
    return jnp.concatenate([table] * (width // table.shape[1]), axis=1)


def qkv_kernel(*refs):
    count = 4
    xs = refs[:count]
    w_ref, gain_ref, cos_ref, sin_ref, a_ref, q_ref, k_ref, v_ref, held = refs[count:]
    step = pl.program_id(0)
    for i in range(count):

        @pl.when(step == i)
        def _():
            held[...] = xs[i][...].astype(F32)

    values = held[...]
    centered = values - jnp.mean(values, axis=1, keepdims=True)
    variance = jnp.mean(centered * centered, axis=1, keepdims=True)
    low = (centered * lax.rsqrt(variance + NORM_EPS) * gain_ref[...]).astype(BF)
    a_ref[...] = low
    p = jnp.dot(low, w_ref[...], preferred_element_type=F32)
    part = p.shape[1] // 3
    turned = p[:, : 2 * part]
    turned = turned * wide(cos_ref[...], 2 * part) + half_swap(turned) * wide(sin_ref[...], 2 * part)
    q_ref[...] = turned[:, :part].astype(BF) * (HD**-0.5)
    k_ref[...] = turned[:, part:].astype(BF)
    v_ref[...] = p[:, 2 * part :].astype(BF)


def project_qkv(blocks, weight, gain, cosine, sine):
    rows, width = blocks[0].shape
    part = (weight.shape[1] - LANES) // 4
    count = len(blocks)
    whole = lambda a: pl.BlockSpec(a.shape, lambda i: (0, 0))
    tile = lambda n: pl.BlockSpec((rows, n), lambda i: (i, 0))
    shape = lambda n: jax.ShapeDtypeStruct((rows * count, n), BF)
    return pl.pallas_call(
        qkv_kernel,
        grid=(count,),
        in_specs=[whole(b) for b in blocks]
        + [pl.BlockSpec((width, 3 * part), lambda i: (0, 0)), whole(gain), tile(cosine.shape[1]), tile(sine.shape[1])],
        out_specs=[tile(width), tile(part), tile(part), tile(part)],
        out_shape=[shape(width), shape(part), shape(part), shape(part)],
        scratch_shapes=[pltpu.VMEM((rows, width), F32)],
        cost_estimate=pl.CostEstimate(
            flops=2 * rows * count * width * 3 * part,
            bytes_accessed=2 * rows * count * (2 * width + 3 * part) + 2 * width * 3 * part,
            transcendentals=0,
        ),
        name="qkv",
    )(*blocks, weight, gain, cosine, sine)


def mask_bias(seg_col, valid_col, seg_row, first_row):
    shape = (seg_col.shape[0], seg_row.shape[1])
    key = lax.broadcasted_iota(jnp.int32, shape, 0)
    query = lax.broadcasted_iota(jnp.int32, shape, 1) + first_row
    allowed = (seg_col == seg_row) & ((valid_col > 0) | (key == query))
    return jnp.where(allowed, 0.0, -1e30)


def forward_kernel(q_ref, k_ref, v_ref, segc_ref, valc_ref, segr_ref, o_ref, lse_ref, vt_ref, ot_ref, bias_ref):
    step = pl.program_id(0)
    rows, width = q_ref.shape

    @pl.when(step == 0)
    def _():
        vt_ref[...] = v_ref[...].T

    bias_ref[...] = mask_bias(segc_ref[...], valc_ref[...], segr_ref[...], step * rows)
    qt = q_ref[...].T
    feature = lax.broadcasted_iota(jnp.int32, qt.shape, 0) // HD

    def head(h, carry):
        mine = jnp.where(feature == h, qt, jnp.zeros_like(qt))
        scores = jnp.dot(k_ref[...], mine, preferred_element_type=F32) + bias_ref[...]
        top = jnp.max(scores, axis=0, keepdims=True)
        exponent = jnp.exp(scores - top)
        total = jnp.sum(exponent, axis=0, keepdims=True)
        weights = (exponent * (1.0 / total)).astype(BF)
        start = pl.multiple_of(h * HD, HD)
        ot_ref[pl.ds(start, HD), :] = jnp.dot(
            vt_ref[pl.ds(start, HD), :], weights, preferred_element_type=F32
        )
        lse_ref[pl.ds(h, 1), :] = top + jnp.log(total)
        return carry

    lax.fori_loop(0, width // HD, head, 0)
    o_ref[...] = ot_ref[...].T.astype(BF)


def attend_forward(q, k, v, seg_col, valid_col, seg_row, rows):
    length, width = q.shape
    whole = lambda a: pl.BlockSpec(a.shape, lambda i: (0, 0))
    tile = pl.BlockSpec((rows, width), lambda i: (i, 0))
    return pl.pallas_call(
        forward_kernel,
        grid=(length // rows,),
        in_specs=[tile, whole(k), whole(v), whole(seg_col), whole(valid_col), pl.BlockSpec((1, rows), lambda i: (0, i))],
        out_specs=[tile, pl.BlockSpec((8, rows), lambda i: (0, i))],
        out_shape=[jax.ShapeDtypeStruct((length, width), BF), jax.ShapeDtypeStruct((8, length), F32)],
        scratch_shapes=[pltpu.VMEM((width, length), BF), pltpu.VMEM((width, rows), F32), pltpu.VMEM((length, rows), F32)],
        cost_estimate=pl.CostEstimate(
            flops=4 * length * length * width, bytes_accessed=8 * length * width, transcendentals=length * length * 4
        ),
        name="attend",
    )(q, k, v, seg_col, valid_col, seg_row)


def backward_kernel(
    q_ref, go_ref, lse_ref, k_ref, v_ref, segc_ref, valc_ref, segr_ref, cos_ref, sin_ref,
    gp_ref, kt_ref, dk_ref, dv_ref, dqt_ref, bias_ref,
):
    step = pl.program_id(0)
    rows, width = q_ref.shape

    @pl.when(step == 0)
    def _():
        kt_ref[...] = k_ref[...].T
        dk_ref[...] = jnp.zeros_like(dk_ref)
        dv_ref[...] = jnp.zeros_like(dv_ref)

    bias_ref[...] = mask_bias(segc_ref[...], valc_ref[...], segr_ref[...], step * rows)
    qt, got = q_ref[...].T, go_ref[...].T
    feature = lax.broadcasted_iota(jnp.int32, qt.shape, 0) // HD
    lane = lax.broadcasted_iota(jnp.int32, (rows, width), 1) // HD
    none = jnp.zeros_like(qt)
    none_row = jnp.zeros((rows, width), BF)

    def head(h, carry):
        scores = jnp.dot(k_ref[...], jnp.where(feature == h, qt, none), preferred_element_type=F32)
        weights = jnp.exp(scores + bias_ref[...] - lse_ref[pl.ds(h, 1), :])
        upstream = jnp.dot(v_ref[...], jnp.where(feature == h, got, none), preferred_element_type=F32)
        inner = jnp.sum(weights * upstream, axis=0, keepdims=True)
        low = (weights * (upstream - inner)).astype(BF)
        dv_ref[...] += jnp.dot(
            weights.astype(BF), jnp.where(lane == h, go_ref[...], none_row), preferred_element_type=F32
        )
        dk_ref[...] += jnp.dot(low, jnp.where(lane == h, q_ref[...], none_row), preferred_element_type=F32)
        start = pl.multiple_of(h * HD, HD)
        dqt_ref[pl.ds(start, HD), :] = jnp.dot(kt_ref[pl.ds(start, HD), :], low, preferred_element_type=F32)
        return carry

    lax.fori_loop(0, width // HD, head, 0)

    def unturn(values, cosine, sine):
        values = values.astype(BF).astype(F32)
        return (values * wide(cosine, width) - half_swap(values) * wide(sine, width)).astype(BF)

    here = pl.ds(pl.multiple_of(step * rows, rows), rows)
    gp_ref[here, :width] = unturn(dqt_ref[...].T * (HD**-0.5), cos_ref[here, :], sin_ref[here, :])

    @pl.when(step == pl.num_programs(0) - 1)
    def _():
        gp_ref[:, width : 2 * width] = unturn(dk_ref[...], cos_ref[...], sin_ref[...])
        gp_ref[:, 2 * width :] = dv_ref[...].astype(BF)


def attend_backward(q, k, v, grad_out, lse, seg_col, valid_col, seg_row, cosine, sine, rows):
    length, width = q.shape
    whole = lambda a: pl.BlockSpec(a.shape, lambda i: (0, 0))
    tile = pl.BlockSpec((rows, width), lambda i: (i, 0))
    return pl.pallas_call(
        backward_kernel,
        grid=(length // rows,),
        in_specs=[
            tile, tile, pl.BlockSpec((8, rows), lambda i: (0, i)), whole(k), whole(v),
            whole(seg_col), whole(valid_col), pl.BlockSpec((1, rows), lambda i: (0, i)), whole(cosine), whole(sine),
        ],
        out_specs=pl.BlockSpec((length, 3 * width), lambda i: (0, 0)),
        out_shape=jax.ShapeDtypeStruct((length, 3 * width), BF),
        scratch_shapes=[
            pltpu.VMEM((width, length), BF), pltpu.VMEM((length, width), F32), pltpu.VMEM((length, width), F32),
            pltpu.VMEM((width, rows), F32), pltpu.VMEM((length, rows), F32),
        ],
        cost_estimate=pl.CostEstimate(
            flops=10 * length * length * width, bytes_accessed=20 * length * width, transcendentals=length * length * 4
        ),
        name="attend_back",
    )(q, grad_out, lse, k, v, seg_col, valid_col, seg_row, cosine, sine)


def erf(x):
    x = jnp.clip(x, -3.832506856900711, 3.832506856900711)
    square = x * x
    top = 0.00022905065861350646
    for c in (0.0034082910107109506, 0.050955695062380861, 0.18520832239976145, 1.128379143519084):
        top = top * square + c
    low = -1.1791602954361697e-7
    for c in (0.000023547966471313185, 0.0010179625278914885, 0.014070470171167667, 0.11098505178285362, 0.49746925110067538, 1.0):
        low = low * square + c
    return x * top / low


def nt(a, b):
    return lax.dot_general(a, b, (((1,), (1,)), ((), ())), preferred_element_type=F32)


def feed_kernel(hidden, me_ref, b_ref, g_ref, w_ref, *refs):
    m_ref, gi_ref, gg_ref, gb_ref, mlp_ref = refs[-5:]
    b = b_ref[...]
    slot = w_ref.shape[1] // 3
    wi_ref, wg_ref, wd_ref = (w_ref.at[:, i * slot : i * slot + hidden] for i in range(3))
    inner = jnp.dot(b, wi_ref[...], preferred_element_type=F32)
    gate = jnp.dot(b, wg_ref[...], preferred_element_type=F32)
    upstream = jnp.dot(g_ref[...], wd_ref[...], preferred_element_type=F32)
    half = 0.5 * (1.0 + erf(inner * 0.7071067811865476))
    gelu = inner * half
    slope = half + inner * jnp.exp(-0.5 * inner * inner) * 0.3989422804014327
    m = (gelu * gate).astype(BF)
    gi = (upstream * gate * slope).astype(BF)
    gg = (upstream * gelu).astype(BF)
    m_ref[...] = m
    gi_ref[...] = gi
    gg_ref[...] = gg
    gb_ref[...] = (nt(gi, wi_ref[...]) + nt(gg, wg_ref[...])).astype(gb_ref.dtype)
    mlp_ref[...] = nt(m, wd_ref[...]).astype(mlp_ref.dtype)


def feed_forward(b, g, w, hidden, me, place, count, dtype, onto):
    rows, width = b.shape
    whole = lambda r, n: pl.BlockSpec((r, n), lambda i, me: (0, 0))
    narrow = jax.ShapeDtypeStruct((rows, hidden), BF)
    operands, specs = [b, g, w], [whole(rows, width), whole(rows, width), whole(*w.shape)]
    if onto is not None:
        operands.append(onto)
        specs.append(pl.BlockSpec(memory_space=pl.ANY))
    return pl.pallas_call(
        functools.partial(feed_kernel, hidden),
        grid_spec=pltpu.PrefetchScalarGridSpec(
            num_scalar_prefetch=1,
            grid=(1,),
            in_specs=specs,
            out_specs=[whole(rows, hidden)] * 3
            + [whole(rows, width), pl.BlockSpec((rows, width), lambda i, me: (me[0] ^ place, 0))],
        ),
        out_shape=[narrow] * 3
        + [jax.ShapeDtypeStruct((rows, width), dtype), jax.ShapeDtypeStruct((rows * count, width), BF)],
        input_output_aliases={} if onto is None else {4: 4},
        cost_estimate=pl.CostEstimate(
            flops=12 * rows * width * hidden,
            bytes_accessed=6 * width * hidden + 8 * rows * width + 6 * rows * hidden,
            transcendentals=rows * hidden,
        ),
        name="feed",
    )(me[None], *operands)


def tn(a, b):
    return lax.dot_general(a, b, (((0,), (0,)), ((), ())), preferred_element_type=F32)


def weight_kernel(count, slot, pairs, *refs):
    out_ref = refs[-1]
    hidden = refs[(pairs[0][1]) * count].shape[1]
    for place, (left, right) in enumerate(pairs):
        total = None
        for i in range(count):
            term = tn(refs[left * count + i][...], refs[right * count + i][...])
            total = term if total is None else total + term
        out_ref[:, place * slot : place * slot + hidden] = total.astype(BF)
        if hidden < slot:
            out_ref[:, place * slot + hidden : (place + 1) * slot] = jnp.zeros((out_ref.shape[0], slot - hidden), BF)


def weight_gradients(lefts, rights, pairs, slots, place, onto=None):
    count = len(lefts[0])
    rows, width = lefts[0][0].shape
    hidden = rights[0][0].shape[1]
    slot = -(-hidden // LANES) * LANES
    wide_spec = pl.BlockSpec((rows, 256), lambda i: (0, i))
    whole = pl.BlockSpec((rows, hidden), lambda i: (0, 0))
    operands = [b for group in lefts for b in group] + [b for group in rights for b in group]
    specs = [wide_spec] * (len(lefts) * count) + [whole] * (len(rights) * count)
    aliases = {}
    if onto is not None:
        aliases = {len(operands): 0}
        operands.append(onto)
        specs.append(pl.BlockSpec(memory_space=pl.ANY))
    return pl.pallas_call(
        functools.partial(weight_kernel, count, slot, pairs),
        grid=(width // 256,),
        in_specs=specs,
        out_specs=pl.BlockSpec((256, len(pairs) * slot), lambda i: (i, place // len(pairs))),
        out_shape=jax.ShapeDtypeStruct((width, slots * slot), BF),
        input_output_aliases=aliases,
        cost_estimate=pl.CostEstimate(
            flops=2 * len(pairs) * rows * count * width * hidden,
            bytes_accessed=2 * count * rows * (len(lefts) * width + len(rights) * hidden),
            transcendentals=0,
        ),
        name="weight_gradients",
    )(*operands)


def last_kernel(me_ref, a_ref, gp_ref, mine_ref, away_ref):
    total = tn(a_ref[...], gp_ref[...])

    @pl.when(pl.program_id(0) % 2 == 0)
    def _():
        mine_ref[...] = total

    @pl.when(pl.program_id(0) % 2 == 1)
    def _():
        away_ref[...] = total.astype(BF)


def last_gradients(a, gp, me, size):
    length, width = a.shape
    rows, columns = width // size, gp.shape[1]
    out = lambda dtype: jax.ShapeDtypeStruct((width // 2, columns), dtype)
    return pl.pallas_call(
        last_kernel,
        grid_spec=pltpu.PrefetchScalarGridSpec(
            num_scalar_prefetch=1,
            grid=(size,),
            in_specs=[
                pl.BlockSpec((length, rows), lambda i, me: (0, me[0] ^ i)),
                pl.BlockSpec((length, columns), lambda i, me: (0, 0)),
            ],
            out_specs=[pl.BlockSpec((rows, columns), lambda i, me: (i // 2, 0))] * 2,
        ),
        out_shape=[out(F32), out(BF)],
        cost_estimate=pl.CostEstimate(
            flops=2 * length * width * columns,
            bytes_accessed=2 * length * (width + columns) + 3 * width * columns,
            transcendentals=0,
        ),
        name="last_gradients",
    )(me[None], a, gp)


def qkv_back_kernel(me_ref, gp_ref, w_ref, out_ref):
    out_ref[...] = nt(gp_ref[...], w_ref[...]).astype(BF)


def project_back(gp, weight, me, count):
    rows, width = gp.shape[0] // count, weight.shape[0]
    return pl.pallas_call(
        qkv_back_kernel,
        grid_spec=pltpu.PrefetchScalarGridSpec(
            num_scalar_prefetch=1,
            grid=(count,),
            in_specs=[
                pl.BlockSpec((rows, gp.shape[1]), lambda i, me: (i, 0)),
                pl.BlockSpec((width, gp.shape[1]), lambda i, me: (0, 0)),
            ],
            out_specs=pl.BlockSpec((rows, width), lambda i, me: (me[0] ^ i, 0)),
        ),
        out_shape=jax.ShapeDtypeStruct((rows * count, width), BF),
        cost_estimate=pl.CostEstimate(
            flops=2 * rows * count * width * gp.shape[1],
            bytes_accessed=2 * (rows * count * (width + gp.shape[1]) + width * gp.shape[1]),
            transcendentals=0,
        ),
        name="project_back",
    )(me[None], gp, weight)


def ordered(refs, me, piece):
    values = [ref[piece] for ref in refs]
    bit = 1
    while bit < len(values):
        flip = (me & bit) != 0
        values = [jnp.where(flip, values[k ^ bit], values[k]) for k in range(len(values))]
        bit *= 2
    return values


def gain_part(w_ref, grad_ref, gain_ref, out_ref):
    total = jnp.sum(w_ref[...].astype(F32) * grad_ref[...], axis=1, keepdims=True)
    out_ref[...] = total / gain_ref[...].astype(F32)


def last_rows_kernel(count, me_ref, *refs):
    blocks, (w_ref, gain_ref, qkv_ref, out_ref, gg_ref) = refs[:count], refs[count:]
    part = blocks[0].shape[1] // (3 + count)
    piece = lambda i: (slice(None), slice(i * part, (i + 1) * part))
    for i in range(3):
        for j, value in enumerate(ordered(blocks, me_ref[0], piece(i))):
            first = (i * count + j) * part
            qkv_ref[:, first : first + part] = value.astype(F32)
    for j in range(count):
        total = None
        for value in ordered(blocks, me_ref[0], piece(3 + j)):
            total = value.astype(F32) if total is None else total + value.astype(F32)
        out_ref[:, j * part : (j + 1) * part] = total
    gain_part(w_ref, qkv_ref, gain_ref, gg_ref)


def in_rows_kernel(count, hidden, me_ref, *refs):
    blocks, (w_ref, gain_ref, in_ref, gg_ref) = refs[:count], refs[count:]
    slot = blocks[0].shape[1] // 2
    for i in range(2):
        piece = (slice(None), slice(i * slot, i * slot + hidden))
        values = [value.astype(F32) for value in ordered(blocks, me_ref[0], piece)]
        in_ref[:, i * count * hidden : (i + 1) * count * hidden] = jnp.concatenate(values, axis=1)
    gain_part(w_ref, in_ref, gain_ref, gg_ref)


def finish_rows(kernel, blocks, weight, gain, me, widths, name):
    rows = weight.shape[0]
    shapes = [jax.ShapeDtypeStruct((rows, n), F32) for n in widths]
    return pl.pallas_call(
        kernel,
        in_specs=[pl.BlockSpec(memory_space=pltpu.SMEM)] + [pl.BlockSpec(memory_space=pltpu.VMEM)] * (len(blocks) + 2),
        out_shape=shapes,
        cost_estimate=pl.CostEstimate(flops=0, bytes_accessed=8 * rows * sum(widths), transcendentals=0),
        name=name,
    )(me[None], *blocks, weight, gain[:, None])


def normal(values):
    centered = values - jnp.mean(values, axis=-1, keepdims=True)
    scale = lax.rsqrt(jnp.mean(centered * centered, axis=-1, keepdims=True) + NORM_EPS)
    return centered * scale, scale


def norm_back(upstream, gain, values):
    unit, scale = normal(values)
    weighted = upstream * gain
    return scale * (
        weighted
        - jnp.mean(weighted, axis=-1, keepdims=True)
        - unit * jnp.mean(weighted * unit, axis=-1, keepdims=True)
    )


def matmul(a, b):
    return jnp.dot(a, b, preferred_element_type=F32)


def matmul_nt(a, b):
    return lax.dot_general(a, b, (((1,), (1,)), ((), ())), preferred_element_type=F32)


def matmul_tn(a, b):
    return lax.dot_general(a, b, (((0,), (0,)), ((), ())), preferred_element_type=F32)


def on_device(
    hidden_in, segment_ids, valid_tokens, w_qkv, w_attn_out, w_in_proj, w_out_proj, attn_gain, mlp_gain, cotangent
):
    seq_size, fsdp_size = lax.axis_size("seq"), lax.axis_size("fsdp")
    seq, fsdp = lax.axis_index("seq"), lax.axis_index("fsdp")
    x_low, cot = hidden_in[0], cotangent[0]
    tokens = x_low.shape[0]
    length = tokens * seq_size
    part = D // seq_size
    hidden = FF // seq_size
    rel = [seq ^ k for k in range(seq_size)]

    first_mine = [lax.dynamic_slice_in_dim(w_qkv, i * D + seq * part, part, axis=1) for i in range(3)]
    first_mine.append(lax.dynamic_slice_in_dim(w_attn_out, seq * part, part, axis=1))
    gains = jnp.stack([attn_gain, mlp_gain], axis=1)
    first_mine.append(jnp.pad(gains, ((0, 0), (0, LANES - 2))))
    first_mine = jnp.concatenate(first_mine, axis=1)
    first_weight = gather_rows(first_mine)
    core = fsdp % 2
    slot = -(-hidden // LANES) * LANES
    if paired():
        down_mine = transpose_devices(lax.dynamic_slice_in_dim(w_out_proj, seq * part, part, axis=1))
    x_near = relay_first(x_low)
    out_mine = first_weight[:, 3 * part : 4 * part]
    gains = first_weight[:, 4 * part :].T.astype(F32)
    gain_one, gain_two = gains[0:1], gains[1:2]
    core = fsdp % 2
    slot = -(-hidden // LANES) * LANES
    def padded(rows):
        return jnp.pad(rows, ((0, 0), (0, slot - hidden)))

    def halves(rows):
        half = rows.shape[1] // 2
        low, high = rows[:, :half], rows[:, half:]
        return jnp.where(core == 0, low, high), jnp.where(core == 0, high, low)

    def by_core(mine, other):
        return jnp.where(core == 0, mine, other), jnp.where(core == 0, other, mine)

    in_mine = [
        padded(lax.dynamic_slice_in_dim(w_in_proj, i * FF + seq * hidden, hidden, axis=1)) for i in range(2)
    ]
    if paired():
        x_near, down_mine = after((x_near, down_mine))
        x_blocks = relay_last(x_low, *x_near)
        kept, sent = halves(down_mine)
        down_mine = jnp.concatenate(by_core(kept, after(swap(sent, "fsdp", 1), *x_blocks)), axis=0)
        feed_weight = gather_rows(jnp.concatenate(in_mine + [padded(down_mine.T)], axis=1))
    else:
        down_weight = lax.all_gather(w_out_proj, "fsdp", axis=0, tiled=True)
        down_weight = lax.dynamic_slice_in_dim(down_weight, seq * hidden, hidden, axis=0)
        feed_weight = jnp.concatenate([gather_rows(jnp.concatenate(in_mine, axis=1)), padded(down_weight.T)], axis=1)
        x_blocks = relay_last(x_low, *x_near)
    cot_near = relay_first(after(cot, *x_blocks))

    def in_order(blocks):
        bit = 1
        while bit < seq_size:
            flip = (seq & bit) != 0
            blocks = [jnp.where(flip, blocks[k ^ bit], blocks[k]) for k in range(seq_size)]
            bit *= 2
        return blocks


    def by_block(row):
        return jnp.concatenate([lax.dynamic_slice_in_dim(row, r * tokens, tokens) for r in rel])

    seg_all, valid_all = by_block(segment_ids[0]), by_block(valid_tokens[0])
    positions = by_block(jnp.arange(length, dtype=jnp.int32))
    frequency = ROPE_BASE ** (-2.0 * jnp.arange(HD // 2, dtype=F32) / HD)
    angles = positions.astype(F32)[:, None] * frequency[None, :]
    cosine, sine = lax.optimization_barrier((jnp.cos(angles), jnp.sin(angles)))
    cosine = jnp.concatenate([cosine] * 4, axis=1)
    sine = jnp.concatenate([-sine, sine] * 2, axis=1)
    seg_col, valid_col, seg_row = seg_all[:, None], valid_all[:, None], seg_all[None, :]

    a_low, q, k, v = project_qkv(x_blocks, first_weight, gain_one, cosine, sine)
    k, cot_near = after((k, cot_near), q)
    cot_blocks = relay_last(cot, *cot_near)
    mixed, lse = attend_forward(q, k, v, seg_col, valid_col, seg_row, tokens)

    out_near = relay_first(out_mine)
    mixed, out_near, cot_blocks = after((mixed, out_near, cot_blocks))
    out_weight = jnp.concatenate(in_order(relay_last(out_mine, *out_near)), axis=1)

    def to_tokens(blocks):
        came = [blocks[:tokens]] + [
            swap(blocks[i * tokens : (i + 1) * tokens], "seq", i) for i in range(1, seq_size)
        ]
        return jnp.concatenate(in_order(came), axis=1)

    mixed_low = to_tokens(mixed)
    x = x_low.astype(F32)
    attn_branch = matmul(mixed_low, out_weight)
    middle = x + attn_branch
    normed_two = (normal(middle)[0] * gain_two).astype(BF)
    normed_two = after(normed_two, *cot_blocks)

    b_blocks = share_seq(normed_two)
    fed, came, mlp_all = [None] * seq_size, [], None
    for i in range(seq_size):
        b = after(b_blocks[i], *came[:-1]) if len(came) > 1 else b_blocks[i]
        fed[i] = feed_forward(
            b, cot_blocks[i], feed_weight, hidden, seq, i, seq_size, F32 if i == 0 else BF, mlp_all
        )
        mlp_all = fed[i][4]
        if i > 0:
            came.append(swap(fed[i][3], "seq", i))
    m_blocks, gz_i, gz_g, gb_blocks, _ = zip(*fed)
    fed_grads = weight_gradients([after(b_blocks, *came[:-1])], [gz_i, gz_g], ((0, 1), (0, 2)), 3, 0)
    fed_grads = weight_gradients([after(cot_blocks, *came)], [m_blocks], ((0, 1),), 3, 2, fed_grads)
    grad_normed_two = gb_blocks[0]
    for block in came:
        grad_normed_two = grad_normed_two + block.astype(F32)
    grad_middle = cot.astype(F32) + norm_back(grad_normed_two, gain_two, middle)
    grad_attn_low = grad_middle.astype(BF)
    grad_mixed = matmul_nt(grad_attn_low, out_weight).astype(BF)

    sent = [lax.dynamic_slice_in_dim(grad_mixed, r * part, part, axis=1) for r in rel]
    came = [sent[0]] + [swap(sent[i], "seq", i) for i in range(1, seq_size)]
    grad_by_heads = jnp.concatenate(came, axis=0)
    out_part = matmul_tn(mixed_low, after(grad_attn_low, grad_by_heads)).astype(BF)
    grad_by_heads = after(grad_by_heads, out_part)
    mlp_came = exchange_seq(after(mlp_all, grad_by_heads))

    def own_rows(partial):
        return lax.psum_scatter(partial, "fsdp", scatter_dimension=0, tiled=True)

    fed_rows = own_rows(fed_grads)
    out_rows = own_rows(out_part)

    gp = attend_backward(
        q, k, v, grad_by_heads, lse, seg_col, valid_col, seg_row, cosine, sine, tokens
    )
    fed_late = after(fed_rows, gp)
    in_rows, down_rows = fed_late[:, : 2 * slot], fed_late[:, 2 * slot : 2 * slot + hidden]
    in_all = share_seq(in_rows)
    mlp_branch = sum_blocks(after(mlp_came, gp))
    result = middle + mlp_branch
    valid_mine = valid_all[:tokens].astype(F32)[:, None]
    stats = jnp.stack(
        [
            jnp.sum(valid_mine * result * result),
            jnp.sum(valid_mine * attn_branch * attn_branch),
            jnp.sum(valid_mine * mlp_branch * mlp_branch),
            jnp.sum(valid_mine),
        ]
    )
    stats = sum_over(jnp.broadcast_to(stats[:, None], (4, 128)), "seq", [1])
    if paired():
        down_rows = transpose_devices(down_rows)
        ga_parts = project_back(gp, first_weight, seq, seq_size)
        gp_late = after(gp, ga_parts, down_rows, *in_all[1:3])
        mine, away = last_gradients(a_low, gp_late, fsdp, fsdp_size)
        mine = mine + swap(away, "fsdp", 1).astype(F32)
        down_rows = after(down_rows, mine)
        kept, sent = halves(down_rows)
        down_rows = jnp.concatenate(by_core(kept, swap(sent, "fsdp", 1)), axis=0).T
        rows = mine.shape[0] // (fsdp_size // 2)
        came = [swap(mine[k * rows : (k + 1) * rows].astype(BF), "fsdp", 2 * k) for k in range(1, fsdp_size // 2)]
        came = after(came, down_rows, out_rows, *in_all)
        last = mine[:rows]
        for block in came:
            last = last + block.astype(F32)
    else:
        mine, ga_parts = matmul_tn(a_low, gp), project_back(gp, first_weight, seq, seq_size)
        last = lax.psum_scatter(mine, "fsdp", scatter_dimension=0, tiled=True)
    ga_came = exchange_seq(ga_parts)
    stats = after(sum_over(after(stats, mine), "seq", [2]), last)
    last = jnp.concatenate([last.astype(BF), out_rows], axis=1)
    ga_came, in_all = after((ga_came, in_all), last)

    grad_in_weight, grad_gain_two = finish_rows(
        functools.partial(in_rows_kernel, seq_size, hidden), in_all, w_in_proj, mlp_gain, seq, (2 * FF, 1), "in_rows"
    )
    if paired():
        grad_down = jnp.concatenate(in_order(share_seq(down_rows)), axis=1).astype(F32)
    else:
        down = lax.all_gather(down_rows, ("seq", "fsdp"), axis=0, tiled=True)
        down = down.reshape(seq_size, D, hidden).transpose(0, 2, 1).reshape(FF, D)
        rows = FF // fsdp_size
        grad_down = lax.dynamic_slice_in_dim(down, fsdp * rows, rows, axis=0).astype(F32)

    grad_normed = sum_blocks(ga_came)
    grad_inputs = grad_middle + norm_back(grad_normed, gain_one, x)
    stats = sum_over(stats, "fsdp", [1])
    last, stats = after((share_seq(last), stats), grad_in_weight, grad_down, grad_inputs)
    grad_qkv_weight, grad_out_weight, grad_gain_one = finish_rows(
        functools.partial(last_rows_kernel, seq_size), last, w_qkv, attn_gain, seq, (3 * D, D, 1), "last_rows"
    )

    if paired():
        stats = sum_over(stats, "fsdp", range(2, fsdp_size, 2))
    else:
        bit = 2
        while bit < fsdp_size:
            stats = sum_over(stats, "fsdp", [bit])
            bit *= 2
    stats = stats[:, 0]
    root_means = jnp.sqrt(stats[:3] / (jnp.maximum(stats[3], 1.0) * D))

    return (
        result.astype(BF)[None],
        grad_inputs[None],
        grad_qkv_weight,
        grad_out_weight,
        grad_in_weight,
        grad_down,
        grad_gain_one[:, 0],
        grad_gain_two[:, 0],
        root_means,
    )


def solution(mesh):
    in_specs = (
        P("fsdp", "seq", None),
        P("fsdp", None),
        P("fsdp", None),
        P("fsdp", None),
        P("fsdp", None),
        P("fsdp", None),
        P("fsdp", None),
        P("fsdp"),
        P("fsdp"),
        P("fsdp", "seq", None),
    )
    out_specs = (
        P("fsdp", "seq", None),
        P("fsdp", "seq", None),
        P("fsdp", None),
        P("fsdp", None),
        P("fsdp", None),
        P("fsdp", None),
        P("fsdp"),
        P("fsdp"),
        P(),
    )
    return jax.shard_map(on_device, mesh=mesh, in_specs=in_specs, out_specs=out_specs, check_vma=False)
```

```python
import functools

import jax
import jax.numpy as jnp
from jax import lax
from jax.experimental import pallas as pl
from jax.experimental.pallas import tpu as pltpu
from jax.sharding import PartitionSpec as P

D = 1024
HEADS = 16
HD = 64
FF = 2624

ROPE_BASE = 160000.0
NORM_EPS = 1e-05
LANES = 128
BF = jnp.bfloat16
F32 = jnp.float32


def swap(x, axis, bit):
    return lax.ppermute(x, axis, [(i, i ^ bit) for i in range(lax.axis_size(axis))])


def after(x, *others):
    return lax.optimization_barrier((x, others))[0]


def share_seq(block):
    return [block] + [swap(block, "seq", k) for k in range(1, lax.axis_size("seq"))]


def relay_first(block):
    return swap(block, "seq", 1), swap(block, "seq", 2)


def relay_last(block, one, two):
    if lax.axis_size("seq") != 4:
        return share_seq(block)
    half = block.shape[0] // 2
    upper, lower = swap(two[:half], "seq", 1), swap(one[half:], "seq", 2)
    return [block, one, two, jnp.concatenate([upper, lower], axis=0)]


def exchange_seq(blocks):
    return lax.all_to_all(blocks, "seq", split_axis=0, concat_axis=0, tiled=True)


def sum_blocks(blocks):
    rows = blocks.shape[0] // lax.axis_size("seq")
    total = blocks[:rows].astype(F32)
    for i in range(1, lax.axis_size("seq")):
        total = total + blocks[i * rows : (i + 1) * rows].astype(F32)
    return total


def paired():
    return lax.axis_size("fsdp") == 2 * lax.axis_size("seq")


def gather_rows(block):
    return lax.all_gather(block, "fsdp", axis=0, tiled=True)


def transpose_devices(x):
    seq, fsdp = lax.axis_size("seq"), lax.axis_size("fsdp")
    pairs = [
        (s * fsdp + 2 * z + c, z * fsdp + 2 * s + c)
        for s in range(seq)
        for z in range(fsdp // 2)
        for c in range(2)
    ]
    return lax.ppermute(x, ("seq", "fsdp"), pairs)


def tree_sum(values):
    while len(values) > 1:
        values = [values[i] + values[i + 1] for i in range(0, len(values), 2)]
    return values[0]


def in_three(values):
    terms = []
    for _ in range(3):
        terms.append(lax.reduce_precision(values, 8, 7))
        values = values - terms[-1]
    return jnp.stack(terms).astype(BF)


def from_three(terms):
    terms = terms.astype(F32)
    return (terms[0] + terms[1]) + terms[2]


def half_swap(values):
    width = values.shape[1]
    lane = lax.broadcasted_iota(jnp.int32, values.shape, 1)
    ahead = pltpu.roll(values, width - HD // 2, 1)
    behind = pltpu.roll(values, HD // 2, 1)
    return jnp.where(lane % HD < HD // 2, ahead, behind)


def wide(table, width):
    return jnp.concatenate([table] * (width // table.shape[1]), axis=1)


def qkv_kernel(*refs):
    count = 4
    xs = refs[:count]
    w_ref, gain_ref, cos_ref, sin_ref, a_ref, q_ref, k_ref, v_ref, held = refs[count:]
    step = pl.program_id(0)
    for i in range(count):

        @pl.when(step == i)
        def _():
            held[...] = xs[i][...].astype(F32)

    values = held[...]
    centered = values - jnp.mean(values, axis=1, keepdims=True)
    variance = jnp.mean(centered * centered, axis=1, keepdims=True)
    low = (centered * lax.rsqrt(variance + NORM_EPS) * gain_ref[...]).astype(BF)
    a_ref[...] = low
    p = jnp.dot(low, w_ref[...], preferred_element_type=F32)
    part = p.shape[1] // 3
    turned = p[:, : 2 * part]
    turned = turned * wide(cos_ref[...], 2 * part) + half_swap(turned) * wide(sin_ref[...], 2 * part)
    q_ref[...] = turned[:, :part].astype(BF) * (HD**-0.5)
    k_ref[...] = turned[:, part:].astype(BF)
    v_ref[...] = p[:, 2 * part :].astype(BF)


def project_qkv(blocks, weight, gain, cosine, sine):
    rows, width = blocks[0].shape
    part = (weight.shape[1] - LANES) // 4
    count = len(blocks)
    whole = lambda a: pl.BlockSpec(a.shape, lambda i: (0, 0))
    tile = lambda n: pl.BlockSpec((rows, n), lambda i: (i, 0))
    shape = lambda n: jax.ShapeDtypeStruct((rows * count, n), BF)
    return pl.pallas_call(
        qkv_kernel,
        grid=(count,),
        in_specs=[whole(b) for b in blocks]
        + [pl.BlockSpec((width, 3 * part), lambda i: (0, 0)), whole(gain), tile(cosine.shape[1]), tile(sine.shape[1])],
        out_specs=[tile(width), tile(part), tile(part), tile(part)],
        out_shape=[shape(width), shape(part), shape(part), shape(part)],
        scratch_shapes=[pltpu.VMEM((rows, width), F32)],
        cost_estimate=pl.CostEstimate(
            flops=2 * rows * count * width * 3 * part,
            bytes_accessed=2 * rows * count * (2 * width + 3 * part) + 2 * width * 3 * part,
            transcendentals=0,
        ),
        name="qkv",
    )(*blocks, weight, gain, cosine, sine)


def mask_bias(seg_col, valid_col, seg_row, first_row):
    shape = (seg_col.shape[0], seg_row.shape[1])
    key = lax.broadcasted_iota(jnp.int32, shape, 0)
    query = lax.broadcasted_iota(jnp.int32, shape, 1) + first_row
    allowed = (seg_col == seg_row) & ((valid_col > 0) | (key == query))
    return jnp.where(allowed, 0.0, -1e30)


def forward_kernel(q_ref, k_ref, v_ref, segc_ref, valc_ref, segr_ref, o_ref, lse_ref, vt_ref, ot_ref, bias_ref):
    step = pl.program_id(0)
    rows, width = q_ref.shape

    @pl.when(step == 0)
    def _():
        vt_ref[...] = v_ref[...].T

    bias_ref[...] = mask_bias(segc_ref[...], valc_ref[...], segr_ref[...], step * rows)
    qt = q_ref[...].T
    feature = lax.broadcasted_iota(jnp.int32, qt.shape, 0) // HD

    def head(h, carry):
        mine = jnp.where(feature == h, qt, jnp.zeros_like(qt))
        scores = jnp.dot(k_ref[...], mine, preferred_element_type=F32) + bias_ref[...]
        top = jnp.max(scores, axis=0, keepdims=True)
        exponent = jnp.exp(scores - top)
        total = jnp.sum(exponent, axis=0, keepdims=True)
        weights = (exponent * (1.0 / total)).astype(BF)
        start = pl.multiple_of(h * HD, HD)
        ot_ref[pl.ds(start, HD), :] = jnp.dot(
            vt_ref[pl.ds(start, HD), :], weights, preferred_element_type=F32
        )
        lse_ref[pl.ds(h, 1), :] = top + jnp.log(total)
        return carry

    lax.fori_loop(0, width // HD, head, 0)
    o_ref[...] = ot_ref[...].T.astype(BF)


def attend_forward(q, k, v, seg_col, valid_col, seg_row, rows):
    length, width = q.shape
    whole = lambda a: pl.BlockSpec(a.shape, lambda i: (0, 0))
    tile = pl.BlockSpec((rows, width), lambda i: (i, 0))
    return pl.pallas_call(
        forward_kernel,
        grid=(length // rows,),
        in_specs=[tile, whole(k), whole(v), whole(seg_col), whole(valid_col), pl.BlockSpec((1, rows), lambda i: (0, i))],
        out_specs=[tile, pl.BlockSpec((8, rows), lambda i: (0, i))],
        out_shape=[jax.ShapeDtypeStruct((length, width), BF), jax.ShapeDtypeStruct((8, length), F32)],
        scratch_shapes=[pltpu.VMEM((width, length), BF), pltpu.VMEM((width, rows), F32), pltpu.VMEM((length, rows), F32)],
        cost_estimate=pl.CostEstimate(
            flops=4 * length * length * width, bytes_accessed=8 * length * width, transcendentals=length * length * 4
        ),
        name="attend",
    )(q, k, v, seg_col, valid_col, seg_row)


def backward_kernel(
    q_ref, go_ref, lse_ref, k_ref, v_ref, segc_ref, valc_ref, segr_ref, cos_ref, sin_ref,
    gp_ref, kt_ref, dk_ref, dv_ref, dqt_ref, bias_ref,
):
    step = pl.program_id(0)
    rows, width = q_ref.shape

    @pl.when(step == 0)
    def _():
        kt_ref[...] = k_ref[...].T
        dk_ref[...] = jnp.zeros_like(dk_ref)
        dv_ref[...] = jnp.zeros_like(dv_ref)

    bias_ref[...] = mask_bias(segc_ref[...], valc_ref[...], segr_ref[...], step * rows)
    qt, got = q_ref[...].T, go_ref[...].T
    feature = lax.broadcasted_iota(jnp.int32, qt.shape, 0) // HD
    lane = lax.broadcasted_iota(jnp.int32, (rows, width), 1) // HD
    none = jnp.zeros_like(qt)
    none_row = jnp.zeros((rows, width), BF)

    def head(h, carry):
        scores = jnp.dot(k_ref[...], jnp.where(feature == h, qt, none), preferred_element_type=F32)
        weights = jnp.exp(scores + bias_ref[...] - lse_ref[pl.ds(h, 1), :])
        upstream = jnp.dot(v_ref[...], jnp.where(feature == h, got, none), preferred_element_type=F32)
        inner = jnp.sum(weights * upstream, axis=0, keepdims=True)
        low = (weights * (upstream - inner)).astype(BF)
        dv_ref[...] += jnp.dot(
            weights.astype(BF), jnp.where(lane == h, go_ref[...], none_row), preferred_element_type=F32
        )
        dk_ref[...] += jnp.dot(low, jnp.where(lane == h, q_ref[...], none_row), preferred_element_type=F32)
        start = pl.multiple_of(h * HD, HD)
        dqt_ref[pl.ds(start, HD), :] = jnp.dot(kt_ref[pl.ds(start, HD), :], low, preferred_element_type=F32)
        return carry

    lax.fori_loop(0, width // HD, head, 0)

    def unturn(values, cosine, sine):
        values = values.astype(BF).astype(F32)
        return (values * wide(cosine, width) - half_swap(values) * wide(sine, width)).astype(BF)

    here = pl.ds(pl.multiple_of(step * rows, rows), rows)
    gp_ref[here, :width] = unturn(dqt_ref[...].T * (HD**-0.5), cos_ref[here, :], sin_ref[here, :])

    @pl.when(step == pl.num_programs(0) - 1)
    def _():
        gp_ref[:, width : 2 * width] = unturn(dk_ref[...], cos_ref[...], sin_ref[...])
        gp_ref[:, 2 * width :] = dv_ref[...].astype(BF)


def attend_backward(q, k, v, grad_out, lse, seg_col, valid_col, seg_row, cosine, sine, rows):
    length, width = q.shape
    whole = lambda a: pl.BlockSpec(a.shape, lambda i: (0, 0))
    tile = pl.BlockSpec((rows, width), lambda i: (i, 0))
    return pl.pallas_call(
        backward_kernel,
        grid=(length // rows,),
        in_specs=[
            tile, tile, pl.BlockSpec((8, rows), lambda i: (0, i)), whole(k), whole(v),
            whole(seg_col), whole(valid_col), pl.BlockSpec((1, rows), lambda i: (0, i)), whole(cosine), whole(sine),
        ],
        out_specs=pl.BlockSpec((length, 3 * width), lambda i: (0, 0)),
        out_shape=jax.ShapeDtypeStruct((length, 3 * width), BF),
        scratch_shapes=[
            pltpu.VMEM((width, length), BF), pltpu.VMEM((length, width), F32), pltpu.VMEM((length, width), F32),
            pltpu.VMEM((width, rows), F32), pltpu.VMEM((length, rows), F32),
        ],
        cost_estimate=pl.CostEstimate(
            flops=10 * length * length * width, bytes_accessed=20 * length * width, transcendentals=length * length * 4
        ),
        name="attend_back",
    )(q, grad_out, lse, k, v, seg_col, valid_col, seg_row, cosine, sine)


def erf(x):
    x = jnp.clip(x, -3.832506856900711, 3.832506856900711)
    square = x * x
    top = 0.00022905065861350646
    for c in (0.0034082910107109506, 0.050955695062380861, 0.18520832239976145, 1.128379143519084):
        top = top * square + c
    low = -1.1791602954361697e-7
    for c in (0.000023547966471313185, 0.0010179625278914885, 0.014070470171167667, 0.11098505178285362, 0.49746925110067538, 1.0):
        low = low * square + c
    return x * top / low


def nt(a, b):
    return lax.dot_general(a, b, (((1,), (1,)), ((), ())), preferred_element_type=F32)


def feed_kernel(hidden, me_ref, b_ref, g_ref, w_ref, *refs):
    m_ref, gi_ref, gg_ref, gb_ref, mlp_ref = refs[-5:]
    b = b_ref[...]
    slot = w_ref.shape[1] // 3
    wi_ref, wg_ref, wd_ref = (w_ref.at[:, i * slot : i * slot + hidden] for i in range(3))
    inner = jnp.dot(b, wi_ref[...], preferred_element_type=F32)
    gate = jnp.dot(b, wg_ref[...], preferred_element_type=F32)
    upstream = jnp.dot(g_ref[...], wd_ref[...], preferred_element_type=F32)
    half = 0.5 * (1.0 + erf(inner * 0.7071067811865476))
    gelu = inner * half
    slope = half + inner * jnp.exp(-0.5 * inner * inner) * 0.3989422804014327
    m = (gelu * gate).astype(BF)
    gi = (upstream * gate * slope).astype(BF)
    gg = (upstream * gelu).astype(BF)
    m_ref[...] = m
    gi_ref[...] = gi
    gg_ref[...] = gg
    gb_ref[...] = (nt(gi, wi_ref[...]) + nt(gg, wg_ref[...])).astype(gb_ref.dtype)
    mlp_ref[...] = nt(m, wd_ref[...]).astype(mlp_ref.dtype)


def feed_forward(b, g, w, hidden, me, place, count, dtype, onto):
    rows, width = b.shape
    whole = lambda r, n: pl.BlockSpec((r, n), lambda i, me: (0, 0))
    narrow = jax.ShapeDtypeStruct((rows, hidden), BF)
    operands, specs = [b, g, w], [whole(rows, width), whole(rows, width), whole(*w.shape)]
    if onto is not None:
        operands.append(onto)
        specs.append(pl.BlockSpec(memory_space=pl.ANY))
    return pl.pallas_call(
        functools.partial(feed_kernel, hidden),
        grid_spec=pltpu.PrefetchScalarGridSpec(
            num_scalar_prefetch=1,
            grid=(1,),
            in_specs=specs,
            out_specs=[whole(rows, hidden)] * 3
            + [whole(rows, width), pl.BlockSpec((rows, width), lambda i, me: (me[0] ^ place, 0))],
        ),
        out_shape=[narrow] * 3
        + [jax.ShapeDtypeStruct((rows, width), dtype), jax.ShapeDtypeStruct((rows * count, width), BF)],
        input_output_aliases={} if onto is None else {4: 4},
        cost_estimate=pl.CostEstimate(
            flops=12 * rows * width * hidden,
            bytes_accessed=6 * width * hidden + 8 * rows * width + 6 * rows * hidden,
            transcendentals=rows * hidden,
        ),
        name="feed",
    )(me[None], *operands)


def tn(a, b):
    return lax.dot_general(a, b, (((0,), (0,)), ((), ())), preferred_element_type=F32)


def weight_kernel(count, slot, pairs, *refs):
    out_ref = refs[-1]
    hidden = refs[(pairs[0][1]) * count].shape[1]
    for place, (left, right) in enumerate(pairs):
        total = None
        for i in range(count):
            term = tn(refs[left * count + i][...], refs[right * count + i][...])
            total = term if total is None else total + term
        out_ref[:, place * slot : place * slot + hidden] = total.astype(BF)
        if hidden < slot:
            out_ref[:, place * slot + hidden : (place + 1) * slot] = jnp.zeros((out_ref.shape[0], slot - hidden), BF)


def weight_gradients(lefts, rights, pairs, slots, place, onto=None):
    count = len(lefts[0])
    rows, width = lefts[0][0].shape
    hidden = rights[0][0].shape[1]
    slot = -(-hidden // LANES) * LANES
    wide_spec = pl.BlockSpec((rows, 256), lambda i: (0, i))
    whole = pl.BlockSpec((rows, hidden), lambda i: (0, 0))
    operands = [b for group in lefts for b in group] + [b for group in rights for b in group]
    specs = [wide_spec] * (len(lefts) * count) + [whole] * (len(rights) * count)
    aliases = {}
    if onto is not None:
        aliases = {len(operands): 0}
        operands.append(onto)
        specs.append(pl.BlockSpec(memory_space=pl.ANY))
    return pl.pallas_call(
        functools.partial(weight_kernel, count, slot, pairs),
        grid=(width // 256,),
        in_specs=specs,
        out_specs=pl.BlockSpec((256, len(pairs) * slot), lambda i: (i, place // len(pairs))),
        out_shape=jax.ShapeDtypeStruct((width, slots * slot), BF),
        input_output_aliases=aliases,
        cost_estimate=pl.CostEstimate(
            flops=2 * len(pairs) * rows * count * width * hidden,
            bytes_accessed=2 * count * rows * (len(lefts) * width + len(rights) * hidden),
            transcendentals=0,
        ),
        name="weight_gradients",
    )(*operands)


def last_kernel(me_ref, a_ref, gp_ref, mine_ref, away_ref):
    total = tn(a_ref[...], gp_ref[...])

    @pl.when(pl.program_id(0) % 2 == 0)
    def _():
        mine_ref[...] = total

    @pl.when(pl.program_id(0) % 2 == 1)
    def _():
        away_ref[...] = total.astype(BF)


def last_gradients(a, gp, me, size):
    length, width = a.shape
    rows, columns = width // size, gp.shape[1]
    out = lambda dtype: jax.ShapeDtypeStruct((width // 2, columns), dtype)
    return pl.pallas_call(
        last_kernel,
        grid_spec=pltpu.PrefetchScalarGridSpec(
            num_scalar_prefetch=1,
            grid=(size,),
            in_specs=[
                pl.BlockSpec((length, rows), lambda i, me: (0, me[0] ^ i)),
                pl.BlockSpec((length, columns), lambda i, me: (0, 0)),
            ],
            out_specs=[pl.BlockSpec((rows, columns), lambda i, me: (i // 2, 0))] * 2,
        ),
        out_shape=[out(F32), out(BF)],
        cost_estimate=pl.CostEstimate(
            flops=2 * length * width * columns,
            bytes_accessed=2 * length * (width + columns) + 3 * width * columns,
            transcendentals=0,
        ),
        name="last_gradients",
    )(me[None], a, gp)


def qkv_back_kernel(me_ref, gp_ref, w_ref, out_ref):
    out_ref[...] = nt(gp_ref[...], w_ref[...]).astype(BF)


def project_back(gp, weight, me, count):
    rows, width = gp.shape[0] // count, weight.shape[0]
    return pl.pallas_call(
        qkv_back_kernel,
        grid_spec=pltpu.PrefetchScalarGridSpec(
            num_scalar_prefetch=1,
            grid=(count,),
            in_specs=[
                pl.BlockSpec((rows, gp.shape[1]), lambda i, me: (i, 0)),
                pl.BlockSpec((width, gp.shape[1]), lambda i, me: (0, 0)),
            ],
            out_specs=pl.BlockSpec((rows, width), lambda i, me: (me[0] ^ i, 0)),
        ),
        out_shape=jax.ShapeDtypeStruct((rows * count, width), BF),
        cost_estimate=pl.CostEstimate(
            flops=2 * rows * count * width * gp.shape[1],
            bytes_accessed=2 * (rows * count * (width + gp.shape[1]) + width * gp.shape[1]),
            transcendentals=0,
        ),
        name="project_back",
    )(me[None], gp, weight)


def ordered(refs, me, piece):
    values = [ref[piece] for ref in refs]
    bit = 1
    while bit < len(values):
        flip = (me & bit) != 0
        values = [jnp.where(flip, values[k ^ bit], values[k]) for k in range(len(values))]
        bit *= 2
    return values


def gain_part(w_ref, grad_ref, gain_ref, out_ref):
    total = jnp.sum(w_ref[...].astype(F32) * grad_ref[...], axis=1, keepdims=True)
    out_ref[...] = total / gain_ref[...].astype(F32)


def last_rows_kernel(count, me_ref, *refs):
    blocks, (w_ref, gain_ref, qkv_ref, out_ref, gg_ref) = refs[:count], refs[count:]
    part = (blocks[0].shape[1] - LANES) // (3 + count)
    piece = lambda i: (slice(None), slice(i * part, (i + 1) * part))
    for i in range(3):
        for j, value in enumerate(ordered(blocks, me_ref[0], piece(i))):
            first = (i * count + j) * part
            qkv_ref[:, first : first + part] = value.astype(F32)
    for j in range(count):
        total = None
        for value in ordered(blocks, me_ref[0], piece(3 + j)):
            total = value.astype(F32) if total is None else total + value.astype(F32)
        out_ref[:, j * part : (j + 1) * part] = total
    gain_part(w_ref, qkv_ref, gain_ref, gg_ref)


def in_rows_kernel(count, hidden, me_ref, *refs):
    blocks, (w_ref, gain_ref, in_ref, gg_ref) = refs[:count], refs[count:]
    slot = blocks[0].shape[1] // 2
    for i in range(2):
        piece = (slice(None), slice(i * slot, i * slot + hidden))
        values = [value.astype(F32) for value in ordered(blocks, me_ref[0], piece)]
        in_ref[:, i * count * hidden : (i + 1) * count * hidden] = jnp.concatenate(values, axis=1)
    gain_part(w_ref, in_ref, gain_ref, gg_ref)


def finish_rows(kernel, blocks, weight, gain, me, widths, name):
    rows = weight.shape[0]
    shapes = [jax.ShapeDtypeStruct((rows, n), F32) for n in widths]
    return pl.pallas_call(
        kernel,
        in_specs=[pl.BlockSpec(memory_space=pltpu.SMEM)] + [pl.BlockSpec(memory_space=pltpu.VMEM)] * (len(blocks) + 2),
        out_shape=shapes,
        cost_estimate=pl.CostEstimate(flops=0, bytes_accessed=8 * rows * sum(widths), transcendentals=0),
        name=name,
    )(me[None], *blocks, weight, gain[:, None])


def normal(values):
    centered = values - jnp.mean(values, axis=-1, keepdims=True)
    scale = lax.rsqrt(jnp.mean(centered * centered, axis=-1, keepdims=True) + NORM_EPS)
    return centered * scale, scale


def norm_back(upstream, gain, values):
    unit, scale = normal(values)
    weighted = upstream * gain
    return scale * (
        weighted
        - jnp.mean(weighted, axis=-1, keepdims=True)
        - unit * jnp.mean(weighted * unit, axis=-1, keepdims=True)
    )


def matmul(a, b):
    return jnp.dot(a, b, preferred_element_type=F32)


def matmul_nt(a, b):
    return lax.dot_general(a, b, (((1,), (1,)), ((), ())), preferred_element_type=F32)


def matmul_tn(a, b):
    return lax.dot_general(a, b, (((0,), (0,)), ((), ())), preferred_element_type=F32)


def on_device(
    hidden_in, segment_ids, valid_tokens, w_qkv, w_attn_out, w_in_proj, w_out_proj, attn_gain, mlp_gain, cotangent
):
    seq_size, fsdp_size = lax.axis_size("seq"), lax.axis_size("fsdp")
    seq, fsdp = lax.axis_index("seq"), lax.axis_index("fsdp")
    x_low, cot = hidden_in[0], cotangent[0]
    tokens = x_low.shape[0]
    length = tokens * seq_size
    part = D // seq_size
    hidden = FF // seq_size
    rel = [seq ^ k for k in range(seq_size)]

    def by_block(row):
        return jnp.concatenate([lax.dynamic_slice_in_dim(row, r * tokens, tokens) for r in rel])

    seg_all, valid_all = by_block(segment_ids[0]), by_block(valid_tokens[0])
    positions = by_block(jnp.arange(length, dtype=jnp.int32))
    frequency = ROPE_BASE ** (-2.0 * jnp.arange(HD // 2, dtype=F32) / HD)
    angles = positions.astype(F32)[:, None] * frequency[None, :]
    cosine, sine = lax.optimization_barrier((jnp.cos(angles), jnp.sin(angles)))
    cosine = jnp.concatenate([cosine] * 4, axis=1)
    sine = jnp.concatenate([-sine, sine] * 2, axis=1)
    seg_col, valid_col, seg_row = seg_all[:, None], valid_all[:, None], seg_all[None, :]

    first_mine = [lax.dynamic_slice_in_dim(w_qkv, i * D + seq * part, part, axis=1) for i in range(3)]
    first_mine.append(lax.dynamic_slice_in_dim(w_attn_out, seq * part, part, axis=1))
    gains = jnp.stack([attn_gain, mlp_gain], axis=1)
    first_mine.append(jnp.pad(gains, ((0, 0), (0, LANES - 2))))
    first_mine = jnp.concatenate(first_mine, axis=1)
    first_weight = gather_rows(first_mine)
    core = fsdp % 2
    slot = -(-hidden // LANES) * LANES
    if paired():
        down_mine = transpose_devices(lax.dynamic_slice_in_dim(w_out_proj, seq * part, part, axis=1))
    x_near = relay_first(x_low)
    out_mine = first_weight[:, 3 * part : 4 * part]
    gains = first_weight[:, 4 * part :].T.astype(F32)
    gain_one, gain_two = gains[0:1], gains[1:2]
    core = fsdp % 2
    slot = -(-hidden // LANES) * LANES
    def padded(rows):
        return jnp.pad(rows, ((0, 0), (0, slot - hidden)))

    def halves(rows):
        half = rows.shape[1] // 2
        low, high = rows[:, :half], rows[:, half:]
        return jnp.where(core == 0, low, high), jnp.where(core == 0, high, low)

    def by_core(mine, other):
        return jnp.where(core == 0, mine, other), jnp.where(core == 0, other, mine)

    in_mine = [
        padded(lax.dynamic_slice_in_dim(w_in_proj, i * FF + seq * hidden, hidden, axis=1)) for i in range(2)
    ]
    if paired():
        x_blocks = relay_last(x_low, *x_near)
        kept, sent = halves(after(down_mine, x_blocks, cosine, sine, seg_col, valid_col))
        down_mine = jnp.concatenate(by_core(kept, swap(sent, "fsdp", 1)), axis=0)
        feed_weight = gather_rows(jnp.concatenate(in_mine + [padded(down_mine.T)], axis=1))
    else:
        down_weight = lax.all_gather(w_out_proj, "fsdp", axis=0, tiled=True)
        down_weight = lax.dynamic_slice_in_dim(down_weight, seq * hidden, hidden, axis=0)
        feed_weight = jnp.concatenate([gather_rows(jnp.concatenate(in_mine, axis=1)), padded(down_weight.T)], axis=1)
        x_blocks = relay_last(x_low, *x_near)
    cot_near = relay_first(after(cot, *x_blocks))

    def in_order(blocks):
        bit = 1
        while bit < seq_size:
            flip = (seq & bit) != 0
            blocks = [jnp.where(flip, blocks[k ^ bit], blocks[k]) for k in range(seq_size)]
            bit *= 2
        return blocks


    a_low, q, k, v = project_qkv(x_blocks, first_weight, gain_one, cosine, sine)
    k, cot_near = after((k, cot_near), q)
    cot_blocks = relay_last(cot, *cot_near)
    mixed, lse = attend_forward(q, k, v, seg_col, valid_col, seg_row, tokens)

    out_near = relay_first(out_mine)
    mixed, out_near, cot_blocks = after((mixed, out_near, cot_blocks))
    out_weight = jnp.concatenate(in_order(relay_last(out_mine, *out_near)), axis=1)

    def to_tokens(blocks):
        came = [blocks[:tokens]] + [
            swap(blocks[i * tokens : (i + 1) * tokens], "seq", i) for i in range(1, seq_size)
        ]
        return jnp.concatenate(in_order(came), axis=1)

    mixed_low = to_tokens(mixed)
    x = x_low.astype(F32)
    attn_branch = matmul(mixed_low, out_weight)
    middle = x + attn_branch
    normed_two = (normal(middle)[0] * gain_two).astype(BF)
    normed_two = after(normed_two, *cot_blocks)

    b_blocks = share_seq(normed_two)
    fed, came, mlp_all = [None] * seq_size, [], None
    for i in range(seq_size):
        b = after(b_blocks[i], *came[:-1]) if len(came) > 1 else b_blocks[i]
        fed[i] = feed_forward(
            b, cot_blocks[i], feed_weight, hidden, seq, i, seq_size, F32 if i == 0 else BF, mlp_all
        )
        mlp_all = fed[i][4]
        if i > 0:
            came.append(swap(fed[i][3], "seq", i))
    m_blocks, gz_i, gz_g, gb_blocks, _ = zip(*fed)
    fed_grads = weight_gradients([after(b_blocks, *came[:-2])], [gz_i, gz_g], ((0, 1), (0, 2)), 3, 0)
    fed_grads = weight_gradients([after(cot_blocks, *came)], [m_blocks], ((0, 1),), 3, 2, fed_grads)
    grad_normed_two = gb_blocks[0]
    for block in came:
        grad_normed_two = grad_normed_two + block.astype(F32)
    grad_middle = cot.astype(F32) + norm_back(grad_normed_two, gain_two, middle)
    grad_attn_low = grad_middle.astype(BF)
    grad_mixed = matmul_nt(grad_attn_low, out_weight).astype(BF)

    sent = [lax.dynamic_slice_in_dim(grad_mixed, r * part, part, axis=1) for r in rel]
    came = [sent[0]] + [swap(sent[i], "seq", i) for i in range(1, seq_size)]
    grad_by_heads = jnp.concatenate(came, axis=0)
    out_part = matmul_tn(mixed_low, after(grad_attn_low, grad_by_heads)).astype(BF)
    grad_by_heads = after(grad_by_heads, out_part)
    mlp_came = exchange_seq(after(mlp_all, grad_by_heads))

    def own_rows(partial):
        return lax.psum_scatter(partial, "fsdp", scatter_dimension=0, tiled=True)

    fed_rows = own_rows(fed_grads)
    out_rows = own_rows(out_part)

    gp = attend_backward(
        q, k, v, grad_by_heads, lse, seg_col, valid_col, seg_row, cosine, sine, tokens
    )
    fed_late = after(fed_rows, gp)
    in_rows, down_rows = fed_late[:, : 2 * slot], fed_late[:, 2 * slot :]
    in_all = share_seq(in_rows)
    if paired():
        down_rows = transpose_devices(down_rows)
        ga_parts = project_back(gp, first_weight, seq, seq_size)
        gp_late = after(gp, ga_parts, down_rows, *in_all[1:3])
        mine, away = last_gradients(a_low, gp_late, fsdp, fsdp_size)
    else:
        mine, ga_parts = matmul_tn(a_low, gp), project_back(gp, first_weight, seq, seq_size)
        away = mine
    mlp_branch = sum_blocks(after(mlp_came, away))
    result = middle + mlp_branch
    valid_mine = valid_all[:tokens].astype(F32)[:, None]
    stats = jnp.stack(
        [
            jnp.sum(valid_mine * result * result),
            jnp.sum(valid_mine * attn_branch * attn_branch),
            jnp.sum(valid_mine * mlp_branch * mlp_branch),
            jnp.sum(valid_mine),
        ]
    )

    def sum_bit(values, bit):
        rows = jnp.broadcast_to(values[:, None], (values.shape[0], LANES))
        return values + swap(rows, "fsdp", bit)[:, 0]

    if paired():
        mine = mine + swap(away, "fsdp", 1).astype(F32)
        down_rows = after(down_rows, mine)
        kept, sent = halves(down_rows[:, :hidden])
        down_rows = jnp.concatenate(by_core(kept, swap(sent, "fsdp", 1)), axis=0).T
        rows = mine.shape[0] // (fsdp_size // 2)
        terms = in_three(sum_bit(stats, 1))
        extra = jnp.pad(terms, ((0, 16 - 3), (0, mine.shape[1] - 4)))
        came = [
            swap(jnp.concatenate([mine[k * rows : (k + 1) * rows].astype(BF), extra]), "fsdp", 2 * k)
            for k in range(1, fsdp_size // 2)
        ]
        ga_came = exchange_seq(ga_parts)
        came, ga_came = after((came, ga_came), down_rows, out_rows, *in_all)
        last = mine[:rows]
        for block in came:
            last = last + block[:rows].astype(F32)
        stats = tree_sum([from_three(terms)] + [from_three(block[rows : rows + 3, :4]) for block in came])
    else:
        last = lax.psum_scatter(mine, "fsdp", scatter_dimension=0, tiled=True)
        ga_came = exchange_seq(ga_parts)
        bit = 1
        while bit < fsdp_size:
            stats = sum_bit(stats, bit)
            bit *= 2
    extra = jnp.pad(in_three(stats), ((0, last.shape[0] - 3), (0, LANES - 4)))
    last = jnp.concatenate([last.astype(BF), out_rows, extra], axis=1)
    ga_came, in_all = after((ga_came, in_all), last)

    grad_in_weight, grad_gain_two = finish_rows(
        functools.partial(in_rows_kernel, seq_size, hidden), in_all, w_in_proj, mlp_gain, seq, (2 * FF, 1), "in_rows"
    )
    if paired():
        grad_down = jnp.concatenate(in_order(share_seq(down_rows)), axis=1).astype(F32)
    else:
        down = lax.all_gather(down_rows[:, :hidden], ("seq", "fsdp"), axis=0, tiled=True)
        down = down.reshape(seq_size, D, hidden).transpose(0, 2, 1).reshape(FF, D)
        rows = FF // fsdp_size
        grad_down = lax.dynamic_slice_in_dim(down, fsdp * rows, rows, axis=0).astype(F32)

    grad_normed = sum_blocks(ga_came)
    grad_inputs = grad_middle + norm_back(grad_normed, gain_one, x)
    last = after(share_seq(last), grad_in_weight, grad_down, grad_inputs)
    grad_qkv_weight, grad_out_weight, grad_gain_one = finish_rows(
        functools.partial(last_rows_kernel, seq_size), last, w_qkv, attn_gain, seq, (3 * D, D, 1), "last_rows"
    )

    stats = tree_sum([from_three(rows[:3, -LANES : 4 - LANES]) for rows in last])
    root_means = jnp.sqrt(stats[:3] / (jnp.maximum(stats[3], 1.0) * D))

    return (
        result.astype(BF)[None],
        grad_inputs[None],
        grad_qkv_weight,
        grad_out_weight,
        grad_in_weight,
        grad_down,
        grad_gain_one[:, 0],
        grad_gain_two[:, 0],
        root_means,
    )


def solution(mesh):
    in_specs = (
        P("fsdp", "seq", None),
        P("fsdp", None),
        P("fsdp", None),
        P("fsdp", None),
        P("fsdp", None),
        P("fsdp", None),
        P("fsdp", None),
        P("fsdp"),
        P("fsdp"),
        P("fsdp", "seq", None),
    )
    out_specs = (
        P("fsdp", "seq", None),
        P("fsdp", "seq", None),
        P("fsdp", None),
        P("fsdp", None),
        P("fsdp", None),
        P("fsdp", None),
        P("fsdp"),
        P("fsdp"),
        P(),
    )
    return jax.shard_map(on_device, mesh=mesh, in_specs=in_specs, out_specs=out_specs, check_vma=False)
```

```python
import functools

import jax
import jax.numpy as jnp
from jax import lax
from jax.experimental import pallas as pl
from jax.experimental.pallas import tpu as pltpu
from jax.sharding import PartitionSpec as P

D = 1024
HEADS = 16
HD = 64
FF = 2624

ROPE_BASE = 160000.0
NORM_EPS = 1e-05
LANES = 128
BF = jnp.bfloat16
F32 = jnp.float32


def swap(x, axis, bit):
    return lax.ppermute(x, axis, [(i, i ^ bit) for i in range(lax.axis_size(axis))])


def after(x, *others):
    return lax.optimization_barrier((x, others))[0]


def share_seq(block):
    return [block] + [swap(block, "seq", k) for k in range(1, lax.axis_size("seq"))]


def relay_first(block):
    return swap(block, "seq", 1), swap(block, "seq", 2)


def relay_last(block, one, two):
    if lax.axis_size("seq") != 4:
        return share_seq(block)
    half = block.shape[0] // 2
    upper, lower = swap(two[:half], "seq", 1), swap(one[half:], "seq", 2)
    return [block, one, two, jnp.concatenate([upper, lower], axis=0)]


def exchange_seq(blocks):
    return lax.all_to_all(blocks, "seq", split_axis=0, concat_axis=0, tiled=True)


def sum_blocks(blocks):
    rows = blocks.shape[0] // lax.axis_size("seq")
    total = blocks[:rows].astype(F32)
    for i in range(1, lax.axis_size("seq")):
        total = total + blocks[i * rows : (i + 1) * rows].astype(F32)
    return total


def paired():
    return lax.axis_size("fsdp") == 2 * lax.axis_size("seq")


def gather_rows(block):
    return lax.all_gather(block, "fsdp", axis=0, tiled=True)


def transpose_devices(x):
    seq, fsdp = lax.axis_size("seq"), lax.axis_size("fsdp")
    pairs = [
        (s * fsdp + 2 * z + c, z * fsdp + 2 * s + c)
        for s in range(seq)
        for z in range(fsdp // 2)
        for c in range(2)
    ]
    return lax.ppermute(x, ("seq", "fsdp"), pairs)


def tree_sum(values):
    while len(values) > 1:
        values = [values[i] + values[i + 1] for i in range(0, len(values), 2)]
    return values[0]


def in_three(values):
    terms = []
    for _ in range(3):
        terms.append(lax.reduce_precision(values, 8, 7))
        values = values - terms[-1]
    return jnp.stack(terms).astype(BF)


def from_three(terms):
    terms = terms.astype(F32)
    return (terms[0] + terms[1]) + terms[2]


def half_swap(values):
    width = values.shape[1]
    lane = lax.broadcasted_iota(jnp.int32, values.shape, 1)
    ahead = pltpu.roll(values, width - HD // 2, 1)
    behind = pltpu.roll(values, HD // 2, 1)
    return jnp.where(lane % HD < HD // 2, ahead, behind)


def wide(table, width):
    return jnp.concatenate([table] * (width // table.shape[1]), axis=1)


def qkv_kernel(*refs):
    count = 4
    xs = refs[:count]
    w_ref, gain_ref, cos_ref, sin_ref, a_ref, q_ref, k_ref, v_ref, held = refs[count:]
    step = pl.program_id(0)
    for i in range(count):

        @pl.when(step == i)
        def _():
            held[...] = xs[i][...].astype(F32)

    values = held[...]
    centered = values - jnp.mean(values, axis=1, keepdims=True)
    variance = jnp.mean(centered * centered, axis=1, keepdims=True)
    low = (centered * lax.rsqrt(variance + NORM_EPS) * gain_ref[...]).astype(BF)
    a_ref[...] = low
    p = jnp.dot(low, w_ref[...], preferred_element_type=F32)
    part = p.shape[1] // 3
    turned = p[:, : 2 * part]
    turned = turned * wide(cos_ref[...], 2 * part) + half_swap(turned) * wide(sin_ref[...], 2 * part)
    q_ref[...] = turned[:, :part].astype(BF) * (HD**-0.5)
    k_ref[...] = turned[:, part:].astype(BF)
    v_ref[...] = p[:, 2 * part :].astype(BF)


def project_qkv(blocks, weight, gain, cosine, sine):
    rows, width = blocks[0].shape
    part = (weight.shape[1] - LANES) // 4
    count = len(blocks)
    whole = lambda a: pl.BlockSpec(a.shape, lambda i: (0, 0))
    tile = lambda n: pl.BlockSpec((rows, n), lambda i: (i, 0))
    shape = lambda n: jax.ShapeDtypeStruct((rows * count, n), BF)
    return pl.pallas_call(
        qkv_kernel,
        grid=(count,),
        in_specs=[whole(b) for b in blocks]
        + [pl.BlockSpec((width, 3 * part), lambda i: (0, 0)), whole(gain), tile(cosine.shape[1]), tile(sine.shape[1])],
        out_specs=[tile(width), tile(part), tile(part), tile(part)],
        out_shape=[shape(width), shape(part), shape(part), shape(part)],
        scratch_shapes=[pltpu.VMEM((rows, width), F32)],
        cost_estimate=pl.CostEstimate(
            flops=2 * rows * count * width * 3 * part,
            bytes_accessed=2 * rows * count * (2 * width + 3 * part) + 2 * width * 3 * part,
            transcendentals=0,
        ),
        name="qkv",
    )(*blocks, weight, gain, cosine, sine)


def mask_bias(seg_col, valid_col, seg_row, first_row):
    shape = (seg_col.shape[0], seg_row.shape[1])
    key = lax.broadcasted_iota(jnp.int32, shape, 0)
    query = lax.broadcasted_iota(jnp.int32, shape, 1) + first_row
    allowed = (seg_col == seg_row) & ((valid_col > 0) | (key == query))
    return jnp.where(allowed, 0.0, -1e30)


def forward_kernel(q_ref, k_ref, v_ref, segc_ref, valc_ref, segr_ref, o_ref, lse_ref, vt_ref, ot_ref, bias_ref):
    step = pl.program_id(0)
    rows, width = q_ref.shape

    @pl.when(step == 0)
    def _():
        vt_ref[...] = v_ref[...].T

    bias_ref[...] = mask_bias(segc_ref[...], valc_ref[...], segr_ref[...], step * rows)
    qt = q_ref[...].T
    feature = lax.broadcasted_iota(jnp.int32, qt.shape, 0) // HD

    def head(h, carry):
        mine = jnp.where(feature == h, qt, jnp.zeros_like(qt))
        scores = jnp.dot(k_ref[...], mine, preferred_element_type=F32) + bias_ref[...]
        top = jnp.max(scores, axis=0, keepdims=True)
        exponent = jnp.exp(scores - top)
        total = jnp.sum(exponent, axis=0, keepdims=True)
        weights = (exponent * (1.0 / total)).astype(BF)
        start = pl.multiple_of(h * HD, HD)
        ot_ref[pl.ds(start, HD), :] = jnp.dot(
            vt_ref[pl.ds(start, HD), :], weights, preferred_element_type=F32
        )
        lse_ref[pl.ds(h, 1), :] = top + jnp.log(total)
        return carry

    lax.fori_loop(0, width // HD, head, 0)
    o_ref[...] = ot_ref[...].T.astype(BF)


def attend_forward(q, k, v, seg_col, valid_col, seg_row, rows):
    length, width = q.shape
    whole = lambda a: pl.BlockSpec(a.shape, lambda i: (0, 0))
    tile = pl.BlockSpec((rows, width), lambda i: (i, 0))
    return pl.pallas_call(
        forward_kernel,
        grid=(length // rows,),
        in_specs=[tile, whole(k), whole(v), whole(seg_col), whole(valid_col), pl.BlockSpec((1, rows), lambda i: (0, i))],
        out_specs=[tile, pl.BlockSpec((8, rows), lambda i: (0, i))],
        out_shape=[jax.ShapeDtypeStruct((length, width), BF), jax.ShapeDtypeStruct((8, length), F32)],
        scratch_shapes=[pltpu.VMEM((width, length), BF), pltpu.VMEM((width, rows), F32), pltpu.VMEM((length, rows), F32)],
        cost_estimate=pl.CostEstimate(
            flops=4 * length * length * width, bytes_accessed=8 * length * width, transcendentals=length * length * 4
        ),
        name="attend",
    )(q, k, v, seg_col, valid_col, seg_row)


def backward_kernel(
    q_ref, go_ref, lse_ref, k_ref, v_ref, segc_ref, valc_ref, segr_ref, cos_ref, sin_ref,
    gp_ref, kt_ref, dk_ref, dv_ref, dqt_ref, bias_ref,
):
    step = pl.program_id(0)
    rows, width = q_ref.shape

    @pl.when(step == 0)
    def _():
        kt_ref[...] = k_ref[...].T
        dk_ref[...] = jnp.zeros_like(dk_ref)
        dv_ref[...] = jnp.zeros_like(dv_ref)

    bias_ref[...] = mask_bias(segc_ref[...], valc_ref[...], segr_ref[...], step * rows)
    qt, got = q_ref[...].T, go_ref[...].T
    feature = lax.broadcasted_iota(jnp.int32, qt.shape, 0) // HD
    lane = lax.broadcasted_iota(jnp.int32, (rows, width), 1) // HD
    none = jnp.zeros_like(qt)
    none_row = jnp.zeros((rows, width), BF)

    def head(h, carry):
        scores = jnp.dot(k_ref[...], jnp.where(feature == h, qt, none), preferred_element_type=F32)
        weights = jnp.exp(scores + bias_ref[...] - lse_ref[pl.ds(h, 1), :])
        upstream = jnp.dot(v_ref[...], jnp.where(feature == h, got, none), preferred_element_type=F32)
        inner = jnp.sum(weights * upstream, axis=0, keepdims=True)
        low = (weights * (upstream - inner)).astype(BF)
        dv_ref[...] += jnp.dot(
            weights.astype(BF), jnp.where(lane == h, go_ref[...], none_row), preferred_element_type=F32
        )
        dk_ref[...] += jnp.dot(low, jnp.where(lane == h, q_ref[...], none_row), preferred_element_type=F32)
        start = pl.multiple_of(h * HD, HD)
        dqt_ref[pl.ds(start, HD), :] = jnp.dot(kt_ref[pl.ds(start, HD), :], low, preferred_element_type=F32)
        return carry

    lax.fori_loop(0, width // HD, head, 0)

    def unturn(values, cosine, sine):
        values = values.astype(BF).astype(F32)
        return (values * wide(cosine, width) - half_swap(values) * wide(sine, width)).astype(BF)

    here = pl.ds(pl.multiple_of(step * rows, rows), rows)
    gp_ref[here, :width] = unturn(dqt_ref[...].T * (HD**-0.5), cos_ref[here, :], sin_ref[here, :])

    @pl.when(step == pl.num_programs(0) - 1)
    def _():
        gp_ref[:, width : 2 * width] = unturn(dk_ref[...], cos_ref[...], sin_ref[...])
        gp_ref[:, 2 * width :] = dv_ref[...].astype(BF)


def attend_backward(q, k, v, grad_out, lse, seg_col, valid_col, seg_row, cosine, sine, rows):
    length, width = q.shape
    whole = lambda a: pl.BlockSpec(a.shape, lambda i: (0, 0))
    tile = pl.BlockSpec((rows, width), lambda i: (i, 0))
    return pl.pallas_call(
        backward_kernel,
        grid=(length // rows,),
        in_specs=[
            tile, tile, pl.BlockSpec((8, rows), lambda i: (0, i)), whole(k), whole(v),
            whole(seg_col), whole(valid_col), pl.BlockSpec((1, rows), lambda i: (0, i)), whole(cosine), whole(sine),
        ],
        out_specs=pl.BlockSpec((length, 3 * width), lambda i: (0, 0)),
        out_shape=jax.ShapeDtypeStruct((length, 3 * width), BF),
        scratch_shapes=[
            pltpu.VMEM((width, length), BF), pltpu.VMEM((length, width), F32), pltpu.VMEM((length, width), F32),
            pltpu.VMEM((width, rows), F32), pltpu.VMEM((length, rows), F32),
        ],
        cost_estimate=pl.CostEstimate(
            flops=10 * length * length * width, bytes_accessed=20 * length * width, transcendentals=length * length * 4
        ),
        name="attend_back",
    )(q, grad_out, lse, k, v, seg_col, valid_col, seg_row, cosine, sine)


def erf(x):
    x = jnp.clip(x, -3.832506856900711, 3.832506856900711)
    square = x * x
    top = 0.00022905065861350646
    for c in (0.0034082910107109506, 0.050955695062380861, 0.18520832239976145, 1.128379143519084):
        top = top * square + c
    low = -1.1791602954361697e-7
    for c in (0.000023547966471313185, 0.0010179625278914885, 0.014070470171167667, 0.11098505178285362, 0.49746925110067538, 1.0):
        low = low * square + c
    return x * top / low


def nt(a, b):
    return lax.dot_general(a, b, (((1,), (1,)), ((), ())), preferred_element_type=F32)


def feed_kernel(hidden, me_ref, b_ref, g_ref, w_ref, *refs):
    m_ref, gi_ref, gg_ref, gb_ref, mlp_ref = refs[-5:]
    b = b_ref[...]
    slot = w_ref.shape[1] // 3
    wi_ref, wg_ref, wd_ref = (w_ref.at[:, i * slot : i * slot + hidden] for i in range(3))
    inner = jnp.dot(b, wi_ref[...], preferred_element_type=F32)
    gate = jnp.dot(b, wg_ref[...], preferred_element_type=F32)
    upstream = jnp.dot(g_ref[...], wd_ref[...], preferred_element_type=F32)
    half = 0.5 * (1.0 + erf(inner * 0.7071067811865476))
    gelu = inner * half
    slope = half + inner * jnp.exp(-0.5 * inner * inner) * 0.3989422804014327
    m = (gelu * gate).astype(BF)
    gi = (upstream * gate * slope).astype(BF)
    gg = (upstream * gelu).astype(BF)
    m_ref[...] = m
    gi_ref[...] = gi
    gg_ref[...] = gg
    gb_ref[...] = (nt(gi, wi_ref[...]) + nt(gg, wg_ref[...])).astype(gb_ref.dtype)
    mlp_ref[...] = nt(m, wd_ref[...]).astype(mlp_ref.dtype)


def feed_forward(b, g, w, hidden, me, place, count, dtype, onto):
    rows, width = b.shape
    whole = lambda r, n: pl.BlockSpec((r, n), lambda i, me: (0, 0))
    narrow = jax.ShapeDtypeStruct((rows, hidden), BF)
    operands, specs = [b, g, w], [whole(rows, width), whole(rows, width), whole(*w.shape)]
    if onto is not None:
        operands.append(onto)
        specs.append(pl.BlockSpec(memory_space=pl.ANY))
    return pl.pallas_call(
        functools.partial(feed_kernel, hidden),
        grid_spec=pltpu.PrefetchScalarGridSpec(
            num_scalar_prefetch=1,
            grid=(1,),
            in_specs=specs,
            out_specs=[whole(rows, hidden)] * 3
            + [whole(rows, width), pl.BlockSpec((rows, width), lambda i, me: (me[0] ^ place, 0))],
        ),
        out_shape=[narrow] * 3
        + [jax.ShapeDtypeStruct((rows, width), dtype), jax.ShapeDtypeStruct((rows * count, width), BF)],
        input_output_aliases={} if onto is None else {4: 4},
        cost_estimate=pl.CostEstimate(
            flops=12 * rows * width * hidden,
            bytes_accessed=6 * width * hidden + 8 * rows * width + 6 * rows * hidden,
            transcendentals=rows * hidden,
        ),
        name="feed",
    )(me[None], *operands)


def tn(a, b):
    return lax.dot_general(a, b, (((0,), (0,)), ((), ())), preferred_element_type=F32)


def weight_kernel(count, slot, pairs, *refs):
    out_ref = refs[-1]
    hidden = refs[(pairs[0][1]) * count].shape[1]
    for place, (left, right) in enumerate(pairs):
        total = None
        for i in range(count):
            term = tn(refs[left * count + i][...], refs[right * count + i][...])
            total = term if total is None else total + term
        out_ref[:, place * slot : place * slot + hidden] = total.astype(BF)
        if hidden < slot:
            out_ref[:, place * slot + hidden : (place + 1) * slot] = jnp.zeros((out_ref.shape[0], slot - hidden), BF)


def weight_gradients(lefts, rights, pairs, slots, place, onto=None):
    count = len(lefts[0])
    rows, width = lefts[0][0].shape
    hidden = rights[0][0].shape[1]
    slot = -(-hidden // LANES) * LANES
    wide_spec = pl.BlockSpec((rows, 256), lambda i: (0, i))
    whole = pl.BlockSpec((rows, hidden), lambda i: (0, 0))
    operands = [b for group in lefts for b in group] + [b for group in rights for b in group]
    specs = [wide_spec] * (len(lefts) * count) + [whole] * (len(rights) * count)
    aliases = {}
    if onto is not None:
        aliases = {len(operands): 0}
        operands.append(onto)
        specs.append(pl.BlockSpec(memory_space=pl.ANY))
    return pl.pallas_call(
        functools.partial(weight_kernel, count, slot, pairs),
        grid=(width // 256,),
        in_specs=specs,
        out_specs=pl.BlockSpec((256, len(pairs) * slot), lambda i: (i, place // len(pairs))),
        out_shape=jax.ShapeDtypeStruct((width, slots * slot), BF),
        input_output_aliases=aliases,
        cost_estimate=pl.CostEstimate(
            flops=2 * len(pairs) * rows * count * width * hidden,
            bytes_accessed=2 * count * rows * (len(lefts) * width + len(rights) * hidden),
            transcendentals=0,
        ),
        name="weight_gradients",
    )(*operands)


def last_kernel(me_ref, a_ref, gp_ref, mine_ref, away_ref):
    total = tn(a_ref[...], gp_ref[...])

    @pl.when(pl.program_id(0) % 2 == 0)
    def _():
        mine_ref[...] = total

    @pl.when(pl.program_id(0) % 2 == 1)
    def _():
        away_ref[...] = total.astype(BF)


def last_gradients(a, gp, me, size):
    length, width = a.shape
    rows, columns = width // size, gp.shape[1]
    out = lambda dtype: jax.ShapeDtypeStruct((width // 2, columns), dtype)
    return pl.pallas_call(
        last_kernel,
        grid_spec=pltpu.PrefetchScalarGridSpec(
            num_scalar_prefetch=1,
            grid=(size,),
            in_specs=[
                pl.BlockSpec((length, rows), lambda i, me: (0, me[0] ^ i)),
                pl.BlockSpec((length, columns), lambda i, me: (0, 0)),
            ],
            out_specs=[pl.BlockSpec((rows, columns), lambda i, me: (i // 2, 0))] * 2,
        ),
        out_shape=[out(F32), out(BF)],
        cost_estimate=pl.CostEstimate(
            flops=2 * length * width * columns,
            bytes_accessed=2 * length * (width + columns) + 3 * width * columns,
            transcendentals=0,
        ),
        name="last_gradients",
    )(me[None], a, gp)


def qkv_back_kernel(me_ref, gp_ref, w_ref, out_ref):
    out_ref[...] = nt(gp_ref[...], w_ref[...]).astype(BF)


def project_back(gp, weight, me, count):
    rows, width = gp.shape[0] // count, weight.shape[0]
    return pl.pallas_call(
        qkv_back_kernel,
        grid_spec=pltpu.PrefetchScalarGridSpec(
            num_scalar_prefetch=1,
            grid=(count,),
            in_specs=[
                pl.BlockSpec((rows, gp.shape[1]), lambda i, me: (i, 0)),
                pl.BlockSpec((width, gp.shape[1]), lambda i, me: (0, 0)),
            ],
            out_specs=pl.BlockSpec((rows, width), lambda i, me: (me[0] ^ i, 0)),
        ),
        out_shape=jax.ShapeDtypeStruct((rows * count, width), BF),
        cost_estimate=pl.CostEstimate(
            flops=2 * rows * count * width * gp.shape[1],
            bytes_accessed=2 * (rows * count * (width + gp.shape[1]) + width * gp.shape[1]),
            transcendentals=0,
        ),
        name="project_back",
    )(me[None], gp, weight)


def ordered(refs, me, piece):
    values = [ref[piece] for ref in refs]
    bit = 1
    while bit < len(values):
        flip = (me & bit) != 0
        values = [jnp.where(flip, values[k ^ bit], values[k]) for k in range(len(values))]
        bit *= 2
    return values


def gain_part(w_ref, grad_ref, gain_ref, out_ref):
    total = jnp.sum(w_ref[...].astype(F32) * grad_ref[...], axis=1, keepdims=True)
    total = jnp.broadcast_to(total, (total.shape[0], LANES)).T
    out_ref[...] = total[:1] / gain_ref[...].astype(F32)


def last_rows_kernel(count, me_ref, *refs):
    blocks, (w_ref, gain_ref, qkv_ref, out_ref, gg_ref) = refs[:count], refs[count:]
    part = (blocks[0].shape[1] - LANES) // (3 + count)
    piece = lambda i: (slice(None), slice(i * part, (i + 1) * part))
    for i in range(3):
        for j, value in enumerate(ordered(blocks, me_ref[0], piece(i))):
            first = (i * count + j) * part
            qkv_ref[:, first : first + part] = value.astype(F32)
    for j in range(count):
        total = None
        for value in ordered(blocks, me_ref[0], piece(3 + j)):
            total = value.astype(F32) if total is None else total + value.astype(F32)
        out_ref[:, j * part : (j + 1) * part] = total
    gain_part(w_ref, qkv_ref, gain_ref, gg_ref)


def in_rows_kernel(count, hidden, me_ref, *refs):
    blocks, (w_ref, gain_ref, in_ref, gg_ref) = refs[:count], refs[count:]
    slot = blocks[0].shape[1] // 2
    for i in range(2):
        piece = (slice(None), slice(i * slot, i * slot + hidden))
        values = [value.astype(F32) for value in ordered(blocks, me_ref[0], piece)]
        in_ref[:, i * count * hidden : (i + 1) * count * hidden] = jnp.concatenate(values, axis=1)
    gain_part(w_ref, in_ref, gain_ref, gg_ref)


def finish_rows(kernel, blocks, weight, gain, me, widths, name):
    rows = weight.shape[0]
    shapes = [jax.ShapeDtypeStruct((rows, n), F32) for n in widths] + [jax.ShapeDtypeStruct((1, rows), F32)]
    return pl.pallas_call(
        kernel,
        in_specs=[pl.BlockSpec(memory_space=pltpu.SMEM)] + [pl.BlockSpec(memory_space=pltpu.VMEM)] * (len(blocks) + 2),
        out_shape=shapes,
        cost_estimate=pl.CostEstimate(flops=0, bytes_accessed=8 * rows * sum(widths), transcendentals=0),
        name=name,
    )(me[None], *blocks, weight, gain[None])


def normal(values):
    centered = values - jnp.mean(values, axis=-1, keepdims=True)
    scale = lax.rsqrt(jnp.mean(centered * centered, axis=-1, keepdims=True) + NORM_EPS)
    return centered * scale, scale


def norm_back(upstream, gain, values):
    unit, scale = normal(values)
    weighted = upstream * gain
    return scale * (
        weighted
        - jnp.mean(weighted, axis=-1, keepdims=True)
        - unit * jnp.mean(weighted * unit, axis=-1, keepdims=True)
    )


def matmul(a, b):
    return jnp.dot(a, b, preferred_element_type=F32)


def matmul_nt(a, b):
    return lax.dot_general(a, b, (((1,), (1,)), ((), ())), preferred_element_type=F32)


def matmul_tn(a, b):
    return lax.dot_general(a, b, (((0,), (0,)), ((), ())), preferred_element_type=F32)


def on_device(
    hidden_in, segment_ids, valid_tokens, w_qkv, w_attn_out, w_in_proj, w_out_proj, attn_gain, mlp_gain, cotangent
):
    seq_size, fsdp_size = lax.axis_size("seq"), lax.axis_size("fsdp")
    seq, fsdp = lax.axis_index("seq"), lax.axis_index("fsdp")
    x_low, cot = hidden_in[0], cotangent[0]
    tokens = x_low.shape[0]
    length = tokens * seq_size
    part = D // seq_size
    hidden = FF // seq_size
    rel = [seq ^ k for k in range(seq_size)]

    def by_block(row):
        return jnp.concatenate([lax.dynamic_slice_in_dim(row, r * tokens, tokens) for r in rel])

    seg_all, valid_all = by_block(segment_ids[0]), by_block(valid_tokens[0])
    positions = by_block(jnp.arange(length, dtype=jnp.int32))
    frequency = ROPE_BASE ** (-2.0 * jnp.arange(HD // 2, dtype=F32) / HD)
    angles = positions.astype(F32)[:, None] * frequency[None, :]
    cosine, sine = lax.optimization_barrier((jnp.cos(angles), jnp.sin(angles)))
    cosine = jnp.concatenate([cosine] * 4, axis=1)
    sine = jnp.concatenate([-sine, sine] * 2, axis=1)
    seg_col, valid_col, seg_row = seg_all[:, None], valid_all[:, None], seg_all[None, :]

    first_mine = [lax.dynamic_slice_in_dim(w_qkv, i * D + seq * part, part, axis=1) for i in range(3)]
    first_mine.append(lax.dynamic_slice_in_dim(w_attn_out, seq * part, part, axis=1))
    gains = jnp.stack([attn_gain, mlp_gain], axis=1)
    first_mine.append(jnp.pad(gains, ((0, 0), (0, LANES - 2))))
    first_mine = jnp.concatenate(first_mine, axis=1)
    first_weight = gather_rows(first_mine)
    core = fsdp % 2
    slot = -(-hidden // LANES) * LANES
    if paired():
        down_mine = transpose_devices(lax.dynamic_slice_in_dim(w_out_proj, seq * part, part, axis=1))
    x_near = relay_first(x_low)
    out_mine = first_weight[:, 3 * part : 4 * part]
    gains = first_weight[:, 4 * part :].T.astype(F32)
    gain_one, gain_two = gains[0:1], gains[1:2]
    core = fsdp % 2
    slot = -(-hidden // LANES) * LANES
    def padded(rows):
        return jnp.pad(rows, ((0, 0), (0, slot - hidden)))

    def halves(rows):
        half = rows.shape[1] // 2
        low, high = rows[:, :half], rows[:, half:]
        return jnp.where(core == 0, low, high), jnp.where(core == 0, high, low)

    def by_core(mine, other):
        return jnp.where(core == 0, mine, other), jnp.where(core == 0, other, mine)

    in_mine = [
        padded(lax.dynamic_slice_in_dim(w_in_proj, i * FF + seq * hidden, hidden, axis=1)) for i in range(2)
    ]
    if paired():
        x_blocks = relay_last(x_low, *x_near)
        kept, sent = halves(after(down_mine, x_blocks, cosine, sine, seg_col, valid_col))
        down_mine = jnp.concatenate(by_core(kept, swap(sent, "fsdp", 1)), axis=0)
        feed_weight = gather_rows(jnp.concatenate(in_mine + [padded(down_mine.T)], axis=1))
    else:
        down_weight = lax.all_gather(w_out_proj, "fsdp", axis=0, tiled=True)
        down_weight = lax.dynamic_slice_in_dim(down_weight, seq * hidden, hidden, axis=0)
        feed_weight = jnp.concatenate([gather_rows(jnp.concatenate(in_mine, axis=1)), padded(down_weight.T)], axis=1)
        x_blocks = relay_last(x_low, *x_near)
    cot_near = relay_first(after(cot, *x_blocks))

    def in_order(blocks):
        bit = 1
        while bit < seq_size:
            flip = (seq & bit) != 0
            blocks = [jnp.where(flip, blocks[k ^ bit], blocks[k]) for k in range(seq_size)]
            bit *= 2
        return blocks


    a_low, q, k, v = project_qkv(x_blocks, first_weight, gain_one, cosine, sine)
    k, cot_near = after((k, cot_near), q)
    cot_blocks = relay_last(cot, *cot_near)
    mixed, lse = attend_forward(q, k, v, seg_col, valid_col, seg_row, tokens)

    out_near = relay_first(out_mine)
    mixed, out_near, cot_blocks = after((mixed, out_near, cot_blocks))
    out_weight = jnp.concatenate(in_order(relay_last(out_mine, *out_near)), axis=1)

    def to_tokens(blocks):
        came = [blocks[:tokens]] + [
            swap(blocks[i * tokens : (i + 1) * tokens], "seq", i) for i in range(1, seq_size)
        ]
        return jnp.concatenate(in_order(came), axis=1)

    mixed_low = to_tokens(mixed)
    x = x_low.astype(F32)
    attn_branch = matmul(mixed_low, out_weight)
    middle = x + attn_branch
    normed_two = (normal(middle)[0] * gain_two).astype(BF)
    normed_two = after(normed_two, *cot_blocks)

    b_blocks = share_seq(normed_two)
    fed, came, mlp_all = [None] * seq_size, [], None
    for i in range(seq_size):
        b = after(b_blocks[i], *came[:-1]) if len(came) > 1 else b_blocks[i]
        fed[i] = feed_forward(
            b, cot_blocks[i], feed_weight, hidden, seq, i, seq_size, F32 if i == 0 else BF, mlp_all
        )
        mlp_all = fed[i][4]
        if i > 0:
            came.append(swap(fed[i][3], "seq", i))
    m_blocks, gz_i, gz_g, gb_blocks, _ = zip(*fed)
    fed_grads = weight_gradients([after(b_blocks, *came[:-2])], [gz_i, gz_g], ((0, 1), (0, 2)), 3, 0)
    fed_grads = weight_gradients([after(cot_blocks, *came)], [m_blocks], ((0, 1),), 3, 2, fed_grads)
    grad_normed_two = gb_blocks[0]
    for block in came:
        grad_normed_two = grad_normed_two + block.astype(F32)
    grad_middle = cot.astype(F32) + norm_back(grad_normed_two, gain_two, middle)
    grad_attn_low = grad_middle.astype(BF)
    grad_mixed = matmul_nt(grad_attn_low, out_weight).astype(BF)

    sent = [lax.dynamic_slice_in_dim(grad_mixed, r * part, part, axis=1) for r in rel]
    came = [sent[0]] + [swap(sent[i], "seq", i) for i in range(1, seq_size)]
    grad_by_heads = jnp.concatenate(came, axis=0)
    out_part = matmul_tn(mixed_low, after(grad_attn_low, grad_by_heads)).astype(BF)
    grad_by_heads = after(grad_by_heads, out_part)
    mlp_came = exchange_seq(after(mlp_all, grad_by_heads))

    def own_rows(partial):
        return lax.psum_scatter(partial, "fsdp", scatter_dimension=0, tiled=True)

    fed_rows = own_rows(fed_grads)
    out_rows = own_rows(out_part)

    gp = attend_backward(
        q, k, v, grad_by_heads, lse, seg_col, valid_col, seg_row, cosine, sine, tokens
    )
    fed_late = after(fed_rows, gp)
    in_rows, down_rows = fed_late[:, : 2 * slot], fed_late[:, 2 * slot :]
    in_all = share_seq(in_rows)
    if paired():
        down_rows = transpose_devices(down_rows)
        ga_parts = project_back(gp, first_weight, seq, seq_size)
        gp_late = after(gp, ga_parts, *in_all[1:])
        ga_parts, down_rows = after((ga_parts, down_rows))
        mine, away = last_gradients(a_low, gp_late, fsdp, fsdp_size)
    else:
        mine, ga_parts = matmul_tn(a_low, gp), project_back(gp, first_weight, seq, seq_size)
        away = mine
    mlp_branch = sum_blocks(after(mlp_came, away))
    result = middle + mlp_branch
    valid_mine = valid_all[:tokens].astype(F32)[:, None]
    stats = jnp.stack(
        [
            jnp.sum(valid_mine * result * result),
            jnp.sum(valid_mine * attn_branch * attn_branch),
            jnp.sum(valid_mine * mlp_branch * mlp_branch),
            jnp.sum(valid_mine),
        ]
    )

    def sum_bit(values, bit):
        rows = jnp.broadcast_to(values[:, None], (values.shape[0], LANES))
        return values + swap(rows, "fsdp", bit)[:, 0]

    if paired():
        mine = mine + swap(away, "fsdp", 1).astype(F32)
        down_rows = after(down_rows, mine)
        kept, sent = halves(down_rows[:, :hidden])
        down_rows = jnp.concatenate(by_core(kept, swap(sent, "fsdp", 1)), axis=0).T
        rows = mine.shape[0] // (fsdp_size // 2)
        terms = in_three(sum_bit(stats, 1))
        extra = jnp.pad(terms, ((0, 16 - 3), (0, mine.shape[1] - 4)))
        came = [
            swap(jnp.concatenate([mine[k * rows : (k + 1) * rows].astype(BF), extra]), "fsdp", 2 * k)
            for k in range(1, fsdp_size // 2)
        ]
        ga_came = exchange_seq(ga_parts)
        came, ga_came = after((came, ga_came), down_rows, out_rows)
        last = mine[:rows]
        for block in came:
            last = last + block[:rows].astype(F32)
        stats = tree_sum([from_three(terms)] + [from_three(block[rows : rows + 3, :4]) for block in came])
    else:
        last = lax.psum_scatter(mine, "fsdp", scatter_dimension=0, tiled=True)
        ga_came = exchange_seq(ga_parts)
        bit = 1
        while bit < fsdp_size:
            stats = sum_bit(stats, bit)
            bit *= 2
    extra = jnp.pad(in_three(stats), ((0, last.shape[0] - 3), (0, LANES - 4)))
    last = jnp.concatenate([last.astype(BF), out_rows, extra], axis=1)
    ga_came, in_all, down_rows = after((ga_came, in_all, down_rows), last)

    grad_in_weight, grad_gain_two = finish_rows(
        functools.partial(in_rows_kernel, seq_size, hidden), in_all, w_in_proj, mlp_gain, seq, (2 * FF,), "in_rows"
    )
    if paired():
        grad_down = jnp.concatenate(in_order(share_seq(down_rows)), axis=1).astype(F32)
    else:
        down = lax.all_gather(down_rows[:, :hidden], ("seq", "fsdp"), axis=0, tiled=True)
        down = down.reshape(seq_size, D, hidden).transpose(0, 2, 1).reshape(FF, D)
        rows = FF // fsdp_size
        grad_down = lax.dynamic_slice_in_dim(down, fsdp * rows, rows, axis=0).astype(F32)

    grad_normed = sum_blocks(ga_came)
    grad_inputs = grad_middle + norm_back(grad_normed, gain_one, x)
    last = after(share_seq(last), grad_in_weight, grad_down, grad_inputs)
    grad_qkv_weight, grad_out_weight, grad_gain_one = finish_rows(
        functools.partial(last_rows_kernel, seq_size), last, w_qkv, attn_gain, seq, (3 * D, D), "last_rows"
    )

    stats = tree_sum([from_three(rows[:3, -LANES : 4 - LANES]) for rows in last])
    root_means = jnp.sqrt(stats[:3] / (jnp.maximum(stats[3], 1.0) * D))

    return (
        result.astype(BF)[None],
        grad_inputs[None],
        grad_qkv_weight,
        grad_out_weight,
        grad_in_weight,
        grad_down,
        grad_gain_one[0],
        grad_gain_two[0],
        root_means,
    )


def solution(mesh):
    in_specs = (
        P("fsdp", "seq", None),
        P("fsdp", None),
        P("fsdp", None),
        P("fsdp", None),
        P("fsdp", None),
        P("fsdp", None),
        P("fsdp", None),
        P("fsdp"),
        P("fsdp"),
        P("fsdp", "seq", None),
    )
    out_specs = (
        P("fsdp", "seq", None),
        P("fsdp", "seq", None),
        P("fsdp", None),
        P("fsdp", None),
        P("fsdp", None),
        P("fsdp", None),
        P("fsdp"),
        P("fsdp"),
        P(),
    )
    return jax.shard_map(on_device, mesh=mesh, in_specs=in_specs, out_specs=out_specs, check_vma=False)
```

```python
import functools

import jax
import jax.numpy as jnp
from jax import lax
from jax.experimental import pallas as pl
from jax.experimental.pallas import tpu as pltpu
from jax.sharding import PartitionSpec as P

D = 1024
HEADS = 16
HD = 64
FF = 2624

ROPE_BASE = 160000.0
NORM_EPS = 1e-05
LANES = 128
BF = jnp.bfloat16
F32 = jnp.float32


def swap(x, axis, bit):
    return lax.ppermute(x, axis, [(i, i ^ bit) for i in range(lax.axis_size(axis))])


def after(x, *others):
    return lax.optimization_barrier((x, others))[0]


def share_seq(block):
    return [block] + [swap(block, "seq", k) for k in range(1, lax.axis_size("seq"))]


def relay_first(block):
    return swap(block, "seq", 1), swap(block, "seq", 2)


def relay_last(block, one, two):
    if lax.axis_size("seq") != 4:
        return share_seq(block)
    half = block.shape[0] // 2
    upper, lower = swap(two[:half], "seq", 1), swap(one[half:], "seq", 2)
    return [block, one, two, jnp.concatenate([upper, lower], axis=0)]


def exchange_seq(blocks):
    return lax.all_to_all(blocks, "seq", split_axis=0, concat_axis=0, tiled=True)


def sum_blocks(blocks):
    rows = blocks.shape[0] // lax.axis_size("seq")
    total = blocks[:rows].astype(F32)
    for i in range(1, lax.axis_size("seq")):
        total = total + blocks[i * rows : (i + 1) * rows].astype(F32)
    return total


def paired():
    return lax.axis_size("fsdp") == 2 * lax.axis_size("seq")


def gather_rows(block):
    return lax.all_gather(block, "fsdp", axis=0, tiled=True)


def transpose_devices(x):
    seq, fsdp = lax.axis_size("seq"), lax.axis_size("fsdp")
    pairs = [
        (s * fsdp + 2 * z + c, z * fsdp + 2 * s + c)
        for s in range(seq)
        for z in range(fsdp // 2)
        for c in range(2)
    ]
    return lax.ppermute(x, ("seq", "fsdp"), pairs)


def tree_sum(values):
    while len(values) > 1:
        values = [values[i] + values[i + 1] for i in range(0, len(values), 2)]
    return values[0]


def in_three(values):
    terms = []
    for _ in range(3):
        terms.append(lax.reduce_precision(values, 8, 7))
        values = values - terms[-1]
    return jnp.stack(terms).astype(BF)


def from_three(terms):
    terms = terms.astype(F32)
    return (terms[0] + terms[1]) + terms[2]


def half_swap(values):
    width = values.shape[1]
    lane = lax.broadcasted_iota(jnp.int32, values.shape, 1)
    ahead = pltpu.roll(values, width - HD // 2, 1)
    behind = pltpu.roll(values, HD // 2, 1)
    return jnp.where(lane % HD < HD // 2, ahead, behind)


def wide(table, width):
    return jnp.concatenate([table] * (width // table.shape[1]), axis=1)


def qkv_kernel(*refs):
    count = 4
    xs = refs[:count]
    w_ref, gain_ref, cos_ref, sin_ref, a_ref, q_ref, k_ref, v_ref, held = refs[count:]
    step = pl.program_id(0)
    for i in range(count):

        @pl.when(step == i)
        def _():
            held[...] = xs[i][...].astype(F32)

    values = held[...]
    centered = values - jnp.mean(values, axis=1, keepdims=True)
    variance = jnp.mean(centered * centered, axis=1, keepdims=True)
    low = (centered * lax.rsqrt(variance + NORM_EPS) * gain_ref[...]).astype(BF)
    a_ref[...] = low
    p = jnp.dot(low, w_ref[...], preferred_element_type=F32)
    part = p.shape[1] // 3
    turned = p[:, : 2 * part]
    turned = turned * wide(cos_ref[...], 2 * part) + half_swap(turned) * wide(sin_ref[...], 2 * part)
    q_ref[...] = turned[:, :part].astype(BF) * (HD**-0.5)
    k_ref[...] = turned[:, part:].astype(BF)
    v_ref[...] = p[:, 2 * part :].astype(BF)


def project_qkv(blocks, weight, gain, cosine, sine):
    rows, width = blocks[0].shape
    part = (weight.shape[1] - LANES) // 4
    count = len(blocks)
    whole = lambda a: pl.BlockSpec(a.shape, lambda i: (0, 0))
    tile = lambda n: pl.BlockSpec((rows, n), lambda i: (i, 0))
    shape = lambda n: jax.ShapeDtypeStruct((rows * count, n), BF)
    return pl.pallas_call(
        qkv_kernel,
        grid=(count,),
        in_specs=[whole(b) for b in blocks]
        + [pl.BlockSpec((width, 3 * part), lambda i: (0, 0)), whole(gain), tile(cosine.shape[1]), tile(sine.shape[1])],
        out_specs=[tile(width), tile(part), tile(part), tile(part)],
        out_shape=[shape(width), shape(part), shape(part), shape(part)],
        scratch_shapes=[pltpu.VMEM((rows, width), F32)],
        cost_estimate=pl.CostEstimate(
            flops=2 * rows * count * width * 3 * part,
            bytes_accessed=2 * rows * count * (2 * width + 3 * part) + 2 * width * 3 * part,
            transcendentals=0,
        ),
        name="qkv",
    )(*blocks, weight, gain, cosine, sine)


def mask_bias(seg_col, valid_col, seg_row, first_row):
    shape = (seg_col.shape[0], seg_row.shape[1])
    key = lax.broadcasted_iota(jnp.int32, shape, 0)
    query = lax.broadcasted_iota(jnp.int32, shape, 1) + first_row
    allowed = (seg_col == seg_row) & ((valid_col > 0) | (key == query))
    return jnp.where(allowed, 0.0, -1e30)


def forward_kernel(q_ref, k_ref, v_ref, segc_ref, valc_ref, segr_ref, o_ref, lse_ref, vt_ref, ot_ref, bias_ref):
    step = pl.program_id(0)
    rows, width = q_ref.shape

    @pl.when(step == 0)
    def _():
        vt_ref[...] = v_ref[...].T

    bias_ref[...] = mask_bias(segc_ref[...], valc_ref[...], segr_ref[...], step * rows)
    qt = q_ref[...].T
    feature = lax.broadcasted_iota(jnp.int32, qt.shape, 0) // HD

    def head(h, carry):
        mine = jnp.where(feature == h, qt, jnp.zeros_like(qt))
        scores = jnp.dot(k_ref[...], mine, preferred_element_type=F32) + bias_ref[...]
        top = jnp.max(scores, axis=0, keepdims=True)
        exponent = jnp.exp(scores - top)
        total = jnp.sum(exponent, axis=0, keepdims=True)
        weights = (exponent * (1.0 / total)).astype(BF)
        start = pl.multiple_of(h * HD, HD)
        ot_ref[pl.ds(start, HD), :] = jnp.dot(
            vt_ref[pl.ds(start, HD), :], weights, preferred_element_type=F32
        )
        lse_ref[pl.ds(h, 1), :] = top + jnp.log(total)
        return carry

    lax.fori_loop(0, width // HD, head, 0)
    o_ref[...] = ot_ref[...].T.astype(BF)


def attend_forward(q, k, v, seg_col, valid_col, seg_row, rows):
    length, width = q.shape
    whole = lambda a: pl.BlockSpec(a.shape, lambda i: (0, 0))
    tile = pl.BlockSpec((rows, width), lambda i: (i, 0))
    return pl.pallas_call(
        forward_kernel,
        grid=(length // rows,),
        in_specs=[tile, whole(k), whole(v), whole(seg_col), whole(valid_col), pl.BlockSpec((1, rows), lambda i: (0, i))],
        out_specs=[tile, pl.BlockSpec((8, rows), lambda i: (0, i))],
        out_shape=[jax.ShapeDtypeStruct((length, width), BF), jax.ShapeDtypeStruct((8, length), F32)],
        scratch_shapes=[pltpu.VMEM((width, length), BF), pltpu.VMEM((width, rows), F32), pltpu.VMEM((length, rows), F32)],
        cost_estimate=pl.CostEstimate(
            flops=4 * length * length * width, bytes_accessed=8 * length * width, transcendentals=length * length * 4
        ),
        name="attend",
    )(q, k, v, seg_col, valid_col, seg_row)


def backward_kernel(
    q_ref, go_ref, lse_ref, k_ref, v_ref, segc_ref, valc_ref, segr_ref, cos_ref, sin_ref,
    gp_ref, kt_ref, dk_ref, dv_ref, dqt_ref, bias_ref,
):
    step = pl.program_id(0)
    rows, width = q_ref.shape

    @pl.when(step == 0)
    def _():
        kt_ref[...] = k_ref[...].T
        dk_ref[...] = jnp.zeros_like(dk_ref)
        dv_ref[...] = jnp.zeros_like(dv_ref)

    bias_ref[...] = mask_bias(segc_ref[...], valc_ref[...], segr_ref[...], step * rows)
    qt, got = q_ref[...].T, go_ref[...].T
    feature = lax.broadcasted_iota(jnp.int32, qt.shape, 0) // HD
    lane = lax.broadcasted_iota(jnp.int32, (rows, width), 1) // HD
    none = jnp.zeros_like(qt)
    none_row = jnp.zeros((rows, width), BF)

    def head(h, carry):
        scores = jnp.dot(k_ref[...], jnp.where(feature == h, qt, none), preferred_element_type=F32)
        weights = jnp.exp(scores + bias_ref[...] - lse_ref[pl.ds(h, 1), :])
        upstream = jnp.dot(v_ref[...], jnp.where(feature == h, got, none), preferred_element_type=F32)
        inner = jnp.sum(weights * upstream, axis=0, keepdims=True)
        low = (weights * (upstream - inner)).astype(BF)
        dv_ref[...] += jnp.dot(
            weights.astype(BF), jnp.where(lane == h, go_ref[...], none_row), preferred_element_type=F32
        )
        dk_ref[...] += jnp.dot(low, jnp.where(lane == h, q_ref[...], none_row), preferred_element_type=F32)
        start = pl.multiple_of(h * HD, HD)
        dqt_ref[pl.ds(start, HD), :] = jnp.dot(kt_ref[pl.ds(start, HD), :], low, preferred_element_type=F32)
        return carry

    lax.fori_loop(0, width // HD, head, 0)

    def unturn(values, cosine, sine):
        values = values.astype(BF).astype(F32)
        return (values * wide(cosine, width) - half_swap(values) * wide(sine, width)).astype(BF)

    here = pl.ds(pl.multiple_of(step * rows, rows), rows)
    gp_ref[here, :width] = unturn(dqt_ref[...].T * (HD**-0.5), cos_ref[here, :], sin_ref[here, :])

    @pl.when(step == pl.num_programs(0) - 1)
    def _():
        gp_ref[:, width : 2 * width] = unturn(dk_ref[...], cos_ref[...], sin_ref[...])
        gp_ref[:, 2 * width :] = dv_ref[...].astype(BF)


def attend_backward(q, k, v, grad_out, lse, seg_col, valid_col, seg_row, cosine, sine, rows):
    length, width = q.shape
    whole = lambda a: pl.BlockSpec(a.shape, lambda i: (0, 0))
    tile = pl.BlockSpec((rows, width), lambda i: (i, 0))
    return pl.pallas_call(
        backward_kernel,
        grid=(length // rows,),
        in_specs=[
            tile, tile, pl.BlockSpec((8, rows), lambda i: (0, i)), whole(k), whole(v),
            whole(seg_col), whole(valid_col), pl.BlockSpec((1, rows), lambda i: (0, i)), whole(cosine), whole(sine),
        ],
        out_specs=pl.BlockSpec((length, 3 * width), lambda i: (0, 0)),
        out_shape=jax.ShapeDtypeStruct((length, 3 * width), BF),
        scratch_shapes=[
            pltpu.VMEM((width, length), BF), pltpu.VMEM((length, width), F32), pltpu.VMEM((length, width), F32),
            pltpu.VMEM((width, rows), F32), pltpu.VMEM((length, rows), F32),
        ],
        cost_estimate=pl.CostEstimate(
            flops=10 * length * length * width, bytes_accessed=20 * length * width, transcendentals=length * length * 4
        ),
        name="attend_back",
    )(q, grad_out, lse, k, v, seg_col, valid_col, seg_row, cosine, sine)


def erf(x):
    x = jnp.clip(x, -3.832506856900711, 3.832506856900711)
    square = x * x
    top = 0.00022905065861350646
    for c in (0.0034082910107109506, 0.050955695062380861, 0.18520832239976145, 1.128379143519084):
        top = top * square + c
    low = -1.1791602954361697e-7
    for c in (0.000023547966471313185, 0.0010179625278914885, 0.014070470171167667, 0.11098505178285362, 0.49746925110067538, 1.0):
        low = low * square + c
    return x * top / low


def nt(a, b):
    return lax.dot_general(a, b, (((1,), (1,)), ((), ())), preferred_element_type=F32)


def feed_kernel(hidden, me_ref, b_ref, g_ref, w_ref, *refs):
    m_ref, gi_ref, gg_ref, gb_ref, mlp_ref = refs[-5:]
    b = b_ref[...]
    slot = w_ref.shape[1] // 3
    wi_ref, wg_ref, wd_ref = (w_ref.at[:, i * slot : i * slot + hidden] for i in range(3))
    inner = jnp.dot(b, wi_ref[...], preferred_element_type=F32)
    gate = jnp.dot(b, wg_ref[...], preferred_element_type=F32)
    upstream = jnp.dot(g_ref[...], wd_ref[...], preferred_element_type=F32)
    half = 0.5 * (1.0 + erf(inner * 0.7071067811865476))
    gelu = inner * half
    slope = half + inner * jnp.exp(-0.5 * inner * inner) * 0.3989422804014327
    m = (gelu * gate).astype(BF)
    gi = (upstream * gate * slope).astype(BF)
    gg = (upstream * gelu).astype(BF)
    m_ref[...] = m
    gi_ref[...] = gi
    gg_ref[...] = gg
    gb_ref[...] = (nt(gi, wi_ref[...]) + nt(gg, wg_ref[...])).astype(gb_ref.dtype)
    mlp_ref[...] = nt(m, wd_ref[...]).astype(mlp_ref.dtype)


def feed_forward(b, g, w, hidden, me, place, count, dtype, onto):
    rows, width = b.shape
    whole = lambda r, n: pl.BlockSpec((r, n), lambda i, me: (0, 0))
    narrow = jax.ShapeDtypeStruct((rows, hidden), BF)
    operands, specs = [b, g, w], [whole(rows, width), whole(rows, width), whole(*w.shape)]
    if onto is not None:
        operands.append(onto)
        specs.append(pl.BlockSpec(memory_space=pl.ANY))
    return pl.pallas_call(
        functools.partial(feed_kernel, hidden),
        grid_spec=pltpu.PrefetchScalarGridSpec(
            num_scalar_prefetch=1,
            grid=(1,),
            in_specs=specs,
            out_specs=[whole(rows, hidden)] * 3
            + [whole(rows, width), pl.BlockSpec((rows, width), lambda i, me: (me[0] ^ place, 0))],
        ),
        out_shape=[narrow] * 3
        + [jax.ShapeDtypeStruct((rows, width), dtype), jax.ShapeDtypeStruct((rows * count, width), BF)],
        input_output_aliases={} if onto is None else {4: 4},
        cost_estimate=pl.CostEstimate(
            flops=12 * rows * width * hidden,
            bytes_accessed=6 * width * hidden + 8 * rows * width + 6 * rows * hidden,
            transcendentals=rows * hidden,
        ),
        name="feed",
    )(me[None], *operands)


def tn(a, b):
    return lax.dot_general(a, b, (((0,), (0,)), ((), ())), preferred_element_type=F32)


def weight_kernel(count, slot, pairs, *refs):
    out_ref = refs[-1]
    hidden = refs[(pairs[0][1]) * count].shape[1]
    for place, (left, right) in enumerate(pairs):
        total = None
        for i in range(count):
            term = tn(refs[left * count + i][...], refs[right * count + i][...])
            total = term if total is None else total + term
        out_ref[:, place * slot : place * slot + hidden] = total.astype(BF)
        if hidden < slot:
            out_ref[:, place * slot + hidden : (place + 1) * slot] = jnp.zeros((out_ref.shape[0], slot - hidden), BF)


def weight_gradients(lefts, rights, pairs, slots, place, onto=None):
    count = len(lefts[0])
    rows, width = lefts[0][0].shape
    hidden = rights[0][0].shape[1]
    slot = -(-hidden // LANES) * LANES
    wide_spec = pl.BlockSpec((rows, 256), lambda i: (0, i))
    whole = pl.BlockSpec((rows, hidden), lambda i: (0, 0))
    operands = [b for group in lefts for b in group] + [b for group in rights for b in group]
    specs = [wide_spec] * (len(lefts) * count) + [whole] * (len(rights) * count)
    aliases = {}
    if onto is not None:
        aliases = {len(operands): 0}
        operands.append(onto)
        specs.append(pl.BlockSpec(memory_space=pl.ANY))
    return pl.pallas_call(
        functools.partial(weight_kernel, count, slot, pairs),
        grid=(width // 256,),
        in_specs=specs,
        out_specs=pl.BlockSpec((256, len(pairs) * slot), lambda i: (i, place // len(pairs))),
        out_shape=jax.ShapeDtypeStruct((width, slots * slot), BF),
        input_output_aliases=aliases,
        cost_estimate=pl.CostEstimate(
            flops=2 * len(pairs) * rows * count * width * hidden,
            bytes_accessed=2 * count * rows * (len(lefts) * width + len(rights) * hidden),
            transcendentals=0,
        ),
        name="weight_gradients",
    )(*operands)


def last_kernel(me_ref, a_ref, gp_ref, mine_ref, away_ref):
    total = tn(a_ref[...], gp_ref[...])

    @pl.when(pl.program_id(0) % 2 == 0)
    def _():
        mine_ref[...] = total

    @pl.when(pl.program_id(0) % 2 == 1)
    def _():
        away_ref[...] = total.astype(BF)


def last_gradients(a, gp, me, size):
    length, width = a.shape
    rows, columns = width // size, gp.shape[1]
    out = lambda dtype: jax.ShapeDtypeStruct((width // 2, columns), dtype)
    return pl.pallas_call(
        last_kernel,
        grid_spec=pltpu.PrefetchScalarGridSpec(
            num_scalar_prefetch=1,
            grid=(size,),
            in_specs=[
                pl.BlockSpec((length, rows), lambda i, me: (0, me[0] ^ i)),
                pl.BlockSpec((length, columns), lambda i, me: (0, 0)),
            ],
            out_specs=[pl.BlockSpec((rows, columns), lambda i, me: (i // 2, 0))] * 2,
        ),
        out_shape=[out(F32), out(BF)],
        cost_estimate=pl.CostEstimate(
            flops=2 * length * width * columns,
            bytes_accessed=2 * length * (width + columns) + 3 * width * columns,
            transcendentals=0,
        ),
        name="last_gradients",
    )(me[None], a, gp)


def qkv_back_kernel(me_ref, gp_ref, w_ref, out_ref):
    out_ref[...] = nt(gp_ref[...], w_ref[...]).astype(BF)


def project_back(gp, weight, me, count):
    rows, width = gp.shape[0] // count, weight.shape[0]
    return pl.pallas_call(
        qkv_back_kernel,
        grid_spec=pltpu.PrefetchScalarGridSpec(
            num_scalar_prefetch=1,
            grid=(count,),
            in_specs=[
                pl.BlockSpec((rows, gp.shape[1]), lambda i, me: (i, 0)),
                pl.BlockSpec((width, gp.shape[1]), lambda i, me: (0, 0)),
            ],
            out_specs=pl.BlockSpec((rows, width), lambda i, me: (me[0] ^ i, 0)),
        ),
        out_shape=jax.ShapeDtypeStruct((rows * count, width), BF),
        cost_estimate=pl.CostEstimate(
            flops=2 * rows * count * width * gp.shape[1],
            bytes_accessed=2 * (rows * count * (width + gp.shape[1]) + width * gp.shape[1]),
            transcendentals=0,
        ),
        name="project_back",
    )(me[None], gp, weight)


def ordered(refs, me, piece):
    values = [ref[piece] for ref in refs]
    bit = 1
    while bit < len(values):
        flip = (me & bit) != 0
        values = [jnp.where(flip, values[k ^ bit], values[k]) for k in range(len(values))]
        bit *= 2
    return values


def gain_part(w_ref, grad_ref, gain_ref, out_ref):
    total = jnp.sum(w_ref[...].astype(F32) * grad_ref[...], axis=1, keepdims=True)
    total = jnp.broadcast_to(total, (total.shape[0], LANES)).T
    out_ref[...] = total[:1] / gain_ref[...].astype(F32)


def last_rows_kernel(count, me_ref, *refs):
    blocks, (w_ref, gain_ref, qkv_ref, out_ref, gg_ref) = refs[:count], refs[count:]
    part = (blocks[0].shape[1] - LANES) // (3 + count)
    piece = lambda i: (slice(None), slice(i * part, (i + 1) * part))
    for i in range(3):
        for j, value in enumerate(ordered(blocks, me_ref[0], piece(i))):
            first = (i * count + j) * part
            qkv_ref[:, first : first + part] = value.astype(F32)
    for j in range(count):
        total = None
        for value in ordered(blocks, me_ref[0], piece(3 + j)):
            total = value.astype(F32) if total is None else total + value.astype(F32)
        out_ref[:, j * part : (j + 1) * part] = total
    gain_part(w_ref, qkv_ref, gain_ref, gg_ref)


def in_rows_kernel(count, hidden, me_ref, *refs):
    blocks, (w_ref, gain_ref, in_ref, gg_ref) = refs[:count], refs[count:]
    slot = blocks[0].shape[1] // 2
    for i in range(2):
        piece = (slice(None), slice(i * slot, i * slot + hidden))
        values = [value.astype(F32) for value in ordered(blocks, me_ref[0], piece)]
        in_ref[:, i * count * hidden : (i + 1) * count * hidden] = jnp.concatenate(values, axis=1)
    gain_part(w_ref, in_ref, gain_ref, gg_ref)


def finish_rows(kernel, blocks, weight, gain, me, widths, name):
    rows = weight.shape[0]
    shapes = [jax.ShapeDtypeStruct((rows, n), F32) for n in widths] + [jax.ShapeDtypeStruct((1, rows), F32)]
    return pl.pallas_call(
        kernel,
        in_specs=[pl.BlockSpec(memory_space=pltpu.SMEM)] + [pl.BlockSpec(memory_space=pltpu.VMEM)] * (len(blocks) + 2),
        out_shape=shapes,
        cost_estimate=pl.CostEstimate(flops=0, bytes_accessed=8 * rows * sum(widths), transcendentals=0),
        name=name,
    )(me[None], *blocks, weight, gain[None])


def normal(values):
    centered = values - jnp.mean(values, axis=-1, keepdims=True)
    scale = lax.rsqrt(jnp.mean(centered * centered, axis=-1, keepdims=True) + NORM_EPS)
    return centered * scale, scale


def norm_back(upstream, gain, values):
    unit, scale = normal(values)
    weighted = upstream * gain
    return scale * (
        weighted
        - jnp.mean(weighted, axis=-1, keepdims=True)
        - unit * jnp.mean(weighted * unit, axis=-1, keepdims=True)
    )


def matmul(a, b):
    return jnp.dot(a, b, preferred_element_type=F32)


def matmul_nt(a, b):
    return lax.dot_general(a, b, (((1,), (1,)), ((), ())), preferred_element_type=F32)


def matmul_tn(a, b):
    return lax.dot_general(a, b, (((0,), (0,)), ((), ())), preferred_element_type=F32)


def on_device(
    hidden_in, segment_ids, valid_tokens, w_qkv, w_attn_out, w_in_proj, w_out_proj, attn_gain, mlp_gain, cotangent
):
    seq_size, fsdp_size = lax.axis_size("seq"), lax.axis_size("fsdp")
    seq, fsdp = lax.axis_index("seq"), lax.axis_index("fsdp")
    x_low, cot = hidden_in[0], cotangent[0]
    tokens = x_low.shape[0]
    length = tokens * seq_size
    part = D // seq_size
    hidden = FF // seq_size
    rel = [seq ^ k for k in range(seq_size)]

    def by_block(row):
        return jnp.concatenate([lax.dynamic_slice_in_dim(row, r * tokens, tokens) for r in rel])

    seg_all, valid_all = by_block(segment_ids[0]), by_block(valid_tokens[0])
    positions = by_block(jnp.arange(length, dtype=jnp.int32))
    frequency = ROPE_BASE ** (-2.0 * jnp.arange(HD // 2, dtype=F32) / HD)
    angles = positions.astype(F32)[:, None] * frequency[None, :]
    cosine, sine = lax.optimization_barrier((jnp.cos(angles), jnp.sin(angles)))
    cosine = jnp.concatenate([cosine] * 4, axis=1)
    sine = jnp.concatenate([-sine, sine] * 2, axis=1)
    seg_col, valid_col, seg_row = seg_all[:, None], valid_all[:, None], seg_all[None, :]

    first_mine = [lax.dynamic_slice_in_dim(w_qkv, i * D + seq * part, part, axis=1) for i in range(3)]
    first_mine.append(lax.dynamic_slice_in_dim(w_attn_out, seq * part, part, axis=1))
    gains = jnp.stack([attn_gain, mlp_gain], axis=1)
    first_mine.append(jnp.pad(gains, ((0, 0), (0, LANES - 2))))
    first_mine = jnp.concatenate(first_mine, axis=1)
    first_weight = gather_rows(first_mine)
    core = fsdp % 2
    slot = -(-hidden // LANES) * LANES
    if paired():
        down_mine = transpose_devices(lax.dynamic_slice_in_dim(w_out_proj, seq * part, part, axis=1))
    x_near = relay_first(x_low)
    out_mine = first_weight[:, 3 * part : 4 * part]
    gains = first_weight[:, 4 * part :].T.astype(F32)
    gain_one, gain_two = gains[0:1], gains[1:2]
    core = fsdp % 2
    slot = -(-hidden // LANES) * LANES
    def padded(rows):
        return jnp.pad(rows, ((0, 0), (0, slot - hidden)))

    def halves(rows):
        half = rows.shape[1] // 2
        low, high = rows[:, :half], rows[:, half:]
        return jnp.where(core == 0, low, high), jnp.where(core == 0, high, low)

    def by_core(mine, other):
        return jnp.where(core == 0, mine, other), jnp.where(core == 0, other, mine)

    in_mine = [
        padded(lax.dynamic_slice_in_dim(w_in_proj, i * FF + seq * hidden, hidden, axis=1)) for i in range(2)
    ]
    if paired():
        x_blocks = relay_last(x_low, *x_near)
        kept, sent = halves(after(down_mine, x_blocks, cosine, sine, seg_col, valid_col))
        down_mine = jnp.concatenate(by_core(kept, swap(sent, "fsdp", 1)), axis=0)
        feed_weight = gather_rows(jnp.concatenate(in_mine + [padded(down_mine.T)], axis=1))
    else:
        down_weight = lax.all_gather(w_out_proj, "fsdp", axis=0, tiled=True)
        down_weight = lax.dynamic_slice_in_dim(down_weight, seq * hidden, hidden, axis=0)
        feed_weight = jnp.concatenate([gather_rows(jnp.concatenate(in_mine, axis=1)), padded(down_weight.T)], axis=1)
        x_blocks = relay_last(x_low, *x_near)
    cot_near = relay_first(after(cot, *x_blocks))

    def in_order(blocks):
        bit = 1
        while bit < seq_size:
            flip = (seq & bit) != 0
            blocks = [jnp.where(flip, blocks[k ^ bit], blocks[k]) for k in range(seq_size)]
            bit *= 2
        return blocks


    a_low, q, k, v = project_qkv(x_blocks, first_weight, gain_one, cosine, sine)
    k, cot_near = after((k, cot_near), q)
    cot_blocks = relay_last(cot, *cot_near)
    mixed, lse = attend_forward(q, k, v, seg_col, valid_col, seg_row, tokens)

    out_near = relay_first(out_mine)
    mixed, out_near, cot_blocks = after((mixed, out_near, cot_blocks))
    out_weight = jnp.concatenate(in_order(relay_last(out_mine, *out_near)), axis=1)

    def to_tokens(blocks):
        came = [blocks[:tokens]] + [
            swap(blocks[i * tokens : (i + 1) * tokens], "seq", i) for i in range(1, seq_size)
        ]
        return jnp.concatenate(in_order(came), axis=1)

    mixed_low = to_tokens(mixed)
    x = x_low.astype(F32)
    attn_branch = matmul(mixed_low, out_weight)
    middle = x + attn_branch
    normed_two = (normal(middle)[0] * gain_two).astype(BF)
    normed_two = after(normed_two, *cot_blocks)

    b_blocks = share_seq(normed_two)
    fed, came, mlp_all = [None] * seq_size, [], None
    for i in range(seq_size):
        b = after(b_blocks[i], *came[:-1]) if len(came) > 1 else b_blocks[i]
        fed[i] = feed_forward(
            b, cot_blocks[i], feed_weight, hidden, seq, i, seq_size, F32 if i == 0 else BF, mlp_all
        )
        mlp_all = fed[i][4]
        if i > 0:
            came.append(swap(fed[i][3], "seq", i))
    m_blocks, gz_i, gz_g, gb_blocks, _ = zip(*fed)
    fed_grads = weight_gradients([after(b_blocks, *came[:-2])], [gz_i, gz_g], ((0, 1), (0, 2)), 3, 0)
    fed_grads = weight_gradients([after(cot_blocks, *came)], [m_blocks], ((0, 1),), 3, 2, fed_grads)
    grad_normed_two = gb_blocks[0]
    for block in came:
        grad_normed_two = grad_normed_two + block.astype(F32)
    grad_middle = cot.astype(F32) + norm_back(grad_normed_two, gain_two, middle)
    grad_attn_low = grad_middle.astype(BF)
    grad_mixed = matmul_nt(grad_attn_low, out_weight).astype(BF)

    sent = [lax.dynamic_slice_in_dim(grad_mixed, r * part, part, axis=1) for r in rel]
    came = [sent[0]] + [swap(sent[i], "seq", i) for i in range(1, seq_size)]
    grad_by_heads = jnp.concatenate(came, axis=0)
    out_part = matmul_tn(mixed_low, after(grad_attn_low, grad_by_heads)).astype(BF)
    grad_by_heads = after(grad_by_heads, out_part)
    mlp_came = exchange_seq(after(mlp_all, grad_by_heads))

    def own_rows(partial):
        return lax.psum_scatter(partial, "fsdp", scatter_dimension=0, tiled=True)

    fed_rows = own_rows(fed_grads)
    out_rows = own_rows(out_part)

    gp = attend_backward(
        q, k, v, grad_by_heads, lse, seg_col, valid_col, seg_row, cosine, sine, tokens
    )
    if paired():
        mine, away = last_gradients(a_low, gp, fsdp, fsdp_size)
    else:
        mine = away = matmul_tn(a_low, gp)
    mlp_branch = sum_blocks(after(mlp_came, away))
    result = middle + mlp_branch
    valid_mine = valid_all[:tokens].astype(F32)[:, None]
    stats = jnp.stack(
        [
            jnp.sum(valid_mine * result * result),
            jnp.sum(valid_mine * attn_branch * attn_branch),
            jnp.sum(valid_mine * mlp_branch * mlp_branch),
            jnp.sum(valid_mine),
        ]
    )

    def sum_bit(values, bit):
        rows = jnp.broadcast_to(values[:, None], (values.shape[0], LANES))
        return values + swap(rows, "fsdp", bit)[:, 0]

    stats = sum_bit(stats, 1)
    gp_late, stats = after((gp, stats))
    fed_late, stats = after((fed_rows, stats))
    in_rows, down_rows = fed_late[:, : 2 * slot], fed_late[:, 2 * slot :]
    in_all = share_seq(in_rows)
    ga_parts = project_back(gp_late, first_weight, seq, seq_size)
    ga_came = exchange_seq(after(ga_parts, *in_all[1:3]))
    if paired():
        mine = mine + after(swap(away, "fsdp", 1), ga_parts).astype(F32)
        down_rows = transpose_devices(down_rows)
        rows = mine.shape[0] // (fsdp_size // 2)
        terms = in_three(stats)
        extra = jnp.pad(terms, ((0, 16 - 3), (0, mine.shape[1] - 4)))
        came = [
            swap(jnp.concatenate([mine[k * rows : (k + 1) * rows].astype(BF), extra]), "fsdp", 2 * k)
            for k in range(1, fsdp_size // 2)
        ]
        came, ga_came = after((came, ga_came), out_rows)
        last = mine[:rows]
        for block in came:
            last = last + block[:rows].astype(F32)
        stats = tree_sum([from_three(terms)] + [from_three(block[rows : rows + 3, :4]) for block in came])
    else:
        last = lax.psum_scatter(mine, "fsdp", scatter_dimension=0, tiled=True)
        bit = 2
        while bit < fsdp_size:
            stats = sum_bit(stats, bit)
            bit *= 2
    extra = jnp.pad(in_three(stats), ((0, last.shape[0] - 3), (0, LANES - 4)))
    last = jnp.concatenate([last.astype(BF), out_rows, extra], axis=1)
    ga_came, in_all, down_rows = after((ga_came, in_all, down_rows), last)

    grad_in_weight, grad_gain_two = finish_rows(
        functools.partial(in_rows_kernel, seq_size, hidden), in_all, w_in_proj, mlp_gain, seq, (2 * FF,), "in_rows"
    )
    if paired():
        kept, sent = halves(down_rows[:, :hidden])
        down_rows = jnp.concatenate(by_core(kept, swap(sent, "fsdp", 1)), axis=0).T
        grad_down = jnp.concatenate(in_order(share_seq(down_rows)), axis=1).astype(F32)
    else:
        down = lax.all_gather(down_rows[:, :hidden], ("seq", "fsdp"), axis=0, tiled=True)
        down = down.reshape(seq_size, D, hidden).transpose(0, 2, 1).reshape(FF, D)
        rows = FF // fsdp_size
        grad_down = lax.dynamic_slice_in_dim(down, fsdp * rows, rows, axis=0).astype(F32)

    grad_normed = sum_blocks(ga_came)
    grad_inputs = grad_middle + norm_back(grad_normed, gain_one, x)
    last = after(share_seq(last), grad_in_weight, grad_down, grad_inputs)
    grad_qkv_weight, grad_out_weight, grad_gain_one = finish_rows(
        functools.partial(last_rows_kernel, seq_size), last, w_qkv, attn_gain, seq, (3 * D, D), "last_rows"
    )

    stats = tree_sum([from_three(rows[:3, -LANES : 4 - LANES]) for rows in last])
    root_means = jnp.sqrt(stats[:3] / (jnp.maximum(stats[3], 1.0) * D))

    return (
        result.astype(BF)[None],
        grad_inputs[None],
        grad_qkv_weight,
        grad_out_weight,
        grad_in_weight,
        grad_down,
        grad_gain_one[0],
        grad_gain_two[0],
        root_means,
    )


def solution(mesh):
    in_specs = (
        P("fsdp", "seq", None),
        P("fsdp", None),
        P("fsdp", None),
        P("fsdp", None),
        P("fsdp", None),
        P("fsdp", None),
        P("fsdp", None),
        P("fsdp"),
        P("fsdp"),
        P("fsdp", "seq", None),
    )
    out_specs = (
        P("fsdp", "seq", None),
        P("fsdp", "seq", None),
        P("fsdp", None),
        P("fsdp", None),
        P("fsdp", None),
        P("fsdp", None),
        P("fsdp"),
        P("fsdp"),
        P(),
    )
    return jax.shard_map(on_device, mesh=mesh, in_specs=in_specs, out_specs=out_specs, check_vma=False)
```

```python
import functools

import jax
import jax.numpy as jnp
from jax import lax
from jax.experimental import pallas as pl
from jax.experimental.pallas import tpu as pltpu
from jax.sharding import PartitionSpec as P

D = 1024
HEADS = 16
HD = 64
FF = 2624

ROPE_BASE = 160000.0
NORM_EPS = 1e-05
LANES = 128
BF = jnp.bfloat16
F32 = jnp.float32


def swap(x, axis, bit):
    return lax.ppermute(x, axis, [(i, i ^ bit) for i in range(lax.axis_size(axis))])


def after(x, *others):
    return lax.optimization_barrier((x, others))[0]


def share_seq(block):
    return [block] + [swap(block, "seq", k) for k in range(1, lax.axis_size("seq"))]


def relay_first(block):
    return swap(block, "seq", 1), swap(block, "seq", 2)


def relay_last(block, one, two):
    if lax.axis_size("seq") != 4:
        return share_seq(block)
    half = block.shape[0] // 2
    upper, lower = swap(two[:half], "seq", 1), swap(one[half:], "seq", 2)
    return [block, one, two, jnp.concatenate([upper, lower], axis=0)]


def exchange_seq(blocks):
    return lax.all_to_all(blocks, "seq", split_axis=0, concat_axis=0, tiled=True)


def sum_blocks(blocks):
    rows = blocks.shape[0] // lax.axis_size("seq")
    total = blocks[:rows].astype(F32)
    for i in range(1, lax.axis_size("seq")):
        total = total + blocks[i * rows : (i + 1) * rows].astype(F32)
    return total


def paired():
    return lax.axis_size("fsdp") == 2 * lax.axis_size("seq")


def gather_rows(block):
    return lax.all_gather(block, "fsdp", axis=0, tiled=True)


def transpose_devices(x):
    seq, fsdp = lax.axis_size("seq"), lax.axis_size("fsdp")
    pairs = [
        (s * fsdp + 2 * z + c, z * fsdp + 2 * s + c)
        for s in range(seq)
        for z in range(fsdp // 2)
        for c in range(2)
    ]
    return lax.ppermute(x, ("seq", "fsdp"), pairs)


def tree_sum(values):
    while len(values) > 1:
        values = [values[i] + values[i + 1] for i in range(0, len(values), 2)]
    return values[0]


def in_three(values):
    terms = []
    for _ in range(3):
        terms.append(lax.reduce_precision(values, 8, 7))
        values = values - terms[-1]
    return jnp.stack(terms).astype(BF)


def from_three(terms):
    terms = terms.astype(F32)
    return (terms[0] + terms[1]) + terms[2]


def half_swap(values):
    width = values.shape[1]
    lane = lax.broadcasted_iota(jnp.int32, values.shape, 1)
    ahead = pltpu.roll(values, width - HD // 2, 1)
    behind = pltpu.roll(values, HD // 2, 1)
    return jnp.where(lane % HD < HD // 2, ahead, behind)


def wide(table, width):
    return jnp.concatenate([table] * (width // table.shape[1]), axis=1)


def qkv_kernel(*refs):
    count = 4
    xs = refs[:count]
    w_ref, gain_ref, cos_ref, sin_ref, a_ref, q_ref, k_ref, v_ref, held = refs[count:]
    step = pl.program_id(0)
    for i in range(count):

        @pl.when(step == i)
        def _():
            held[...] = xs[i][...].astype(F32)

    values = held[...]
    centered = values - jnp.mean(values, axis=1, keepdims=True)
    variance = jnp.mean(centered * centered, axis=1, keepdims=True)
    low = (centered * lax.rsqrt(variance + NORM_EPS) * gain_ref[...]).astype(BF)
    a_ref[...] = low
    p = jnp.dot(low, w_ref[...], preferred_element_type=F32)
    part = p.shape[1] // 3
    turned = p[:, : 2 * part]
    turned = turned * wide(cos_ref[...], 2 * part) + half_swap(turned) * wide(sin_ref[...], 2 * part)
    q_ref[...] = turned[:, :part].astype(BF) * (HD**-0.5)
    k_ref[...] = turned[:, part:].astype(BF)
    v_ref[...] = p[:, 2 * part :].astype(BF)


def project_qkv(blocks, weight, gain, cosine, sine):
    rows, width = blocks[0].shape
    part = (weight.shape[1] - LANES) // 4
    count = len(blocks)
    whole = lambda a: pl.BlockSpec(a.shape, lambda i: (0, 0))
    tile = lambda n: pl.BlockSpec((rows, n), lambda i: (i, 0))
    shape = lambda n: jax.ShapeDtypeStruct((rows * count, n), BF)
    return pl.pallas_call(
        qkv_kernel,
        grid=(count,),
        in_specs=[whole(b) for b in blocks]
        + [pl.BlockSpec((width, 3 * part), lambda i: (0, 0)), whole(gain), tile(cosine.shape[1]), tile(sine.shape[1])],
        out_specs=[tile(width), tile(part), tile(part), tile(part)],
        out_shape=[shape(width), shape(part), shape(part), shape(part)],
        scratch_shapes=[pltpu.VMEM((rows, width), F32)],
        cost_estimate=pl.CostEstimate(
            flops=2 * rows * count * width * 3 * part,
            bytes_accessed=2 * rows * count * (2 * width + 3 * part) + 2 * width * 3 * part,
            transcendentals=0,
        ),
        name="qkv",
    )(*blocks, weight, gain, cosine, sine)


def mask_bias(seg_col, valid_col, seg_row, first_row):
    shape = (seg_col.shape[0], seg_row.shape[1])
    key = lax.broadcasted_iota(jnp.int32, shape, 0)
    query = lax.broadcasted_iota(jnp.int32, shape, 1) + first_row
    allowed = (seg_col == seg_row) & ((valid_col > 0) | (key == query))
    return jnp.where(allowed, 0.0, -1e30)


def forward_kernel(q_ref, k_ref, v_ref, segc_ref, valc_ref, segr_ref, o_ref, lse_ref, vt_ref, ot_ref, bias_ref):
    step = pl.program_id(0)
    rows, width = q_ref.shape

    @pl.when(step == 0)
    def _():
        vt_ref[...] = v_ref[...].T

    bias_ref[...] = mask_bias(segc_ref[...], valc_ref[...], segr_ref[...], step * rows)
    qt = q_ref[...].T
    feature = lax.broadcasted_iota(jnp.int32, qt.shape, 0) // HD

    def head(h, carry):
        mine = jnp.where(feature == h, qt, jnp.zeros_like(qt))
        scores = jnp.dot(k_ref[...], mine, preferred_element_type=F32) + bias_ref[...]
        top = jnp.max(scores, axis=0, keepdims=True)
        exponent = jnp.exp(scores - top)
        total = jnp.sum(exponent, axis=0, keepdims=True)
        weights = (exponent * (1.0 / total)).astype(BF)
        start = pl.multiple_of(h * HD, HD)
        ot_ref[pl.ds(start, HD), :] = jnp.dot(
            vt_ref[pl.ds(start, HD), :], weights, preferred_element_type=F32
        )
        lse_ref[pl.ds(h, 1), :] = top + jnp.log(total)
        return carry

    lax.fori_loop(0, width // HD, head, 0)
    o_ref[...] = ot_ref[...].T.astype(BF)


def attend_forward(q, k, v, seg_col, valid_col, seg_row, rows):
    length, width = q.shape
    whole = lambda a: pl.BlockSpec(a.shape, lambda i: (0, 0))
    tile = pl.BlockSpec((rows, width), lambda i: (i, 0))
    return pl.pallas_call(
        forward_kernel,
        grid=(length // rows,),
        in_specs=[tile, whole(k), whole(v), whole(seg_col), whole(valid_col), pl.BlockSpec((1, rows), lambda i: (0, i))],
        out_specs=[tile, pl.BlockSpec((8, rows), lambda i: (0, i))],
        out_shape=[jax.ShapeDtypeStruct((length, width), BF), jax.ShapeDtypeStruct((8, length), F32)],
        scratch_shapes=[pltpu.VMEM((width, length), BF), pltpu.VMEM((width, rows), F32), pltpu.VMEM((length, rows), F32)],
        cost_estimate=pl.CostEstimate(
            flops=4 * length * length * width, bytes_accessed=8 * length * width, transcendentals=length * length * 4
        ),
        name="attend",
    )(q, k, v, seg_col, valid_col, seg_row)


def backward_kernel(
    q_ref, go_ref, lse_ref, k_ref, v_ref, segc_ref, valc_ref, segr_ref, cos_ref, sin_ref,
    gp_ref, kt_ref, dk_ref, dv_ref, dqt_ref, bias_ref,
):
    step = pl.program_id(0)
    rows, width = q_ref.shape

    @pl.when(step == 0)
    def _():
        kt_ref[...] = k_ref[...].T
        dk_ref[...] = jnp.zeros_like(dk_ref)
        dv_ref[...] = jnp.zeros_like(dv_ref)

    bias_ref[...] = mask_bias(segc_ref[...], valc_ref[...], segr_ref[...], step * rows)
    qt, got = q_ref[...].T, go_ref[...].T
    feature = lax.broadcasted_iota(jnp.int32, qt.shape, 0) // HD
    lane = lax.broadcasted_iota(jnp.int32, (rows, width), 1) // HD
    none = jnp.zeros_like(qt)
    none_row = jnp.zeros((rows, width), BF)

    def head(h, carry):
        scores = jnp.dot(k_ref[...], jnp.where(feature == h, qt, none), preferred_element_type=F32)
        weights = jnp.exp(scores + bias_ref[...] - lse_ref[pl.ds(h, 1), :])
        upstream = jnp.dot(v_ref[...], jnp.where(feature == h, got, none), preferred_element_type=F32)
        inner = jnp.sum(weights * upstream, axis=0, keepdims=True)
        low = (weights * (upstream - inner)).astype(BF)
        dv_ref[...] += jnp.dot(
            weights.astype(BF), jnp.where(lane == h, go_ref[...], none_row), preferred_element_type=F32
        )
        dk_ref[...] += jnp.dot(low, jnp.where(lane == h, q_ref[...], none_row), preferred_element_type=F32)
        start = pl.multiple_of(h * HD, HD)
        dqt_ref[pl.ds(start, HD), :] = jnp.dot(kt_ref[pl.ds(start, HD), :], low, preferred_element_type=F32)
        return carry

    lax.fori_loop(0, width // HD, head, 0)

    def unturn(values, cosine, sine):
        values = values.astype(BF).astype(F32)
        return (values * wide(cosine, width) - half_swap(values) * wide(sine, width)).astype(BF)

    here = pl.ds(pl.multiple_of(step * rows, rows), rows)
    gp_ref[here, :width] = unturn(dqt_ref[...].T * (HD**-0.5), cos_ref[here, :], sin_ref[here, :])

    @pl.when(step == pl.num_programs(0) - 1)
    def _():
        gp_ref[:, width : 2 * width] = unturn(dk_ref[...], cos_ref[...], sin_ref[...])
        gp_ref[:, 2 * width :] = dv_ref[...].astype(BF)


def attend_backward(q, k, v, grad_out, lse, seg_col, valid_col, seg_row, cosine, sine, rows):
    length, width = q.shape
    whole = lambda a: pl.BlockSpec(a.shape, lambda i: (0, 0))
    tile = pl.BlockSpec((rows, width), lambda i: (i, 0))
    return pl.pallas_call(
        backward_kernel,
        grid=(length // rows,),
        in_specs=[
            tile, tile, pl.BlockSpec((8, rows), lambda i: (0, i)), whole(k), whole(v),
            whole(seg_col), whole(valid_col), pl.BlockSpec((1, rows), lambda i: (0, i)), whole(cosine), whole(sine),
        ],
        out_specs=pl.BlockSpec((length, 3 * width), lambda i: (0, 0)),
        out_shape=jax.ShapeDtypeStruct((length, 3 * width), BF),
        scratch_shapes=[
            pltpu.VMEM((width, length), BF), pltpu.VMEM((length, width), F32), pltpu.VMEM((length, width), F32),
            pltpu.VMEM((width, rows), F32), pltpu.VMEM((length, rows), F32),
        ],
        cost_estimate=pl.CostEstimate(
            flops=10 * length * length * width, bytes_accessed=20 * length * width, transcendentals=length * length * 4
        ),
        name="attend_back",
    )(q, grad_out, lse, k, v, seg_col, valid_col, seg_row, cosine, sine)


def erf(x):
    x = jnp.clip(x, -3.832506856900711, 3.832506856900711)
    square = x * x
    top = 0.00022905065861350646
    for c in (0.0034082910107109506, 0.050955695062380861, 0.18520832239976145, 1.128379143519084):
        top = top * square + c
    low = -1.1791602954361697e-7
    for c in (0.000023547966471313185, 0.0010179625278914885, 0.014070470171167667, 0.11098505178285362, 0.49746925110067538, 1.0):
        low = low * square + c
    return x * top / low


def nt(a, b):
    return lax.dot_general(a, b, (((1,), (1,)), ((), ())), preferred_element_type=F32)


def feed_kernel(hidden, me_ref, b_ref, g_ref, w_ref, *refs):
    m_ref, gi_ref, gg_ref, gb_ref, mlp_ref = refs[-5:]
    b = b_ref[...]
    slot = w_ref.shape[1] // 3
    wi_ref, wg_ref, wd_ref = (w_ref.at[:, i * slot : i * slot + hidden] for i in range(3))
    inner = jnp.dot(b, wi_ref[...], preferred_element_type=F32)
    gate = jnp.dot(b, wg_ref[...], preferred_element_type=F32)
    upstream = jnp.dot(g_ref[...], wd_ref[...], preferred_element_type=F32)
    half = 0.5 * (1.0 + erf(inner * 0.7071067811865476))
    gelu = inner * half
    slope = half + inner * jnp.exp(-0.5 * inner * inner) * 0.3989422804014327
    m = (gelu * gate).astype(BF)
    gi = (upstream * gate * slope).astype(BF)
    gg = (upstream * gelu).astype(BF)
    m_ref[...] = m
    gi_ref[...] = gi
    gg_ref[...] = gg
    gb_ref[...] = (nt(gi, wi_ref[...]) + nt(gg, wg_ref[...])).astype(gb_ref.dtype)
    mlp_ref[...] = nt(m, wd_ref[...]).astype(mlp_ref.dtype)


def feed_forward(b, g, w, hidden, me, place, count, dtype, onto):
    rows, width = b.shape
    whole = lambda r, n: pl.BlockSpec((r, n), lambda i, me: (0, 0))
    narrow = jax.ShapeDtypeStruct((rows, hidden), BF)
    operands, specs = [b, g, w], [whole(rows, width), whole(rows, width), whole(*w.shape)]
    if onto is not None:
        operands.append(onto)
        specs.append(pl.BlockSpec(memory_space=pl.ANY))
    return pl.pallas_call(
        functools.partial(feed_kernel, hidden),
        grid_spec=pltpu.PrefetchScalarGridSpec(
            num_scalar_prefetch=1,
            grid=(1,),
            in_specs=specs,
            out_specs=[whole(rows, hidden)] * 3
            + [whole(rows, width), pl.BlockSpec((rows, width), lambda i, me: (me[0] ^ place, 0))],
        ),
        out_shape=[narrow] * 3
        + [jax.ShapeDtypeStruct((rows, width), dtype), jax.ShapeDtypeStruct((rows * count, width), BF)],
        input_output_aliases={} if onto is None else {4: 4},
        cost_estimate=pl.CostEstimate(
            flops=12 * rows * width * hidden,
            bytes_accessed=6 * width * hidden + 8 * rows * width + 6 * rows * hidden,
            transcendentals=rows * hidden,
        ),
        name="feed",
    )(me[None], *operands)


def tn(a, b):
    return lax.dot_general(a, b, (((0,), (0,)), ((), ())), preferred_element_type=F32)


def weight_kernel(count, slot, pairs, *refs):
    out_ref = refs[-1]
    hidden = refs[(pairs[0][1]) * count].shape[1]
    for place, (left, right) in enumerate(pairs):
        total = None
        for i in range(count):
            term = tn(refs[left * count + i][...], refs[right * count + i][...])
            total = term if total is None else total + term
        out_ref[:, place * slot : place * slot + hidden] = total.astype(BF)
        if hidden < slot:
            out_ref[:, place * slot + hidden : (place + 1) * slot] = jnp.zeros((out_ref.shape[0], slot - hidden), BF)


def weight_gradients(lefts, rights, pairs, slots, place, onto=None):
    count = len(lefts[0])
    rows, width = lefts[0][0].shape
    hidden = rights[0][0].shape[1]
    slot = -(-hidden // LANES) * LANES
    wide_spec = pl.BlockSpec((rows, 256), lambda i: (0, i))
    whole = pl.BlockSpec((rows, hidden), lambda i: (0, 0))
    operands = [b for group in lefts for b in group] + [b for group in rights for b in group]
    specs = [wide_spec] * (len(lefts) * count) + [whole] * (len(rights) * count)
    aliases = {}
    if onto is not None:
        aliases = {len(operands): 0}
        operands.append(onto)
        specs.append(pl.BlockSpec(memory_space=pl.ANY))
    return pl.pallas_call(
        functools.partial(weight_kernel, count, slot, pairs),
        grid=(width // 256,),
        in_specs=specs,
        out_specs=pl.BlockSpec((256, len(pairs) * slot), lambda i: (i, place // len(pairs))),
        out_shape=jax.ShapeDtypeStruct((width, slots * slot), BF),
        input_output_aliases=aliases,
        cost_estimate=pl.CostEstimate(
            flops=2 * len(pairs) * rows * count * width * hidden,
            bytes_accessed=2 * count * rows * (len(lefts) * width + len(rights) * hidden),
            transcendentals=0,
        ),
        name="weight_gradients",
    )(*operands)


def last_kernel(me_ref, a_ref, gp_ref, mine_ref, away_ref):
    total = tn(a_ref[...], gp_ref[...])

    @pl.when(pl.program_id(0) % 2 == 0)
    def _():
        mine_ref[...] = total

    @pl.when(pl.program_id(0) % 2 == 1)
    def _():
        away_ref[...] = total.astype(BF)


def last_gradients(a, gp, me, size):
    length, width = a.shape
    rows, columns = width // size, gp.shape[1]
    out = lambda dtype: jax.ShapeDtypeStruct((width // 2, columns), dtype)
    return pl.pallas_call(
        last_kernel,
        grid_spec=pltpu.PrefetchScalarGridSpec(
            num_scalar_prefetch=1,
            grid=(size,),
            in_specs=[
                pl.BlockSpec((length, rows), lambda i, me: (0, me[0] ^ i)),
                pl.BlockSpec((length, columns), lambda i, me: (0, 0)),
            ],
            out_specs=[pl.BlockSpec((rows, columns), lambda i, me: (i // 2, 0))] * 2,
        ),
        out_shape=[out(F32), out(BF)],
        cost_estimate=pl.CostEstimate(
            flops=2 * length * width * columns,
            bytes_accessed=2 * length * (width + columns) + 3 * width * columns,
            transcendentals=0,
        ),
        name="last_gradients",
    )(me[None], a, gp)


def qkv_back_kernel(me_ref, gp_ref, w_ref, out_ref):
    out_ref[...] = nt(gp_ref[...], w_ref[...]).astype(BF)


def project_back(gp, weight, me, count):
    rows, width = gp.shape[0] // count, weight.shape[0]
    return pl.pallas_call(
        qkv_back_kernel,
        grid_spec=pltpu.PrefetchScalarGridSpec(
            num_scalar_prefetch=1,
            grid=(count,),
            in_specs=[
                pl.BlockSpec((rows, gp.shape[1]), lambda i, me: (i, 0)),
                pl.BlockSpec((width, gp.shape[1]), lambda i, me: (0, 0)),
            ],
            out_specs=pl.BlockSpec((rows, width), lambda i, me: (me[0] ^ i, 0)),
        ),
        out_shape=jax.ShapeDtypeStruct((rows * count, width), BF),
        cost_estimate=pl.CostEstimate(
            flops=2 * rows * count * width * gp.shape[1],
            bytes_accessed=2 * (rows * count * (width + gp.shape[1]) + width * gp.shape[1]),
            transcendentals=0,
        ),
        name="project_back",
    )(me[None], gp, weight)


def ordered(refs, me, piece):
    values = [ref[piece] for ref in refs]
    bit = 1
    while bit < len(values):
        flip = (me & bit) != 0
        values = [jnp.where(flip, values[k ^ bit], values[k]) for k in range(len(values))]
        bit *= 2
    return values


def gain_part(w_ref, grad_ref, gain_ref, out_ref):
    total = jnp.sum(w_ref[...].astype(F32) * grad_ref[...], axis=1, keepdims=True)
    total = jnp.broadcast_to(total, (total.shape[0], LANES)).T
    out_ref[...] = total[:1] / gain_ref[...].astype(F32)


def last_rows_kernel(count, me_ref, *refs):
    blocks, (w_ref, gain_ref, qkv_ref, out_ref, gg_ref) = refs[:count], refs[count:]
    part = (blocks[0].shape[1] - LANES) // (3 + count)
    piece = lambda i: (slice(None), slice(i * part, (i + 1) * part))
    for i in range(3):
        for j, value in enumerate(ordered(blocks, me_ref[0], piece(i))):
            first = (i * count + j) * part
            qkv_ref[:, first : first + part] = value.astype(F32)
    for j in range(count):
        total = None
        for value in ordered(blocks, me_ref[0], piece(3 + j)):
            total = value.astype(F32) if total is None else total + value.astype(F32)
        out_ref[:, j * part : (j + 1) * part] = total
    gain_part(w_ref, qkv_ref, gain_ref, gg_ref)


def in_rows_kernel(count, hidden, me_ref, *refs):
    blocks, (w_ref, gain_ref, in_ref, gg_ref) = refs[:count], refs[count:]
    slot = blocks[0].shape[1] // 2
    for i in range(2):
        piece = (slice(None), slice(i * slot, i * slot + hidden))
        values = [value.astype(F32) for value in ordered(blocks, me_ref[0], piece)]
        in_ref[:, i * count * hidden : (i + 1) * count * hidden] = jnp.concatenate(values, axis=1)
    gain_part(w_ref, in_ref, gain_ref, gg_ref)


def finish_rows(kernel, blocks, weight, gain, me, widths, name):
    rows = weight.shape[0]
    shapes = [jax.ShapeDtypeStruct((rows, n), F32) for n in widths] + [jax.ShapeDtypeStruct((1, rows), F32)]
    return pl.pallas_call(
        kernel,
        in_specs=[pl.BlockSpec(memory_space=pltpu.SMEM)] + [pl.BlockSpec(memory_space=pltpu.VMEM)] * (len(blocks) + 2),
        out_shape=shapes,
        cost_estimate=pl.CostEstimate(flops=0, bytes_accessed=8 * rows * sum(widths), transcendentals=0),
        name=name,
    )(me[None], *blocks, weight, gain[None])


def normal(values):
    centered = values - jnp.mean(values, axis=-1, keepdims=True)
    scale = lax.rsqrt(jnp.mean(centered * centered, axis=-1, keepdims=True) + NORM_EPS)
    return centered * scale, scale


def norm_back(upstream, gain, values):
    unit, scale = normal(values)
    weighted = upstream * gain
    return scale * (
        weighted
        - jnp.mean(weighted, axis=-1, keepdims=True)
        - unit * jnp.mean(weighted * unit, axis=-1, keepdims=True)
    )


def matmul(a, b):
    return jnp.dot(a, b, preferred_element_type=F32)


def matmul_nt(a, b):
    return lax.dot_general(a, b, (((1,), (1,)), ((), ())), preferred_element_type=F32)


def matmul_tn(a, b):
    return lax.dot_general(a, b, (((0,), (0,)), ((), ())), preferred_element_type=F32)


def on_device(
    hidden_in, segment_ids, valid_tokens, w_qkv, w_attn_out, w_in_proj, w_out_proj, attn_gain, mlp_gain, cotangent
):
    seq_size, fsdp_size = lax.axis_size("seq"), lax.axis_size("fsdp")
    seq, fsdp = lax.axis_index("seq"), lax.axis_index("fsdp")
    x_low, cot = hidden_in[0], cotangent[0]
    tokens = x_low.shape[0]
    length = tokens * seq_size
    part = D // seq_size
    hidden = FF // seq_size
    rel = [seq ^ k for k in range(seq_size)]

    def by_block(row):
        return jnp.concatenate([lax.dynamic_slice_in_dim(row, r * tokens, tokens) for r in rel])

    seg_all, valid_all = by_block(segment_ids[0]), by_block(valid_tokens[0])
    positions = by_block(jnp.arange(length, dtype=jnp.int32))
    frequency = ROPE_BASE ** (-2.0 * jnp.arange(HD // 2, dtype=F32) / HD)
    angles = positions.astype(F32)[:, None] * frequency[None, :]
    cosine, sine = lax.optimization_barrier((jnp.cos(angles), jnp.sin(angles)))
    cosine = jnp.concatenate([cosine] * 4, axis=1)
    sine = jnp.concatenate([-sine, sine] * 2, axis=1)
    seg_col, valid_col, seg_row = seg_all[:, None], valid_all[:, None], seg_all[None, :]

    first_mine = [lax.dynamic_slice_in_dim(w_qkv, i * D + seq * part, part, axis=1) for i in range(3)]
    first_mine.append(lax.dynamic_slice_in_dim(w_attn_out, seq * part, part, axis=1))
    gains = jnp.stack([attn_gain, mlp_gain], axis=1)
    first_mine.append(jnp.pad(gains, ((0, 0), (0, LANES - 2))))
    first_mine = jnp.concatenate(first_mine, axis=1)
    first_weight = gather_rows(first_mine)
    core = fsdp % 2
    slot = -(-hidden // LANES) * LANES
    if paired():
        down_mine = transpose_devices(lax.dynamic_slice_in_dim(w_out_proj, seq * part, part, axis=1))
    x_near = relay_first(x_low)
    out_mine = first_weight[:, 3 * part : 4 * part]
    gains = first_weight[:, 4 * part :].T.astype(F32)
    gain_one, gain_two = gains[0:1], gains[1:2]
    core = fsdp % 2
    slot = -(-hidden // LANES) * LANES
    def padded(rows):
        return jnp.pad(rows, ((0, 0), (0, slot - hidden)))

    def halves(rows):
        half = rows.shape[1] // 2
        low, high = rows[:, :half], rows[:, half:]
        return jnp.where(core == 0, low, high), jnp.where(core == 0, high, low)

    def by_core(mine, other):
        return jnp.where(core == 0, mine, other), jnp.where(core == 0, other, mine)

    in_mine = [
        padded(lax.dynamic_slice_in_dim(w_in_proj, i * FF + seq * hidden, hidden, axis=1)) for i in range(2)
    ]
    if paired():
        x_blocks = relay_last(x_low, *x_near)
        kept, sent = halves(after(down_mine, x_blocks, cosine, sine, seg_col, valid_col))
        down_mine = jnp.concatenate(by_core(kept, swap(sent, "fsdp", 1)), axis=0)
        feed_weight = gather_rows(jnp.concatenate(in_mine + [padded(down_mine.T)], axis=1))
    else:
        down_weight = lax.all_gather(w_out_proj, "fsdp", axis=0, tiled=True)
        down_weight = lax.dynamic_slice_in_dim(down_weight, seq * hidden, hidden, axis=0)
        feed_weight = jnp.concatenate([gather_rows(jnp.concatenate(in_mine, axis=1)), padded(down_weight.T)], axis=1)
        x_blocks = relay_last(x_low, *x_near)
    cot_near = relay_first(after(cot, *x_blocks))

    def in_order(blocks):
        bit = 1
        while bit < seq_size:
            flip = (seq & bit) != 0
            blocks = [jnp.where(flip, blocks[k ^ bit], blocks[k]) for k in range(seq_size)]
            bit *= 2
        return blocks


    a_low, q, k, v = project_qkv(x_blocks, first_weight, gain_one, cosine, sine)
    k, cot_near = after((k, cot_near), q)
    cot_blocks = relay_last(cot, *cot_near)
    mixed, lse = attend_forward(q, k, v, seg_col, valid_col, seg_row, tokens)

    out_near = relay_first(out_mine)
    mixed, out_near, cot_blocks = after((mixed, out_near, cot_blocks))
    out_weight = jnp.concatenate(in_order(relay_last(out_mine, *out_near)), axis=1)

    def to_tokens(blocks):
        came = [blocks[:tokens]] + [
            swap(blocks[i * tokens : (i + 1) * tokens], "seq", i) for i in range(1, seq_size)
        ]
        return jnp.concatenate(in_order(came), axis=1)

    mixed_low = to_tokens(mixed)
    x = x_low.astype(F32)
    attn_branch = matmul(mixed_low, out_weight)
    middle = x + attn_branch
    normed_two = (normal(middle)[0] * gain_two).astype(BF)
    normed_two = after(normed_two, *cot_blocks)

    b_blocks = share_seq(normed_two)
    fed, came, mlp_all = [None] * seq_size, [], None
    for i in range(seq_size):
        b = after(b_blocks[i], *came[:-1]) if len(came) > 1 else b_blocks[i]
        fed[i] = feed_forward(
            b, cot_blocks[i], feed_weight, hidden, seq, i, seq_size, F32 if i == 0 else BF, mlp_all
        )
        mlp_all = fed[i][4]
        if i > 0:
            came.append(swap(fed[i][3], "seq", i))
    m_blocks, gz_i, gz_g, gb_blocks, _ = zip(*fed)
    fed_grads = weight_gradients([after(b_blocks, *came[:-2])], [gz_i, gz_g], ((0, 1), (0, 2)), 3, 0)
    fed_grads = weight_gradients([after(cot_blocks, *came)], [m_blocks], ((0, 1),), 3, 2, fed_grads)
    grad_normed_two = gb_blocks[0]
    for block in came:
        grad_normed_two = grad_normed_two + block.astype(F32)
    grad_middle = cot.astype(F32) + norm_back(grad_normed_two, gain_two, middle)
    grad_attn_low = grad_middle.astype(BF)
    grad_mixed = matmul_nt(grad_attn_low, out_weight).astype(BF)

    sent = [lax.dynamic_slice_in_dim(grad_mixed, r * part, part, axis=1) for r in rel]
    came = [sent[0]] + [swap(sent[i], "seq", i) for i in range(1, seq_size)]
    grad_by_heads = jnp.concatenate(came, axis=0)
    out_part = matmul_tn(mixed_low, after(grad_attn_low, grad_by_heads)).astype(BF)
    grad_by_heads = after(grad_by_heads, out_part)
    mlp_came = exchange_seq(after(mlp_all, grad_by_heads))

    def own_rows(partial):
        return lax.psum_scatter(partial, "fsdp", scatter_dimension=0, tiled=True)

    fed_rows = own_rows(fed_grads)
    out_rows = own_rows(out_part)

    gp = attend_backward(
        q, k, v, grad_by_heads, lse, seg_col, valid_col, seg_row, cosine, sine, tokens
    )
    if paired():
        mine, away = last_gradients(a_low, gp, fsdp, fsdp_size)
    else:
        mine = away = matmul_tn(a_low, gp)
    mlp_branch = sum_blocks(after(mlp_came, away))
    result = middle + mlp_branch
    valid_mine = valid_all[:tokens].astype(F32)[:, None]
    stats = jnp.stack(
        [
            jnp.sum(valid_mine * result * result),
            jnp.sum(valid_mine * attn_branch * attn_branch),
            jnp.sum(valid_mine * mlp_branch * mlp_branch),
            jnp.sum(valid_mine),
        ]
    )

    def sum_bit(values, bit):
        rows = jnp.broadcast_to(values[:, None], (values.shape[0], LANES))
        return values + swap(rows, "fsdp", bit)[:, 0]

    stats = sum_bit(stats, 1)
    gp_late, stats = after((gp, stats))
    fed_late, stats = after((fed_rows, stats))
    in_rows, down_rows = fed_late[:, : 2 * slot], fed_late[:, 2 * slot :]
    in_all = share_seq(in_rows)
    ga_parts = project_back(gp_late, first_weight, seq, seq_size)
    ga_came = exchange_seq(after(ga_parts, *in_all[1:3]))
    if paired():
        mine = mine + after(swap(away, "fsdp", 1), ga_parts).astype(F32)
        down_rows = transpose_devices(down_rows)
        rows = mine.shape[0] // (fsdp_size // 2)
        terms = in_three(stats)
        extra = jnp.pad(terms, ((0, 16 - 3), (0, mine.shape[1] - 4)))
        came = [
            swap(jnp.concatenate([mine[k * rows : (k + 1) * rows].astype(BF), extra]), "fsdp", 2 * k)
            for k in range(1, fsdp_size // 2)
        ]
        came, ga_came = after((came, ga_came), out_rows)
        last = mine[:rows]
        for block in came:
            last = last + block[:rows].astype(F32)
        stats = tree_sum([from_three(terms)] + [from_three(block[rows : rows + 3, :4]) for block in came])
    else:
        last = lax.psum_scatter(mine, "fsdp", scatter_dimension=0, tiled=True)
        bit = 2
        while bit < fsdp_size:
            stats = sum_bit(stats, bit)
            bit *= 2
    extra = jnp.pad(in_three(stats), ((0, last.shape[0] - 3), (0, LANES - 4)))
    last = jnp.concatenate([last.astype(BF), out_rows, extra], axis=1)
    ga_came, in_all, down_rows = after((ga_came, in_all, down_rows), last)

    grad_in_weight, grad_gain_two = finish_rows(
        functools.partial(in_rows_kernel, seq_size, hidden), in_all, w_in_proj, mlp_gain, seq, (2 * FF,), "in_rows"
    )
    last_blocks = share_seq(last)
    grad_normed = sum_blocks(ga_came)
    grad_inputs = grad_middle + norm_back(grad_normed, gain_one, x)
    if paired():
        kept, sent = halves(down_rows[:, :hidden])
        down_rows = jnp.concatenate(by_core(kept, swap(sent, "fsdp", 1)), axis=0).T
        down_rows = after(down_rows, grad_in_weight, grad_inputs, last_blocks[1])
        grad_down = jnp.concatenate(in_order(share_seq(down_rows)), axis=1).astype(F32)
    else:
        down = lax.all_gather(down_rows[:, :hidden], ("seq", "fsdp"), axis=0, tiled=True)
        down = down.reshape(seq_size, D, hidden).transpose(0, 2, 1).reshape(FF, D)
        rows = FF // fsdp_size
        grad_down = lax.dynamic_slice_in_dim(down, fsdp * rows, rows, axis=0).astype(F32)

    last = after(last_blocks, grad_in_weight, grad_inputs)
    grad_qkv_weight, grad_out_weight, grad_gain_one = finish_rows(
        functools.partial(last_rows_kernel, seq_size), last, w_qkv, attn_gain, seq, (3 * D, D), "last_rows"
    )

    stats = tree_sum([from_three(rows[:3, -LANES : 4 - LANES]) for rows in last])
    root_means = jnp.sqrt(stats[:3] / (jnp.maximum(stats[3], 1.0) * D))

    return (
        result.astype(BF)[None],
        grad_inputs[None],
        grad_qkv_weight,
        grad_out_weight,
        grad_in_weight,
        grad_down,
        grad_gain_one[0],
        grad_gain_two[0],
        root_means,
    )


def solution(mesh):
    in_specs = (
        P("fsdp", "seq", None),
        P("fsdp", None),
        P("fsdp", None),
        P("fsdp", None),
        P("fsdp", None),
        P("fsdp", None),
        P("fsdp", None),
        P("fsdp"),
        P("fsdp"),
        P("fsdp", "seq", None),
    )
    out_specs = (
        P("fsdp", "seq", None),
        P("fsdp", "seq", None),
        P("fsdp", None),
        P("fsdp", None),
        P("fsdp", None),
        P("fsdp", None),
        P("fsdp"),
        P("fsdp"),
        P(),
    )
    return jax.shard_map(on_device, mesh=mesh, in_specs=in_specs, out_specs=out_specs, check_vma=False)
```

```python
import functools

import jax
import jax.numpy as jnp
from jax import lax
from jax.experimental import pallas as pl
from jax.experimental.pallas import tpu as pltpu
from jax.sharding import PartitionSpec as P

D = 1024
HEADS = 16
HD = 64
FF = 2624

ROPE_BASE = 160000.0
NORM_EPS = 1e-05
LANES = 128
BF = jnp.bfloat16
F32 = jnp.float32


def swap(x, axis, bit):
    return lax.ppermute(x, axis, [(i, i ^ bit) for i in range(lax.axis_size(axis))])


def after(x, *others):
    return lax.optimization_barrier((x, others))[0]


def share_seq(block):
    return [block] + [swap(block, "seq", k) for k in range(1, lax.axis_size("seq"))]


def relay_first(block):
    return swap(block, "seq", 1), swap(block, "seq", 2)


def relay_last(block, one, two):
    if lax.axis_size("seq") != 4:
        return share_seq(block)
    half = block.shape[0] // 2
    upper, lower = swap(two[:half], "seq", 1), swap(one[half:], "seq", 2)
    return [block, one, two, jnp.concatenate([upper, lower], axis=0)]


def exchange_seq(blocks):
    return lax.all_to_all(blocks, "seq", split_axis=0, concat_axis=0, tiled=True)


def sum_blocks(blocks):
    rows = blocks.shape[0] // lax.axis_size("seq")
    total = blocks[:rows].astype(F32)
    for i in range(1, lax.axis_size("seq")):
        total = total + blocks[i * rows : (i + 1) * rows].astype(F32)
    return total


def paired():
    return lax.axis_size("fsdp") == 2 * lax.axis_size("seq")


def gather_rows(block):
    return lax.all_gather(block, "fsdp", axis=0, tiled=True)


def transpose_devices(x):
    seq, fsdp = lax.axis_size("seq"), lax.axis_size("fsdp")
    pairs = [
        (s * fsdp + 2 * z + c, z * fsdp + 2 * s + c)
        for s in range(seq)
        for z in range(fsdp // 2)
        for c in range(2)
    ]
    return lax.ppermute(x, ("seq", "fsdp"), pairs)


def tree_sum(values):
    while len(values) > 1:
        values = [values[i] + values[i + 1] for i in range(0, len(values), 2)]
    return values[0]


def in_three(values):
    terms = []
    for _ in range(3):
        terms.append(lax.reduce_precision(values, 8, 7))
        values = values - terms[-1]
    return jnp.stack(terms).astype(BF)


def from_three(terms):
    terms = terms.astype(F32)
    return (terms[0] + terms[1]) + terms[2]


def half_swap(values):
    width = values.shape[1]
    lane = lax.broadcasted_iota(jnp.int32, values.shape, 1)
    ahead = pltpu.roll(values, width - HD // 2, 1)
    behind = pltpu.roll(values, HD // 2, 1)
    return jnp.where(lane % HD < HD // 2, ahead, behind)


def wide(table, width):
    return jnp.concatenate([table] * (width // table.shape[1]), axis=1)


def qkv_kernel(*refs):
    count = 4
    xs = refs[:count]
    w_ref, gain_ref, cos_ref, sin_ref, a_ref, q_ref, k_ref, v_ref, held = refs[count:]
    step = pl.program_id(0)
    for i in range(count):

        @pl.when(step == i)
        def _():
            held[...] = xs[i][...].astype(F32)

    values = held[...]
    centered = values - jnp.mean(values, axis=1, keepdims=True)
    variance = jnp.mean(centered * centered, axis=1, keepdims=True)
    low = (centered * lax.rsqrt(variance + NORM_EPS) * gain_ref[...]).astype(BF)
    a_ref[...] = low
    p = jnp.dot(low, w_ref[...], preferred_element_type=F32)
    part = p.shape[1] // 3
    turned = p[:, : 2 * part]
    turned = turned * wide(cos_ref[...], 2 * part) + half_swap(turned) * wide(sin_ref[...], 2 * part)
    q_ref[...] = turned[:, :part].astype(BF) * (HD**-0.5)
    k_ref[...] = turned[:, part:].astype(BF)
    v_ref[...] = p[:, 2 * part :].astype(BF)


def project_qkv(blocks, weight, gain, cosine, sine):
    rows, width = blocks[0].shape
    part = (weight.shape[1] - LANES) // 4
    count = len(blocks)
    whole = lambda a: pl.BlockSpec(a.shape, lambda i: (0, 0))
    tile = lambda n: pl.BlockSpec((rows, n), lambda i: (i, 0))
    shape = lambda n: jax.ShapeDtypeStruct((rows * count, n), BF)
    return pl.pallas_call(
        qkv_kernel,
        grid=(count,),
        in_specs=[whole(b) for b in blocks]
        + [pl.BlockSpec((width, 3 * part), lambda i: (0, 0)), whole(gain), tile(cosine.shape[1]), tile(sine.shape[1])],
        out_specs=[tile(width), tile(part), tile(part), tile(part)],
        out_shape=[shape(width), shape(part), shape(part), shape(part)],
        scratch_shapes=[pltpu.VMEM((rows, width), F32)],
        cost_estimate=pl.CostEstimate(
            flops=2 * rows * count * width * 3 * part,
            bytes_accessed=2 * rows * count * (2 * width + 3 * part) + 2 * width * 3 * part,
            transcendentals=0,
        ),
        name="qkv",
    )(*blocks, weight, gain, cosine, sine)


def mask_bias(seg_col, valid_col, seg_row, first_row):
    shape = (seg_col.shape[0], seg_row.shape[1])
    key = lax.broadcasted_iota(jnp.int32, shape, 0)
    query = lax.broadcasted_iota(jnp.int32, shape, 1) + first_row
    allowed = (seg_col == seg_row) & ((valid_col > 0) | (key == query))
    return jnp.where(allowed, 0.0, -1e30)


def forward_kernel(q_ref, k_ref, v_ref, segc_ref, valc_ref, segr_ref, o_ref, lse_ref, vt_ref, ot_ref, bias_ref):
    step = pl.program_id(0)
    rows, width = q_ref.shape

    @pl.when(step == 0)
    def _():
        vt_ref[...] = v_ref[...].T

    bias_ref[...] = mask_bias(segc_ref[...], valc_ref[...], segr_ref[...], step * rows)
    qt = q_ref[...].T
    feature = lax.broadcasted_iota(jnp.int32, qt.shape, 0) // HD

    def head(h, carry):
        mine = jnp.where(feature == h, qt, jnp.zeros_like(qt))
        scores = jnp.dot(k_ref[...], mine, preferred_element_type=F32) + bias_ref[...]
        top = jnp.max(scores, axis=0, keepdims=True)
        exponent = jnp.exp(scores - top)
        total = jnp.sum(exponent, axis=0, keepdims=True)
        weights = (exponent * (1.0 / total)).astype(BF)
        start = pl.multiple_of(h * HD, HD)
        ot_ref[pl.ds(start, HD), :] = jnp.dot(
            vt_ref[pl.ds(start, HD), :], weights, preferred_element_type=F32
        )
        lse_ref[pl.ds(h, 1), :] = top + jnp.log(total)
        return carry

    lax.fori_loop(0, width // HD, head, 0)
    o_ref[...] = ot_ref[...].T.astype(BF)


def attend_forward(q, k, v, seg_col, valid_col, seg_row, rows):
    length, width = q.shape
    whole = lambda a: pl.BlockSpec(a.shape, lambda i: (0, 0))
    tile = pl.BlockSpec((rows, width), lambda i: (i, 0))
    return pl.pallas_call(
        forward_kernel,
        grid=(length // rows,),
        in_specs=[tile, whole(k), whole(v), whole(seg_col), whole(valid_col), pl.BlockSpec((1, rows), lambda i: (0, i))],
        out_specs=[tile, pl.BlockSpec((8, rows), lambda i: (0, i))],
        out_shape=[jax.ShapeDtypeStruct((length, width), BF), jax.ShapeDtypeStruct((8, length), F32)],
        scratch_shapes=[pltpu.VMEM((width, length), BF), pltpu.VMEM((width, rows), F32), pltpu.VMEM((length, rows), F32)],
        cost_estimate=pl.CostEstimate(
            flops=4 * length * length * width, bytes_accessed=8 * length * width, transcendentals=length * length * 4
        ),
        name="attend",
    )(q, k, v, seg_col, valid_col, seg_row)


def backward_kernel(
    q_ref, go_ref, lse_ref, k_ref, v_ref, segc_ref, valc_ref, segr_ref, cos_ref, sin_ref,
    gp_ref, kt_ref, dk_ref, dv_ref, dqt_ref, bias_ref,
):
    step = pl.program_id(0)
    rows, width = q_ref.shape

    @pl.when(step == 0)
    def _():
        kt_ref[...] = k_ref[...].T
        dk_ref[...] = jnp.zeros_like(dk_ref)
        dv_ref[...] = jnp.zeros_like(dv_ref)

    bias_ref[...] = mask_bias(segc_ref[...], valc_ref[...], segr_ref[...], step * rows)
    qt, got = q_ref[...].T, go_ref[...].T
    feature = lax.broadcasted_iota(jnp.int32, qt.shape, 0) // HD
    lane = lax.broadcasted_iota(jnp.int32, (rows, width), 1) // HD
    none = jnp.zeros_like(qt)
    none_row = jnp.zeros((rows, width), BF)

    def head(h, carry):
        scores = jnp.dot(k_ref[...], jnp.where(feature == h, qt, none), preferred_element_type=F32)
        weights = jnp.exp(scores + bias_ref[...] - lse_ref[pl.ds(h, 1), :])
        upstream = jnp.dot(v_ref[...], jnp.where(feature == h, got, none), preferred_element_type=F32)
        inner = jnp.sum(weights * upstream, axis=0, keepdims=True)
        low = (weights * (upstream - inner)).astype(BF)
        dv_ref[...] += jnp.dot(
            weights.astype(BF), jnp.where(lane == h, go_ref[...], none_row), preferred_element_type=F32
        )
        dk_ref[...] += jnp.dot(low, jnp.where(lane == h, q_ref[...], none_row), preferred_element_type=F32)
        start = pl.multiple_of(h * HD, HD)
        dqt_ref[pl.ds(start, HD), :] = jnp.dot(kt_ref[pl.ds(start, HD), :], low, preferred_element_type=F32)
        return carry

    lax.fori_loop(0, width // HD, head, 0)

    def unturn(values, cosine, sine):
        values = values.astype(BF).astype(F32)
        return (values * wide(cosine, width) - half_swap(values) * wide(sine, width)).astype(BF)

    here = pl.ds(pl.multiple_of(step * rows, rows), rows)
    gp_ref[here, :width] = unturn(dqt_ref[...].T * (HD**-0.5), cos_ref[here, :], sin_ref[here, :])

    @pl.when(step == pl.num_programs(0) - 1)
    def _():
        gp_ref[:, width : 2 * width] = unturn(dk_ref[...], cos_ref[...], sin_ref[...])
        gp_ref[:, 2 * width :] = dv_ref[...].astype(BF)


def attend_backward(q, k, v, grad_out, lse, seg_col, valid_col, seg_row, cosine, sine, rows):
    length, width = q.shape
    whole = lambda a: pl.BlockSpec(a.shape, lambda i: (0, 0))
    tile = pl.BlockSpec((rows, width), lambda i: (i, 0))
    return pl.pallas_call(
        backward_kernel,
        grid=(length // rows,),
        in_specs=[
            tile, tile, pl.BlockSpec((8, rows), lambda i: (0, i)), whole(k), whole(v),
            whole(seg_col), whole(valid_col), pl.BlockSpec((1, rows), lambda i: (0, i)), whole(cosine), whole(sine),
        ],
        out_specs=pl.BlockSpec((length, 3 * width), lambda i: (0, 0)),
        out_shape=jax.ShapeDtypeStruct((length, 3 * width), BF),
        scratch_shapes=[
            pltpu.VMEM((width, length), BF), pltpu.VMEM((length, width), F32), pltpu.VMEM((length, width), F32),
            pltpu.VMEM((width, rows), F32), pltpu.VMEM((length, rows), F32),
        ],
        cost_estimate=pl.CostEstimate(
            flops=10 * length * length * width, bytes_accessed=20 * length * width, transcendentals=length * length * 4
        ),
        name="attend_back",
    )(q, grad_out, lse, k, v, seg_col, valid_col, seg_row, cosine, sine)


def erf(x):
    x = jnp.clip(x, -3.832506856900711, 3.832506856900711)
    square = x * x
    top = 0.00022905065861350646
    for c in (0.0034082910107109506, 0.050955695062380861, 0.18520832239976145, 1.128379143519084):
        top = top * square + c
    low = -1.1791602954361697e-7
    for c in (0.000023547966471313185, 0.0010179625278914885, 0.014070470171167667, 0.11098505178285362, 0.49746925110067538, 1.0):
        low = low * square + c
    return x * top / low


def nt(a, b):
    return lax.dot_general(a, b, (((1,), (1,)), ((), ())), preferred_element_type=F32)


def feed_kernel(hidden, me_ref, b_ref, g_ref, w_ref, *refs):
    m_ref, gi_ref, gg_ref, gb_ref, mlp_ref = refs[-5:]
    b = b_ref[...]
    slot = w_ref.shape[1] // 3
    wi_ref, wg_ref, wd_ref = (w_ref.at[:, i * slot : i * slot + hidden] for i in range(3))
    inner = jnp.dot(b, wi_ref[...], preferred_element_type=F32)
    gate = jnp.dot(b, wg_ref[...], preferred_element_type=F32)
    upstream = jnp.dot(g_ref[...], wd_ref[...], preferred_element_type=F32)
    half = 0.5 * (1.0 + erf(inner * 0.7071067811865476))
    gelu = inner * half
    slope = half + inner * jnp.exp(-0.5 * inner * inner) * 0.3989422804014327
    m = (gelu * gate).astype(BF)
    gi = (upstream * gate * slope).astype(BF)
    gg = (upstream * gelu).astype(BF)
    m_ref[...] = m
    gi_ref[...] = gi
    gg_ref[...] = gg
    gb_ref[...] = (nt(gi, wi_ref[...]) + nt(gg, wg_ref[...])).astype(gb_ref.dtype)
    mlp_ref[...] = nt(m, wd_ref[...]).astype(mlp_ref.dtype)


def feed_forward(b, g, w, hidden, me, place, count, dtype, onto):
    rows, width = b.shape
    whole = lambda r, n: pl.BlockSpec((r, n), lambda i, me: (0, 0))
    narrow = jax.ShapeDtypeStruct((rows, hidden), BF)
    operands, specs = [b, g, w], [whole(rows, width), whole(rows, width), whole(*w.shape)]
    if onto is not None:
        operands.append(onto)
        specs.append(pl.BlockSpec(memory_space=pl.ANY))
    return pl.pallas_call(
        functools.partial(feed_kernel, hidden),
        grid_spec=pltpu.PrefetchScalarGridSpec(
            num_scalar_prefetch=1,
            grid=(1,),
            in_specs=specs,
            out_specs=[whole(rows, hidden)] * 3
            + [whole(rows, width), pl.BlockSpec((rows, width), lambda i, me: (me[0] ^ place, 0))],
        ),
        out_shape=[narrow] * 3
        + [jax.ShapeDtypeStruct((rows, width), dtype), jax.ShapeDtypeStruct((rows * count, width), BF)],
        input_output_aliases={} if onto is None else {4: 4},
        cost_estimate=pl.CostEstimate(
            flops=12 * rows * width * hidden,
            bytes_accessed=6 * width * hidden + 8 * rows * width + 6 * rows * hidden,
            transcendentals=rows * hidden,
        ),
        name="feed",
    )(me[None], *operands)


def tn(a, b):
    return lax.dot_general(a, b, (((0,), (0,)), ((), ())), preferred_element_type=F32)


def weight_kernel(count, slot, pairs, *refs):
    out_ref = refs[-1]
    hidden = refs[(pairs[0][1]) * count].shape[1]
    for place, (left, right) in enumerate(pairs):
        total = None
        for i in range(count):
            term = tn(refs[left * count + i][...], refs[right * count + i][...])
            total = term if total is None else total + term
        out_ref[:, place * slot : place * slot + hidden] = total.astype(BF)
        if hidden < slot:
            out_ref[:, place * slot + hidden : (place + 1) * slot] = jnp.zeros((out_ref.shape[0], slot - hidden), BF)


def weight_gradients(lefts, rights, pairs, slots, place, onto=None):
    count = len(lefts[0])
    rows, width = lefts[0][0].shape
    hidden = rights[0][0].shape[1]
    slot = -(-hidden // LANES) * LANES
    wide_spec = pl.BlockSpec((rows, 256), lambda i: (0, i))
    whole = pl.BlockSpec((rows, hidden), lambda i: (0, 0))
    operands = [b for group in lefts for b in group] + [b for group in rights for b in group]
    specs = [wide_spec] * (len(lefts) * count) + [whole] * (len(rights) * count)
    aliases = {}
    if onto is not None:
        aliases = {len(operands): 0}
        operands.append(onto)
        specs.append(pl.BlockSpec(memory_space=pl.ANY))
    return pl.pallas_call(
        functools.partial(weight_kernel, count, slot, pairs),
        grid=(width // 256,),
        in_specs=specs,
        out_specs=pl.BlockSpec((256, len(pairs) * slot), lambda i: (i, place // len(pairs))),
        out_shape=jax.ShapeDtypeStruct((width, slots * slot), BF),
        input_output_aliases=aliases,
        cost_estimate=pl.CostEstimate(
            flops=2 * len(pairs) * rows * count * width * hidden,
            bytes_accessed=2 * count * rows * (len(lefts) * width + len(rights) * hidden),
            transcendentals=0,
        ),
        name="weight_gradients",
    )(*operands)


def last_kernel(me_ref, a_ref, gp_ref, mine_ref, away_ref):
    total = tn(a_ref[...], gp_ref[...])

    @pl.when(pl.program_id(0) % 2 == 0)
    def _():
        mine_ref[...] = total

    @pl.when(pl.program_id(0) % 2 == 1)
    def _():
        away_ref[...] = total.astype(BF)


def last_gradients(a, gp, me, size):
    length, width = a.shape
    rows, columns = width // size, gp.shape[1]
    out = lambda dtype: jax.ShapeDtypeStruct((width // 2, columns), dtype)
    return pl.pallas_call(
        last_kernel,
        grid_spec=pltpu.PrefetchScalarGridSpec(
            num_scalar_prefetch=1,
            grid=(size,),
            in_specs=[
                pl.BlockSpec((length, rows), lambda i, me: (0, me[0] ^ i)),
                pl.BlockSpec((length, columns), lambda i, me: (0, 0)),
            ],
            out_specs=[pl.BlockSpec((rows, columns), lambda i, me: (i // 2, 0))] * 2,
        ),
        out_shape=[out(F32), out(BF)],
        cost_estimate=pl.CostEstimate(
            flops=2 * length * width * columns,
            bytes_accessed=2 * length * (width + columns) + 3 * width * columns,
            transcendentals=0,
        ),
        name="last_gradients",
    )(me[None], a, gp)


def qkv_back_kernel(me_ref, gp_ref, w_ref, out_ref):
    out_ref[...] = nt(gp_ref[...], w_ref[...]).astype(BF)


def project_back(gp, weight, me, count):
    rows, width = gp.shape[0] // count, weight.shape[0]
    return pl.pallas_call(
        qkv_back_kernel,
        grid_spec=pltpu.PrefetchScalarGridSpec(
            num_scalar_prefetch=1,
            grid=(count,),
            in_specs=[
                pl.BlockSpec((rows, gp.shape[1]), lambda i, me: (i, 0)),
                pl.BlockSpec((width, gp.shape[1]), lambda i, me: (0, 0)),
            ],
            out_specs=pl.BlockSpec((rows, width), lambda i, me: (me[0] ^ i, 0)),
        ),
        out_shape=jax.ShapeDtypeStruct((rows * count, width), BF),
        cost_estimate=pl.CostEstimate(
            flops=2 * rows * count * width * gp.shape[1],
            bytes_accessed=2 * (rows * count * (width + gp.shape[1]) + width * gp.shape[1]),
            transcendentals=0,
        ),
        name="project_back",
    )(me[None], gp, weight)


def ordered(refs, me, piece):
    values = [ref[piece] for ref in refs]
    bit = 1
    while bit < len(values):
        flip = (me & bit) != 0
        values = [jnp.where(flip, values[k ^ bit], values[k]) for k in range(len(values))]
        bit *= 2
    return values


def gain_part(w_ref, grad_ref, gain_ref, out_ref):
    total = jnp.sum(w_ref[...].astype(F32) * grad_ref[...], axis=1, keepdims=True)
    total = jnp.broadcast_to(total, (total.shape[0], LANES)).T
    out_ref[...] = total[:1] / gain_ref[...].astype(F32)


def last_rows_kernel(count, me_ref, *refs):
    blocks, (w_ref, gain_ref, qkv_ref, out_ref, gg_ref) = refs[:count], refs[count:]
    part = (blocks[0].shape[1] - LANES) // (3 + count)
    piece = lambda i: (slice(None), slice(i * part, (i + 1) * part))
    for i in range(3):
        for j, value in enumerate(ordered(blocks, me_ref[0], piece(i))):
            first = (i * count + j) * part
            qkv_ref[:, first : first + part] = value.astype(F32)
    for j in range(count):
        total = None
        for value in ordered(blocks, me_ref[0], piece(3 + j)):
            total = value.astype(F32) if total is None else total + value.astype(F32)
        out_ref[:, j * part : (j + 1) * part] = total
    gain_part(w_ref, qkv_ref, gain_ref, gg_ref)


def in_rows_kernel(count, hidden, me_ref, *refs):
    blocks, (w_ref, gain_ref, in_ref, gg_ref) = refs[:count], refs[count:]
    slot = blocks[0].shape[1] // 2
    for i in range(2):
        piece = (slice(None), slice(i * slot, i * slot + hidden))
        values = [value.astype(F32) for value in ordered(blocks, me_ref[0], piece)]
        in_ref[:, i * count * hidden : (i + 1) * count * hidden] = jnp.concatenate(values, axis=1)
    gain_part(w_ref, in_ref, gain_ref, gg_ref)


def finish_rows(kernel, blocks, weight, gain, me, widths, name):
    rows = weight.shape[0]
    shapes = [jax.ShapeDtypeStruct((rows, n), F32) for n in widths] + [jax.ShapeDtypeStruct((1, rows), F32)]
    return pl.pallas_call(
        kernel,
        in_specs=[pl.BlockSpec(memory_space=pltpu.SMEM)] + [pl.BlockSpec(memory_space=pltpu.VMEM)] * (len(blocks) + 2),
        out_shape=shapes,
        cost_estimate=pl.CostEstimate(flops=0, bytes_accessed=8 * rows * sum(widths), transcendentals=0),
        name=name,
    )(me[None], *blocks, weight, gain[None])


def normal(values):
    centered = values - jnp.mean(values, axis=-1, keepdims=True)
    scale = lax.rsqrt(jnp.mean(centered * centered, axis=-1, keepdims=True) + NORM_EPS)
    return centered * scale, scale


def norm_back(upstream, gain, values):
    unit, scale = normal(values)
    weighted = upstream * gain
    return scale * (
        weighted
        - jnp.mean(weighted, axis=-1, keepdims=True)
        - unit * jnp.mean(weighted * unit, axis=-1, keepdims=True)
    )


def matmul(a, b):
    return jnp.dot(a, b, preferred_element_type=F32)


def matmul_nt(a, b):
    return lax.dot_general(a, b, (((1,), (1,)), ((), ())), preferred_element_type=F32)


def matmul_tn(a, b):
    return lax.dot_general(a, b, (((0,), (0,)), ((), ())), preferred_element_type=F32)


def on_device(
    hidden_in, segment_ids, valid_tokens, w_qkv, w_attn_out, w_in_proj, w_out_proj, attn_gain, mlp_gain, cotangent
):
    seq_size, fsdp_size = lax.axis_size("seq"), lax.axis_size("fsdp")
    seq, fsdp = lax.axis_index("seq"), lax.axis_index("fsdp")
    x_low, cot = hidden_in[0], cotangent[0]
    tokens = x_low.shape[0]
    length = tokens * seq_size
    part = D // seq_size
    hidden = FF // seq_size
    rel = [seq ^ k for k in range(seq_size)]

    def by_block(row):
        return jnp.concatenate([lax.dynamic_slice_in_dim(row, r * tokens, tokens) for r in rel])

    seg_all, valid_all = by_block(segment_ids[0]), by_block(valid_tokens[0])
    positions = by_block(jnp.arange(length, dtype=jnp.int32))
    frequency = ROPE_BASE ** (-2.0 * jnp.arange(HD // 2, dtype=F32) / HD)
    angles = positions.astype(F32)[:, None] * frequency[None, :]
    cosine, sine = lax.optimization_barrier((jnp.cos(angles), jnp.sin(angles)))
    cosine = jnp.concatenate([cosine] * 4, axis=1)
    sine = jnp.concatenate([-sine, sine] * 2, axis=1)
    seg_col, valid_col, seg_row = seg_all[:, None], valid_all[:, None], seg_all[None, :]

    first_mine = [lax.dynamic_slice_in_dim(w_qkv, i * D + seq * part, part, axis=1) for i in range(3)]
    first_mine.append(lax.dynamic_slice_in_dim(w_attn_out, seq * part, part, axis=1))
    gains = jnp.stack([attn_gain, mlp_gain], axis=1)
    first_mine.append(jnp.pad(gains, ((0, 0), (0, LANES - 2))))
    first_mine = jnp.concatenate(first_mine, axis=1)
    first_weight = gather_rows(first_mine)
    core = fsdp % 2
    slot = -(-hidden // LANES) * LANES
    if paired():
        down_mine = transpose_devices(lax.dynamic_slice_in_dim(w_out_proj, seq * part, part, axis=1))
    x_near = relay_first(x_low)
    out_mine = first_weight[:, 3 * part : 4 * part]
    gains = first_weight[:, 4 * part :].T.astype(F32)
    gain_one, gain_two = gains[0:1], gains[1:2]
    core = fsdp % 2
    slot = -(-hidden // LANES) * LANES
    def padded(rows):
        return jnp.pad(rows, ((0, 0), (0, slot - hidden)))

    def halves(rows):
        half = rows.shape[1] // 2
        low, high = rows[:, :half], rows[:, half:]
        return jnp.where(core == 0, low, high), jnp.where(core == 0, high, low)

    def by_core(mine, other):
        return jnp.where(core == 0, mine, other), jnp.where(core == 0, other, mine)

    in_mine = [
        padded(lax.dynamic_slice_in_dim(w_in_proj, i * FF + seq * hidden, hidden, axis=1)) for i in range(2)
    ]
    if paired():
        x_blocks = relay_last(x_low, *x_near)
        kept, sent = halves(after(down_mine, x_blocks, cosine, sine, seg_col, valid_col))
        down_mine = jnp.concatenate(by_core(kept, swap(sent, "fsdp", 1)), axis=0)
        feed_weight = gather_rows(jnp.concatenate(in_mine + [padded(down_mine.T)], axis=1))
    else:
        down_weight = lax.all_gather(w_out_proj, "fsdp", axis=0, tiled=True)
        down_weight = lax.dynamic_slice_in_dim(down_weight, seq * hidden, hidden, axis=0)
        feed_weight = jnp.concatenate([gather_rows(jnp.concatenate(in_mine, axis=1)), padded(down_weight.T)], axis=1)
        x_blocks = relay_last(x_low, *x_near)
    cot_near = relay_first(after(cot, *x_blocks))

    def in_order(blocks):
        bit = 1
        while bit < seq_size:
            flip = (seq & bit) != 0
            blocks = [jnp.where(flip, blocks[k ^ bit], blocks[k]) for k in range(seq_size)]
            bit *= 2
        return blocks


    a_low, q, k, v = project_qkv(x_blocks, first_weight, gain_one, cosine, sine)
    k, cot_near = after((k, cot_near), q)
    cot_blocks = relay_last(cot, *cot_near)
    mixed, lse = attend_forward(q, k, v, seg_col, valid_col, seg_row, tokens)

    out_near = relay_first(out_mine)
    mixed, out_near, cot_blocks = after((mixed, out_near, cot_blocks))
    out_weight = jnp.concatenate(in_order(relay_last(out_mine, *out_near)), axis=1)

    def to_tokens(blocks):
        came = [blocks[:tokens]] + [
            swap(blocks[i * tokens : (i + 1) * tokens], "seq", i) for i in range(1, seq_size)
        ]
        return jnp.concatenate(in_order(came), axis=1)

    mixed_low = to_tokens(mixed)
    x = x_low.astype(F32)
    attn_branch = matmul(mixed_low, out_weight)
    middle = x + attn_branch
    normed_two = (normal(middle)[0] * gain_two).astype(BF)
    normed_two = after(normed_two, *cot_blocks)

    b_blocks = share_seq(normed_two)
    fed, came, mlp_all = [None] * seq_size, [], None
    for i in range(seq_size):
        b = after(b_blocks[i], *came[:-1]) if len(came) > 1 else b_blocks[i]
        fed[i] = feed_forward(
            b, cot_blocks[i], feed_weight, hidden, seq, i, seq_size, F32 if i == 0 else BF, mlp_all
        )
        mlp_all = fed[i][4]
        if i > 0:
            came.append(swap(fed[i][3], "seq", i))
    m_blocks, gz_i, gz_g, gb_blocks, _ = zip(*fed)
    fed_grads = weight_gradients([after(b_blocks, *came[:-2])], [gz_i, gz_g], ((0, 1), (0, 2)), 3, 0)
    fed_grads = weight_gradients([after(cot_blocks, *came)], [m_blocks], ((0, 1),), 3, 2, fed_grads)
    grad_normed_two = gb_blocks[0]
    for block in came:
        grad_normed_two = grad_normed_two + block.astype(F32)
    grad_middle = cot.astype(F32) + norm_back(grad_normed_two, gain_two, middle)
    grad_attn_low = grad_middle.astype(BF)
    grad_mixed = matmul_nt(grad_attn_low, out_weight).astype(BF)

    sent = [lax.dynamic_slice_in_dim(grad_mixed, r * part, part, axis=1) for r in rel]
    came = [sent[0]] + [swap(sent[i], "seq", i) for i in range(1, seq_size)]
    grad_by_heads = jnp.concatenate(came, axis=0)
    out_part = matmul_tn(mixed_low, after(grad_attn_low, grad_by_heads)).astype(BF)
    grad_by_heads = after(grad_by_heads, out_part)
    mlp_came = exchange_seq(after(mlp_all, grad_by_heads))

    def own_rows(partial):
        return lax.psum_scatter(partial, "fsdp", scatter_dimension=0, tiled=True)

    fed_rows = own_rows(fed_grads)
    out_rows = own_rows(out_part)

    gp = attend_backward(
        q, k, v, grad_by_heads, lse, seg_col, valid_col, seg_row, cosine, sine, tokens
    )
    if paired():
        mine, away = last_gradients(a_low, gp, fsdp, fsdp_size)
    else:
        mine = away = matmul_tn(a_low, gp)
    mlp_branch = sum_blocks(after(mlp_came, away))
    result = middle + mlp_branch
    valid_mine = valid_all[:tokens].astype(F32)[:, None]
    stats = jnp.stack(
        [
            jnp.sum(valid_mine * result * result),
            jnp.sum(valid_mine * attn_branch * attn_branch),
            jnp.sum(valid_mine * mlp_branch * mlp_branch),
            jnp.sum(valid_mine),
        ]
    )

    def sum_bit(values, bit):
        rows = jnp.broadcast_to(values[:, None], (values.shape[0], LANES))
        return values + swap(rows, "fsdp", bit)[:, 0]

    stats = sum_bit(stats, 1)
    gp_late, stats = after((gp, stats))
    fed_late = after(fed_rows, away)
    in_rows, down_rows = fed_late[:, : 2 * slot], fed_late[:, 2 * slot :]
    in_all = share_seq(in_rows)
    ga_parts = project_back(gp_late, first_weight, seq, seq_size)
    ga_came = exchange_seq(after(ga_parts, *in_all[1:3]))
    if paired():
        mine = mine + after(swap(away, "fsdp", 1), ga_parts).astype(F32)
        down_rows = transpose_devices(down_rows)
        rows = mine.shape[0] // (fsdp_size // 2)
        terms = in_three(stats)
        extra = jnp.pad(terms, ((0, 16 - 3), (0, mine.shape[1] - 4)))
        came = [
            swap(jnp.concatenate([mine[k * rows : (k + 1) * rows].astype(BF), extra]), "fsdp", 2 * k)
            for k in range(1, fsdp_size // 2)
        ]
        came, ga_came = after((came, ga_came), out_rows)
        last = mine[:rows]
        for block in came:
            last = last + block[:rows].astype(F32)
        stats = tree_sum([from_three(terms)] + [from_three(block[rows : rows + 3, :4]) for block in came])
    else:
        last = lax.psum_scatter(mine, "fsdp", scatter_dimension=0, tiled=True)
        bit = 2
        while bit < fsdp_size:
            stats = sum_bit(stats, bit)
            bit *= 2
    extra = jnp.pad(in_three(stats), ((0, last.shape[0] - 3), (0, LANES - 4)))
    last = jnp.concatenate([last.astype(BF), out_rows, extra], axis=1)
    ga_came, in_all, down_rows = after((ga_came, in_all, down_rows), last)

    grad_in_weight, grad_gain_two = finish_rows(
        functools.partial(in_rows_kernel, seq_size, hidden), in_all, w_in_proj, mlp_gain, seq, (2 * FF,), "in_rows"
    )
    last_blocks = share_seq(last)
    grad_normed = sum_blocks(ga_came)
    grad_inputs = grad_middle + norm_back(grad_normed, gain_one, x)
    if paired():
        kept, sent = halves(down_rows[:, :hidden])
        down_rows = jnp.concatenate(by_core(kept, swap(sent, "fsdp", 1)), axis=0).T
        down_rows = after(down_rows, grad_in_weight, grad_inputs, last_blocks[1])
        grad_down = jnp.concatenate(in_order(share_seq(down_rows)), axis=1).astype(F32)
    else:
        down = lax.all_gather(down_rows[:, :hidden], ("seq", "fsdp"), axis=0, tiled=True)
        down = down.reshape(seq_size, D, hidden).transpose(0, 2, 1).reshape(FF, D)
        rows = FF // fsdp_size
        grad_down = lax.dynamic_slice_in_dim(down, fsdp * rows, rows, axis=0).astype(F32)

    last = after(last_blocks, grad_in_weight, grad_inputs)
    grad_qkv_weight, grad_out_weight, grad_gain_one = finish_rows(
        functools.partial(last_rows_kernel, seq_size), last, w_qkv, attn_gain, seq, (3 * D, D), "last_rows"
    )

    stats = tree_sum([from_three(rows[:3, -LANES : 4 - LANES]) for rows in last])
    root_means = jnp.sqrt(stats[:3] / (jnp.maximum(stats[3], 1.0) * D))

    return (
        result.astype(BF)[None],
        grad_inputs[None],
        grad_qkv_weight,
        grad_out_weight,
        grad_in_weight,
        grad_down,
        grad_gain_one[0],
        grad_gain_two[0],
        root_means,
    )


def solution(mesh):
    in_specs = (
        P("fsdp", "seq", None),
        P("fsdp", None),
        P("fsdp", None),
        P("fsdp", None),
        P("fsdp", None),
        P("fsdp", None),
        P("fsdp", None),
        P("fsdp"),
        P("fsdp"),
        P("fsdp", "seq", None),
    )
    out_specs = (
        P("fsdp", "seq", None),
        P("fsdp", "seq", None),
        P("fsdp", None),
        P("fsdp", None),
        P("fsdp", None),
        P("fsdp", None),
        P("fsdp"),
        P("fsdp"),
        P(),
    )
    return jax.shard_map(on_device, mesh=mesh, in_specs=in_specs, out_specs=out_specs, check_vma=False)
```
